32 devices in a mesh: dp: 32 (over z, y, x, core).
Axes of the slice: x: 2, y: 2, z: 4, core: 2. Of those that a mesh axis runs over, the one named last changes fastest.
Arguments:
- tokens: bfloat16 [8192, 1152], P('dp'), may hold values from -6 to 6
- qkv_weights: bfloat16 [3981312], P('dp'), may hold values from -0.1875 to 0.1875
- out_weights: bfloat16 [1327104], P('dp'), may hold values from -3 to 3
- fc1_weights: bfloat16 [4958208], P('dp'), may hold values from -0.1875 to 0.1875
- fc2_weights: bfloat16 [4958208], P('dp'), may hold values from -0.09375 to 0.09375
- ln_gain: float32 [2, 1152], replicated, may hold values from 0.25 to 1.75
- bias_model: float32 [6, 1152], replicated, may hold values from -3 to 3
- first_feedforward_bias: float32 [4304], replicated, may hold values from -3 to 3
- qkv_down: bfloat16 [3, 1152, 128], replicated, may hold values from -0.1875 to 0.1875
- qkv_up: bfloat16 [3, 128, 1152], replicated, may hold values from -0.75 to 0.75
- out_down: bfloat16 [1152, 128], replicated, may hold values from -3 to 3
- out_up: bfloat16 [128, 1152], replicated, may hold values from -0.75 to 0.75
- first_feedforward_down: bfloat16 [1152, 128], replicated, may hold values from -0.1875 to 0.1875
- fc1_up: bfloat16 [128, 4304], replicated, may hold values from -0.75 to 0.75
- fc2_down: bfloat16 [4304, 128], replicated, may hold values from -0.09375 to 0.09375
- fc2_up: bfloat16 [128, 1152], replicated, may hold values from -0.75 to 0.75
- adapter_of_image: int32 [12], replicated, may hold values from 0 to 7
- cotangent: bfloat16 [8192, 1152], P('dp'), may hold values from -6 to 6
Outputs:
- output: bfloat16 [8192, 1152], P('dp')
- grad_tokens: bfloat16 [8192, 1152], P('dp')
- grad_qkv_down: float32 [442368], P('dp')
- grad_qkv_up: float32 [442368], P('dp')
- grad_out_down: float32 [147456], P('dp')
- grad_out_up: float32 [147456], P('dp')
- grad_fc1_down: float32 [147456], P('dp')
- grad_fc1_up: float32 [550912], P('dp')
- grad_fc2_down: float32 [550912], P('dp')
- grad_fc2_up: float32 [147456], P('dp')
The draws below stay inside these ranges and needn't reach their ends.
All inputs are finite; a program needn't handle non-finite values.
Results may differ from the reference program's by a relative error of at most 0.015.
Values may be sent and summed in bfloat16 or wider, within the bound.
A program may use at most 256 MiB of HBM per device.

```python
import jax
import jax.numpy as jnp
from jax import lax

D = 1152
HEADS = 16
HEAD_DIM = 72
FF = 4304
IMG = 729
RANK = 16
ADAPTERS = 8
TOKENS = 8192
IMAGES = 12


def plant(values, rng, smallest, high):
    dims = values.shape
    index_at = [jax.random.randint(jax.random.fold_in(rng, axis), (), 0, dims[axis]) for axis in range(len(dims))]
    values = values.at[tuple(index_at)].set(smallest)
    longest = dims.index(max(dims))
    index_at[longest] = (index_at[longest] + 1) % dims[longest]
    return values.at[tuple(index_at)].set(high)


def block_scale(rng, extent, cuts, least, top_value):
    factor_of = 1.0
    for position, shards_of in cuts:
        steps = jax.random.uniform(jax.random.fold_in(jax.random.fold_in(rng, 6), position), (shards_of,), jnp.float32, least / len(cuts), top_value / len(cuts))
        factor_of = factor_of * jnp.repeat(jnp.exp(steps), extent[position] // shards_of).reshape((-1,) + (1,) * (len(extent) - 1 - position))
    return factor_of


def scatter_about(own_key, dims, width, reach, split=(), kind=jnp.bfloat16):
    array = width * jax.random.normal(own_key, dims, jnp.float32)
    if split:
        array = array * block_scale(own_key, dims, split, -0.22, 0.18)
    return jnp.clip(array, -reach, reach).astype(kind)


def setup_inputs(seed: int = 0) -> dict:
    seeds = jax.random.split(jax.random.key(seed), 19)
    return {
        "tokens": scatter_about(seeds[0], (TOKENS, D), 1.0, 6.0, ((0, 32),)),
        "qkv_weights": scatter_about(seeds[1], (3 * D * D,), D ** -0.5, 0.1875, ((0, 32),)),
        "out_weights": scatter_about(seeds[2], (D * D,), (max(1, D // 256)) ** -0.5, 3.0, ((0, 32),)),
        "fc1_weights": scatter_about(seeds[3], (D * FF,), D ** -0.5, 0.1875, ((0, 32),)),
        "fc2_weights": scatter_about(seeds[4], (FF * D,), FF ** -0.5, 0.09375, ((0, 32),)),
        "ln_gain": jnp.clip(1.0 + 0.15 * jax.random.normal(seeds[5], (2, D), jnp.float32), 0.25, 1.75),
        "bias_model": scatter_about(seeds[6], (6, D), 0.3, 3.0, (), jnp.float32),
        "first_feedforward_bias": scatter_about(seeds[7], (FF,), 0.3, 3.0, (), jnp.float32),
        "qkv_down": scatter_about(seeds[8], (3, D, ADAPTERS * RANK), D ** -0.5, 0.1875),
        "qkv_up": scatter_about(seeds[9], (3, ADAPTERS * RANK, D), (4 * RANK) ** -0.5, 0.75),
        "out_down": scatter_about(seeds[10], (D, ADAPTERS * RANK), (max(1, D // 256)) ** -0.5, 3.0),
        "out_up": scatter_about(seeds[11], (ADAPTERS * RANK, D), (4 * RANK) ** -0.5, 0.75),
        "first_feedforward_down": scatter_about(seeds[12], (D, ADAPTERS * RANK), D ** -0.5, 0.1875),
        "fc1_up": scatter_about(seeds[13], (ADAPTERS * RANK, FF), (4 * RANK) ** -0.5, 0.75),
        "fc2_down": scatter_about(seeds[14], (FF, ADAPTERS * RANK), FF ** -0.5, 0.09375),
        "fc2_up": scatter_about(seeds[15], (ADAPTERS * RANK, D), (4 * RANK) ** -0.5, 0.75),
        "adapter_of_image": plant(jax.random.randint(seeds[16], (IMAGES,), 0, ADAPTERS), jax.random.fold_in(seeds[16], 1), 0, ADAPTERS - 1).astype(jnp.int32),
        "cotangent": scatter_about(seeds[17], (TOKENS, D), 1.0, 6.0, ((0, 32),)),
    }


@jax.custom_vjp
def low(v):
    return lax.optimization_barrier(v.astype(jnp.bfloat16)).astype(jnp.float32)

@jax.custom_vjp
def low_back(v):
    return v

def low_keep(v):
    return (low(v), None)

def low_pass(kept, grad):
    return (grad,)

def back_keep(v):
    return (v, None)

def back_low(kept, grad):
    return (low(grad),)
low.defvjp(low_keep, low_pass)
low_back.defvjp(back_keep, back_low)
epsilon = 1e-06
highest = lax.Precision.HIGHEST

def norm_rows(inputs, gain_row, shift_row):
    center = inputs - lax.optimization_barrier(jnp.mean(inputs, axis=-1, keepdims=True))
    spread_inv = lax.rsqrt(lax.optimization_barrier(jnp.mean(center * center, axis=-1, keepdims=True)) + epsilon)
    return center * spread_inv * gain_row + shift_row

def gelu_tanh(inputs):
    return 0.5 * inputs * (1.0 + jnp.tanh(0.7978845608028654 * (inputs + 0.044715 * inputs * inputs * inputs)))

def product(left, right):
    return jnp.dot(left, right, precision=highest, preferred_element_type=jnp.float32)

def reference(tokens, qkv_weights, out_weights, fc1_weights, fc2_weights, ln_gain, bias_model, first_feedforward_bias, qkv_down, qkv_up, out_down, out_up, first_feedforward_down, fc1_up, fc2_down, fc2_up, adapter_of_image, cotangent):
    w_qkv = qkv_weights.astype(jnp.float32).reshape(3, D, D)
    w_out = out_weights.astype(jnp.float32).reshape(D, D)
    w_fc1 = fc1_weights.astype(jnp.float32).reshape(D, FF)
    w_fc2 = fc2_weights.astype(jnp.float32).reshape(FF, D)
    gain_rows = ln_gain.astype(jnp.float32)
    bias_rows = bias_model.astype(jnp.float32)
    fc1_bias = first_feedforward_bias.astype(jnp.float32)
    image_ids = jnp.arange(TOKENS, dtype=jnp.int32) // IMG
    chosen = adapter_of_image[image_ids]
    column_ids = jnp.arange(ADAPTERS * RANK, dtype=jnp.int32) // RANK
    select = (column_ids[None, :] == chosen[:, None]).astype(jnp.float32)
    padded_len = IMAGES * IMG
    key_valid = (jnp.arange(padded_len, dtype=jnp.int32) < TOKENS).reshape(IMAGES, IMG)
    score_scale = HEAD_DIM ** (-0.5)

    def adapt(source, down_map, up_map):
        lowrank = low_back(low(select * product(source, down_map)))
        return product(lowrank, up_map)

    def one_image(pieces):
        query_img, key_img, value_img, valid_img = pieces
        raw_scores = jnp.einsum('qhd,khd->hqk', query_img, key_img, precision=highest) * score_scale
        scores = jnp.where(valid_img[None, None, :], low_back(raw_scores), -1e+30)
        attn_probs = low(jax.nn.softmax(scores, axis=-1))
        return jnp.einsum('hqk,khd->qhd', attn_probs, value_img, precision=highest)
    attend = jax.checkpoint(one_image)

    def split_heads(rows_all):
        padded = jnp.pad(rows_all, ((0, padded_len - TOKENS), (0, 0)))
        return padded.reshape(IMAGES, IMG, HEADS, HEAD_DIM)

    def forward(tokens_f, qkv_d, qkv_u, out_d, out_u, fc1_d, fc1_u, fc2_d, fc2_u):
        normed1 = low(norm_rows(tokens_f, gain_rows[0], bias_rows[0]))
        queries = low_back(low(product(normed1, w_qkv[0]) + bias_rows[1] + adapt(normed1, qkv_d[0], qkv_u[0])))
        key_rows = low_back(low(product(normed1, w_qkv[1]) + adapt(normed1, qkv_d[1], qkv_u[1])))
        values = low_back(low(product(normed1, w_qkv[2]) + bias_rows[2] + adapt(normed1, qkv_d[2], qkv_u[2])))
        mixed = lax.map(attend, (split_heads(queries), split_heads(key_rows), split_heads(values), key_valid))
        attended = low_back(low(mixed.reshape(padded_len, D)[:TOKENS]))
        branch = low_back(product(attended, w_out) + bias_rows[3] + adapt(attended, out_d, out_u))
        resid = tokens_f + branch
        normed2 = low(norm_rows(resid, gain_rows[1], bias_rows[4]))
        pre_act = low_back(product(normed2, w_fc1) + fc1_bias + adapt(normed2, fc1_d, fc1_u))
        activated = low(gelu_tanh(pre_act))
        return resid + product(activated, w_fc2) + bias_rows[5] + adapt(activated, fc2_d, fc2_u)
    inputs = (tokens.astype(jnp.float32), qkv_down.astype(jnp.float32), qkv_up.astype(jnp.float32), out_down.astype(jnp.float32), out_up.astype(jnp.float32), first_feedforward_down.astype(jnp.float32), fc1_up.astype(jnp.float32), fc2_down.astype(jnp.float32), fc2_up.astype(jnp.float32))
    output, pull_back = jax.vjp(forward, *inputs)
    grads = pull_back(cotangent.astype(jnp.float32))
    return (output.astype(jnp.bfloat16), grads[0].astype(jnp.bfloat16), grads[1].reshape(-1), grads[2].reshape(-1), grads[3].reshape(-1), grads[4].reshape(-1), grads[5].reshape(-1), grads[6].reshape(-1), grads[7].reshape(-1), grads[8].reshape(-1))
```

```python
import functools
from functools import partial

import jax
import jax.numpy as jnp
from jax import lax
from jax.experimental import pallas as pl
from jax.experimental.pallas import tpu as pltpu
from jax.sharding import PartitionSpec as P

D = 1152
HEADS = 16
HEAD_DIM = 72
FF = 4304
FP = 4352
IMG = 729
RANK = 16
ADAPTERS = 8
REACH = 3
IMAGE_SLOTS = 2


epsilon = 1e-06


def shifted(value, axis, steps):
    count = lax.axis_size(axis)
    first, last = (max(0, -steps), min(count, count - steps))
    return lax.ppermute(value, axis, [(source, source + steps) for source in range(first, last)])


def norm_rows(inputs, gain_row, shift_row):
    center = inputs - jnp.mean(inputs, axis=-1, keepdims=True)
    spread_inv = lax.rsqrt(jnp.mean(center * center, axis=-1, keepdims=True) + epsilon)
    return center * spread_inv * gain_row + shift_row


def gelu_tanh(inputs):
    return (
        0.5
        * inputs
        * (1.0 + jnp.tanh(0.7978845608028654 * (inputs + 0.044715 * inputs * inputs * inputs)))
    )


def product(left, right):
    return jnp.dot(left, right, preferred_element_type=jnp.float32)


def inner_product(left, right):
    return lax.dot_general(
        left, right, (((0,), (0,)), ((), ())), preferred_element_type=jnp.float32
    )


def product_with_transpose(left, right):
    return lax.dot_general(
        left, right, (((1,), (1,)), ((), ())), preferred_element_type=jnp.float32
    )


MESH = pl.DeviceIdType.MESH
PLANE = 8
STRIDE = 1
ROWS = (216, 72, 72, 272)
WIDE = (D, D, FP, D)
TILES = tuple(rows // 8 for rows in ROWS)
PIECES = (
    (0, (0, 14), (14, 13)),
    (1, (0, 5), (5, 4)),
    (2, (0, 4), (4, 5)),
    (3, (0, 17), (17, 17)),
)


def remote(src, dst, send, recv, to):
    return pltpu.make_async_remote_copy(src_ref=src, dst_ref=dst, send_sem=send, recv_sem=recv, device_id=(to,), device_id_type=MESH)

def gather_kernel(layers, qkv, out, fc1, fc2, o_qkv, o_out, o_fc1, o_fc2,
                  h_qkv, h_out, h_fc1, h_fc2, ahead, ahead_in, wide, b_qkv, b_out, b_fc1, b_fc2,
                  pair_send, pair_recv, ahead_sem, own_sem, z_send, hop_send, pair_out, ici_recv, pair_in):
    me = lax.axis_index("dp")
    core = lax.rem(me, 2)
    x = lax.rem(me // 2, 2)
    y = lax.rem(me // 4, 2)
    z = me // PLANE
    chip = me // 2
    chips = 4 * layers
    mate = me + 1 - 2 * core
    to_x = me + 2 - 4 * x
    to_y = me + 4 - 8 * y
    barrier = pltpu.get_barrier_semaphore()
    def greet(peer):
        pl.semaphore_signal(barrier, inc=1, device_id=(peer,), device_id_type=MESH)
    for peer in (mate, to_x, to_y):
        greet(peer)
    nxt = lax.rem(chip + 1, chips) * 2 + core
    prv = lax.rem(chip + chips - 1, chips) * 2 + core
    greet(nxt)
    greet(prv)
    spot_in_layer = lax.rem(me, PLANE)
    greet(lax.rem(z + 1, layers) * PLANE + spot_in_layer)
    greet(lax.rem(z + layers - 1, layers) * PLANE + spot_in_layer)
    pl.semaphore_wait(barrier, 7)

    ins = (qkv, out, fc1, fc2)
    held = (h_qkv, h_out, h_fc1, h_fc2)
    outs = (o_qkv, o_out, o_fc1, o_fc2)
    blocks = (b_qkv, b_out, b_fc1, b_fc2)
    for a in range(4):
        remote(ins[a], held[a].at[core], pair_send.at[a], pair_recv.at[a], mate).start()
        pltpu.make_async_copy(ins[a], held[a].at[core], own_sem.at[a]).start()

    def pair_wait(a):
        pltpu.make_async_copy(ins[a], held[a].at[core], own_sem.at[a]).wait()
        remote(ins[a], held[a].at[1 - core], pair_send.at[a], pair_recv.at[a], mate).wait_recv()

    def build(a):
        half = ROWS[a] // 2
        w = WIDE[a]
        wide[0:half, 0:w] = held[a][0].astype(jnp.float32)
        wide[half:2 * half, 0:w] = held[a][1].astype(jnp.float32)
        blocks[a][...] = wide[0:2 * half, 0:w].reshape(half // 4, 8, w).astype(jnp.bfloat16)

    def build_fc2():
        wide[0:135, 0:D] = held[3][0].astype(jnp.float32)
        lead = wide[134:135, 0:D] + held[3][1, 0:1].astype(jnp.float32)
        wide[134:135, 0:D] = lead
        wide[135:269, 0:D] = held[3][1].astype(jnp.float32)[1:135]
        ahead[...] = wide[0:48, 0:D].astype(jnp.bfloat16)
        remote(ahead, ahead_in, ahead_sem.at[0], ahead_sem.at[1], prv).start()
    def finish_fc2():
        remote(ahead, ahead_in, ahead_sem.at[0], ahead_sem.at[1], prv).wait_recv()
        more = ahead_in[...].astype(jnp.float32)
        wide[269:269 + 48, 0:D] = jnp.where(chip + 1 < chips, more, 0.0)
        moved = pltpu.roll(wide[0:320, 0:D], 320 - 3 * chip, axis=0)[0:272]
        b_fc2[...] = moved.reshape(34, 8, D).astype(jnp.bfloat16)

    def spot(p, m, c):
        a, *cuts = PIECES[p]
        at, rows = cuts[c]
        return outs[a].at[pl.ds(m * TILES[a] + at, rows)]

    levels = [(d, s) for d in range(layers) for s in ((0,) if d == 0 else (-1, 1))]
    plane = lax.rem(chip, 4)
    corners = (plane, plane + 1 - 2 * x, plane + 2 - 4 * y, 3 - plane)

    def there(d, s):
        return (z - d >= 0) if s < 0 else (z + d < layers)

    def also(yes, go):
        if yes is None:
            go()
        else:
            pl.when(yes)(go)

    def level(d, s, go):
        also(None if d == 0 else there(d, s), go)

    def run(c):
        def cut(p):
            a, *cuts = PIECES[p]
            return blocks[a].at[pl.ds(*cuts[c])]

        def hops(p, src, m, slot, ways):
            for w in ways:
                if w == 2:
                    remote(src, spot(p, m, c), pair_out.at[p, slot], pair_in.at[p, m], mate).start()
                else:
                    remote(src, spot(p, m, c), hop_send.at[p, slot, w], ici_recv.at[p, m], (to_x, to_y)[w]).start()

        def along(p, src, m, slot, up, act):
            def go():
                d = remote(src, spot(p, m, c), z_send.at[p, slot, up], ici_recv.at[p, m], me + PLANE if up else me - PLANE)
                act(d)
            pl.when((z + 1 < layers) if up else (z > 0))(go)

        def arrived(p, m):
            s = spot(p, m, c)
            pltpu.make_async_copy(s, s, ici_recv.at[p, m]).wait()
            return s

        start = lambda d: d.start()
        finish = lambda d: d.wait_send()

        def event(p, g, act):
            n = len(levels)
            if g == 0:
                hops(p, cut(p), chip, 0, (0, 1))
                for up in (0, 1):
                    along(p, cut(p), chip, 0, up, start)
            for i, (d, s) in enumerate(levels):
                zz = z + s * d
                if d >= 1 and d == g:
                    def go():
                        m = zz * 4 + corners[0]
                        src = arrived(p, m)
                        along(p, src, m, i, int(s < 0), start)
                        hops(p, src, m, i, (0, 1, 2))
                    level(d, s, go)
                if d + 1 == g:
                    def go():
                        m = zz * 4 + corners[1]
                        hops(p, arrived(p, m), m, n + i, (1, 2) if c == 0 else (2,))
                        m = zz * 4 + corners[2]
                        hops(p, arrived(p, m), m, 2 * n + i, (2,) if c == 0 else (0, 2))
                    level(d, s, go)
                if d + 2 == g:
                    def go():
                        m = zz * 4 + corners[3]
                        hops(p, arrived(p, m), m, 3 * n + i, (2,))
                    level(d, s, go)

        launched = {0: 0, 1: 1, 2: 2, 3: 3}
        made = -1
        count = len(PIECES)
        last = STRIDE * (count - 1) + layers + 1
        for t in range(last + 1):
            for p in range(count):
                g = t - STRIDE * p
                if 0 <= g <= layers + 1:
                    a = PIECES[p][0]
                    if g == 0 and a > made:
                        made = a
                        pair_wait(a)
                        if a < 3:
                            build(a)
                        else:
                            build_fc2()
                            finish_fc2()
                        pltpu.make_async_copy(blocks[a], outs[a].at[pl.ds(chip * TILES[a], TILES[a])], own_sem.at[a]).start()
                    event(p, g, start)
        for p in range(count):
            for k in range(4):
                for d, s in levels:
                    if k == 0 and d == 0:
                        continue
                    def go():
                        m = (z + s * d) * 4 + corners[k]
                        q = spot(p, m, 1 - c)
                        pltpu.make_async_copy(q, q, pair_in.at[p, m]).wait()
                    level(d, s, go)
        n = len(levels)
        for p in range(count):
            src = cut(p)
            def sent(sem):
                pltpu.make_async_copy(src, src, sem).wait()
            for i, (d, s) in enumerate(levels):
                def go():
                    sent(hop_send.at[p, i, 0])
                    sent(hop_send.at[p, i, 1])
                    if c == 0:
                        sent(hop_send.at[p, n + i, 1])
                    else:
                        sent(hop_send.at[p, 2 * n + i, 0])
                    for k in range(4):
                        if k or d:
                            sent(pair_out.at[p, k * n + i])
                    for up in (0, 1):
                        if d == 0 or up == int(s < 0):
                            pl.when((z + 1 < layers) if up else (z > 0))(lambda: sent(z_send.at[p, i, up]))
                level(d, s, go)
        for a in range(4):
            remote(ins[a], held[a].at[core], pair_send.at[a], pair_recv.at[a], mate).wait_send()
            pltpu.make_async_copy(blocks[a], outs[a].at[pl.ds(chip * TILES[a], TILES[a])], own_sem.at[a]).wait()
        remote(ahead, ahead_in, ahead_sem.at[0], ahead_sem.at[1], prv).wait_send()

    for c in (0, 1):
        @pl.when(core == c)
        def _():
            run(c)

def gather(n, qkv, out, fc1, fc2):
    layers = n // PLANE
    core = lax.rem(lax.axis_index("dp"), 2)
    qkv = qkv.reshape(108, D)
    out = out.reshape(36, D)
    fc1 = jnp.pad(fc1.reshape(36, FF), ((0, 0), (0, FP - FF)))
    half = jnp.zeros((576,), fc2.dtype)
    fc2 = jnp.where(core == 0, jnp.concatenate([fc2, half]), jnp.concatenate([half, fc2])).reshape(135, D)
    chips = 4 * layers
    slots = 2 * layers - 1
    count = len(PIECES)
    dma = pltpu.SemaphoreType.DMA
    return pl.pallas_call(
        functools.partial(gather_kernel, layers),
        out_shape=[jax.ShapeDtypeStruct((TILES[a] * chips, 8, WIDE[a]), jnp.bfloat16) for a in range(4)],
        in_specs=[pl.BlockSpec(memory_space=pl.ANY)] * 4,
        out_specs=[pl.BlockSpec(memory_space=pl.ANY)] * 4,
        scratch_shapes=[
            pltpu.VMEM((2, 108, D), jnp.bfloat16),
            pltpu.VMEM((2, 36, D), jnp.bfloat16),
            pltpu.VMEM((2, 36, FP), jnp.bfloat16),
            pltpu.VMEM((2, 135, D), jnp.bfloat16),
            pltpu.VMEM((48, D), jnp.bfloat16),
            pltpu.VMEM((48, D), jnp.bfloat16),
            pltpu.VMEM((320, FP), jnp.float32),
            pltpu.VMEM((27, 8, D), jnp.bfloat16),
            pltpu.VMEM((9, 8, D), jnp.bfloat16),
            pltpu.VMEM((9, 8, FP), jnp.bfloat16),
            pltpu.VMEM((34, 8, D), jnp.bfloat16),
            dma((4,)), dma((4,)), dma((2,)), dma((4,)), dma((count, slots, 2)),
            dma((count, 3 * slots, 2)), dma((count, 4 * slots)), dma((count, chips)), dma((count, chips)),
        ],
        compiler_params=pltpu.CompilerParams(collective_id=0, has_side_effects=True, vmem_limit_bytes=40 << 20),
        name="gather_weights",
    )(qkv, out, fc1, fc2)


def frozen(qkv, out, fc1, fc2):
    n = lax.axis_size("dp")
    if n == 4 * PLANE:
        w_qkv, w_out, w_fc1, w_fc2 = gather(n, qkv, out, fc1, fc2)
        return (w_qkv.reshape(3, D, D), w_out.reshape(D, D), w_fc1.reshape(D, FP), w_fc2.reshape(FP, D))
    qkv, out, fc1, fc2 = (lax.all_gather(v, "dp", axis=0, tiled=True) for v in (qkv, out, fc1, fc2))
    return (
        qkv.reshape(3, D, D),
        out.reshape(D, D),
        jnp.pad(fc1.reshape(D, FF), ((0, 0), (0, FP - FF))),
        jnp.pad(fc2.reshape(FF, D), ((0, FP - FF), (0, 0))),
    )


def local(
    tokens,
    qkv_weights,
    out_weights,
    fc1_weights,
    fc2_weights,
    ln_gain,
    bias_model,
    first_feedforward_bias,
    qkv_down,
    qkv_up,
    out_down,
    out_up,
    first_feedforward_down,
    fc1_up,
    fc2_down,
    fc2_up,
    adapter_of_image,
    cotangent,
):
    local_rows = tokens.shape[0]
    devices = lax.axis_size("dp")
    all_tokens = local_rows * devices
    images = adapter_of_image.shape[0]
    row_start = lax.axis_index("dp") * local_rows
    positions = row_start + jnp.arange(local_rows, dtype=jnp.int32)
    image_ids = positions // IMG
    first_image = row_start // IMG
    chosen = jnp.zeros((local_rows,), jnp.int32)
    for image_slot_index in range(IMAGE_SLOTS):
        clamped = jnp.minimum(first_image + image_slot_index, images - 1)
        adapter_id = lax.dynamic_index_in_dim(adapter_of_image, clamped, 0, keepdims=False)
        chosen = jnp.where(image_ids == first_image + image_slot_index, adapter_id, chosen)
    column_ids = jnp.arange(ADAPTERS * RANK, dtype=jnp.int32) // RANK
    select = (column_ids[None, :] == chosen[:, None]).astype(jnp.float32)
    score_scale = HEAD_DIM ** (-0.5)
    ext_len = local_rows + 2 * (IMG - 1)
    w_qkv, w_out, w_fc1, w_fc2 = frozen(qkv_weights, out_weights, fc1_weights, fc2_weights)
    tail = FP - FF
    first_feedforward_bias = jnp.pad(first_feedforward_bias, (0, tail))
    fc1_up = jnp.pad(fc1_up, ((0, 0), (0, tail)))
    fc2_down = jnp.pad(fc2_down, ((0, tail), (0, 0)))
    tokens_f = tokens.astype(jnp.float32)
    normed1 = norm_rows(tokens_f, ln_gain[0], bias_model[0]).astype(jnp.bfloat16)
    shift_terms = (bias_model[1], jnp.zeros_like(bias_model[1]), bias_model[2])
    lowrank_qkv = []
    projected = []
    for part_id in range(3):
        lowrank = (select * product(normed1, qkv_down[part_id])).astype(jnp.bfloat16)
        lowrank_qkv.append(lowrank)
        projected.append(
            (
                product(normed1, w_qkv[part_id])
                + shift_terms[part_id]
                + product(lowrank, qkv_up[part_id])
            ).astype(jnp.bfloat16)
        )
    queries, key_rows, values = projected
    lower_keys = []
    lower_values = []
    upper_keys = []
    upper_values = []
    for distance in range(1, REACH + 1):
        rim_rows = min(local_rows, IMG - 1 - (distance - 1) * local_rows)
        from_below = shifted(
            (key_rows[local_rows - rim_rows :], values[local_rows - rim_rows :]), "dp", distance
        )
        from_above = shifted((key_rows[:rim_rows], values[:rim_rows]), "dp", -distance)
        lower_keys.insert(0, from_below[0])
        lower_values.insert(0, from_below[1])
        upper_keys.append(from_above[0])
        upper_values.append(from_above[1])
    ext_keys = jnp.concatenate(lower_keys + [key_rows] + upper_keys, axis=0).reshape(
        ext_len, HEADS, HEAD_DIM
    )
    ext_values = jnp.concatenate(lower_values + [values] + upper_values, axis=0).reshape(
        ext_len, HEADS, HEAD_DIM
    )
    query_heads = queries.reshape(local_rows, HEADS, HEAD_DIM)

    def slot_view(image_slot_index):
        image_id = first_image + image_slot_index
        offset = jnp.clip(image_id * IMG - row_start + IMG - 1, 0, ext_len - IMG)
        key_pos = row_start - (IMG - 1) + offset + jnp.arange(IMG, dtype=jnp.int32)
        key_ok = (key_pos >= 0) & (key_pos < all_tokens) & (key_pos // IMG == image_id)
        query_ok = (image_ids == image_id).astype(jnp.float32)
        slot_keys = lax.dynamic_slice_in_dim(ext_keys, offset, IMG, 0)
        slot_values = lax.dynamic_slice_in_dim(ext_values, offset, IMG, 0)
        raw_scores = (
            jnp.einsum("qhd,khd->hqk", query_heads, slot_keys, preferred_element_type=jnp.float32)
            * score_scale
        )
        scores = jnp.where(key_ok[None, None, :], raw_scores, -1e30)
        return (offset, query_ok, slot_keys, slot_values, scores)

    attended_f = jnp.zeros((local_rows, HEADS, HEAD_DIM), jnp.float32)
    log_totals = []
    for image_slot_index in range(IMAGE_SLOTS):
        offset, query_ok, slot_keys, slot_values, scores = slot_view(image_slot_index)
        row_max = jnp.max(scores, axis=-1, keepdims=True)
        log_total = row_max + jnp.log(jnp.sum(jnp.exp(scores - row_max), axis=-1, keepdims=True))
        log_totals.append(log_total)
        attn_probs = (jnp.exp(scores - log_total) * query_ok[None, :, None]).astype(jnp.bfloat16)
        attended_f = attended_f + jnp.einsum(
            "hqk,khd->qhd", attn_probs, slot_values, preferred_element_type=jnp.float32
        )
    attended = attended_f.reshape(local_rows, D).astype(jnp.bfloat16)
    lowrank_out = (select * product(attended, out_down)).astype(jnp.bfloat16)
    resid = tokens_f + product(attended, w_out) + bias_model[3] + product(lowrank_out, out_up)
    normed2 = norm_rows(resid, ln_gain[1], bias_model[4]).astype(jnp.bfloat16)
    lowrank_fc1 = (select * product(normed2, first_feedforward_down)).astype(jnp.bfloat16)
    pre_act = product(normed2, w_fc1) + first_feedforward_bias + product(lowrank_fc1, fc1_up)
    activated = gelu_tanh(pre_act).astype(jnp.bfloat16)
    lowrank_fc2 = (select * product(activated, fc2_down)).astype(jnp.bfloat16)
    output = (
        resid + product(activated, w_fc2) + bias_model[5] + product(lowrank_fc2, fc2_up)
    ).astype(jnp.bfloat16)
    back_qkv, back_out, back_fc1, back_fc2 = w_qkv, w_out, w_fc1, w_fc2
    grad_fc2_up = inner_product(lowrank_fc2, cotangent)
    glow_fc2 = (select * product_with_transpose(cotangent, fc2_up)).astype(jnp.bfloat16)
    grad_fc2_down = inner_product(activated, glow_fc2)
    grad_act = product_with_transpose(cotangent, back_fc2) + product_with_transpose(
        glow_fc2, fc2_down
    )
    gelu_back = jax.vjp(gelu_tanh, pre_act)[1]
    grad_pre = gelu_back(grad_act)[0].astype(jnp.bfloat16)
    grad_fc1_up = inner_product(lowrank_fc1, grad_pre)
    glow_fc1 = (select * product_with_transpose(grad_pre, fc1_up)).astype(jnp.bfloat16)
    grad_fc1_down = inner_product(normed2, glow_fc1)
    grad_norm2 = product_with_transpose(grad_pre, back_fc1) + product_with_transpose(
        glow_fc1, first_feedforward_down
    )
    second_norm_backward = jax.vjp(
        partial(norm_rows, gain_row=ln_gain[1], shift_row=bias_model[4]), resid
    )[1]
    residual_gradient = cotangent.astype(jnp.float32) + second_norm_backward(grad_norm2)[0]
    grad_branch = residual_gradient.astype(jnp.bfloat16)
    grad_out_up = inner_product(lowrank_out, grad_branch)
    glow_out = (select * product_with_transpose(grad_branch, out_up)).astype(jnp.bfloat16)
    grad_out_down = inner_product(attended, glow_out)
    grad_attended = (
        product_with_transpose(grad_branch, back_out) + product_with_transpose(glow_out, out_down)
    ).astype(jnp.bfloat16)
    grad_heads = grad_attended.reshape(local_rows, HEADS, HEAD_DIM)
    grad_queries = jnp.zeros((local_rows, HEADS, HEAD_DIM), jnp.float32)
    grad_ext_keys = jnp.zeros((ext_len, HEADS, HEAD_DIM), jnp.float32)
    grad_ext_values = jnp.zeros((ext_len, HEADS, HEAD_DIM), jnp.float32)
    for image_slot_index in range(IMAGE_SLOTS):
        offset, query_ok, slot_keys, slot_values, scores = slot_view(image_slot_index)
        probs_f = jnp.exp(scores - log_totals[image_slot_index]) * query_ok[None, :, None]
        probability_matrix = probs_f.astype(jnp.bfloat16)
        grad_probs = jnp.einsum(
            "qhd,khd->hqk", grad_heads, slot_values, preferred_element_type=jnp.float32
        )
        row_dot = jnp.sum(grad_probs * probs_f, axis=-1, keepdims=True)
        grad_scores = (probs_f * (grad_probs - row_dot)).astype(jnp.bfloat16)
        grad_queries = grad_queries + score_scale * jnp.einsum(
            "hqk,khd->qhd", grad_scores, slot_keys, preferred_element_type=jnp.float32
        )
        key_part = score_scale * jnp.einsum(
            "hqk,qhd->khd", grad_scores, query_heads, preferred_element_type=jnp.float32
        )
        value_part = jnp.einsum(
            "hqk,qhd->khd", probability_matrix, grad_heads, preferred_element_type=jnp.float32
        )
        grad_ext_keys = lax.dynamic_update_slice_in_dim(
            grad_ext_keys,
            lax.dynamic_slice_in_dim(grad_ext_keys, offset, IMG, 0) + key_part,
            offset,
            0,
        )
        grad_ext_values = lax.dynamic_update_slice_in_dim(
            grad_ext_values,
            lax.dynamic_slice_in_dim(grad_ext_values, offset, IMG, 0) + value_part,
            offset,
            0,
        )
    grad_ext_keys = grad_ext_keys.reshape(ext_len, D)
    grad_ext_values = grad_ext_values.reshape(ext_len, D)
    grad_keys_f = grad_ext_keys[IMG - 1 : IMG - 1 + local_rows]
    grad_values_f = grad_ext_values[IMG - 1 : IMG - 1 + local_rows]
    for distance in range(1, REACH + 1):
        rim_rows = min(local_rows, IMG - 1 - (distance - 1) * local_rows)
        low_begin = IMG - 1 - (distance - 1) * local_rows - rim_rows
        high_begin = IMG - 1 + distance * local_rows
        from_above = (
            shifted(
                grad_ext_keys[low_begin : low_begin + rim_rows].astype(jnp.bfloat16),
                "dp",
                -distance,
            ).astype(jnp.float32),
            shifted(
                grad_ext_values[low_begin : low_begin + rim_rows].astype(jnp.bfloat16),
                "dp",
                -distance,
            ).astype(jnp.float32),
        )
        from_below = (
            shifted(
                grad_ext_keys[high_begin : high_begin + rim_rows].astype(jnp.bfloat16),
                "dp",
                distance,
            ).astype(jnp.float32),
            shifted(
                grad_ext_values[high_begin : high_begin + rim_rows].astype(jnp.bfloat16),
                "dp",
                distance,
            ).astype(jnp.float32),
        )
        grad_keys_f = grad_keys_f.at[local_rows - rim_rows :].add(from_above[0])
        grad_values_f = grad_values_f.at[local_rows - rim_rows :].add(from_above[1])
        grad_keys_f = grad_keys_f.at[:rim_rows].add(from_below[0])
        grad_values_f = grad_values_f.at[:rim_rows].add(from_below[1])
    grad_parts = [
        grad_queries.reshape(local_rows, D).astype(jnp.bfloat16),
        grad_keys_f.astype(jnp.bfloat16),
        grad_values_f.astype(jnp.bfloat16),
    ]
    grad_norm1 = jnp.zeros((local_rows, D), jnp.float32)
    downs_list = []
    ups_list = []
    for part_id in range(3):
        grad_part = grad_parts[part_id]
        ups_list.append(inner_product(lowrank_qkv[part_id], grad_part))
        glow_part = (select * product_with_transpose(grad_part, qkv_up[part_id])).astype(
            jnp.bfloat16
        )
        downs_list.append(inner_product(normed1, glow_part))
        grad_norm1 = (
            grad_norm1
            + product_with_transpose(grad_part, back_qkv[part_id])
            + product_with_transpose(glow_part, qkv_down[part_id])
        )
    norm1_back = jax.vjp(
        partial(norm_rows, gain_row=ln_gain[0], shift_row=bias_model[0]), tokens_f
    )[1]
    grad_tokens = (residual_gradient + norm1_back(grad_norm1)[0]).astype(jnp.bfloat16)
    summed = (
        lax.psum_scatter(jnp.stack(downs_list).reshape(-1), "dp", scatter_dimension=0, tiled=True),
        lax.psum_scatter(jnp.stack(ups_list).reshape(-1), "dp", scatter_dimension=0, tiled=True),
        lax.psum_scatter(grad_out_down.reshape(-1), "dp", scatter_dimension=0, tiled=True),
        lax.psum_scatter(grad_out_up.reshape(-1), "dp", scatter_dimension=0, tiled=True),
        lax.psum_scatter(grad_fc1_down.reshape(-1), "dp", scatter_dimension=0, tiled=True),
        lax.psum_scatter(grad_fc1_up[:, :FF].reshape(-1), "dp", scatter_dimension=0, tiled=True),
        lax.psum_scatter(grad_fc2_down[:FF].reshape(-1), "dp", scatter_dimension=0, tiled=True),
        lax.psum_scatter(grad_fc2_up.reshape(-1), "dp", scatter_dimension=0, tiled=True),
    )
    return (
        output,
        grad_tokens,
        summed[0],
        summed[1],
        summed[2],
        summed[3],
        summed[4],
        summed[5],
        summed[6],
        summed[7],
    )


def solution(mesh):
    return jax.shard_map(
        local,
        mesh=mesh,
        in_specs=(
            P("dp", None),
            P("dp"),
            P("dp"),
            P("dp"),
            P("dp"),
            P(),
            P(),
            P(),
            P(),
            P(),
            P(),
            P(),
            P(),
            P(),
            P(),
            P(),
            P(),
            P("dp", None),
        ),
        out_specs=(
            P("dp", None),
            P("dp", None),
            P("dp"),
            P("dp"),
            P("dp"),
            P("dp"),
            P("dp"),
            P("dp"),
            P("dp"),
            P("dp"),
        ),
        check_vma=False,
    )
```

```python
import functools

import jax
import jax.numpy as jnp
from jax import lax
from jax.experimental import pallas as pl
from jax.experimental.pallas import tpu as pltpu
from jax.sharding import PartitionSpec as P

D = 1152
HEADS = 16
HEAD_DIM = 72
FF = 4304
FP = 4352
IMG = 729
RANK = 16
ADAPTERS = 8
epsilon = 1e-06


MESH = pl.DeviceIdType.MESH
PLANE = 8
STRIDE = 1
ROWS = (216, 72, 72, 272)
WIDE = (D, D, FP, D)
TILES = tuple(rows // 8 for rows in ROWS)
PIECES = (
    (0, (0, 14), (14, 13)),
    (1, (0, 5), (5, 4)),
    (2, (0, 4), (4, 5)),
    (3, (0, 17), (17, 17)),
)


def remote(src, dst, send, recv, to):
    return pltpu.make_async_remote_copy(src_ref=src, dst_ref=dst, send_sem=send, recv_sem=recv, device_id=(to,), device_id_type=MESH)

def gather_kernel(layers, qkv, out, fc1, fc2, o_qkv, o_out, o_fc1, o_fc2,
                  h_qkv, h_out, h_fc1, h_fc2, ahead, ahead_in, wide, b_qkv, b_out, b_fc1, b_fc2,
                  pair_send, pair_recv, ahead_sem, own_sem, z_send, hop_send, pair_out, ici_recv, pair_in):
    me = lax.axis_index("dp")
    core = lax.rem(me, 2)
    x = lax.rem(me // 2, 2)
    y = lax.rem(me // 4, 2)
    z = me // PLANE
    chip = me // 2
    chips = 4 * layers
    mate = me + 1 - 2 * core
    to_x = me + 2 - 4 * x
    to_y = me + 4 - 8 * y
    barrier = pltpu.get_barrier_semaphore()
    def greet(peer):
        pl.semaphore_signal(barrier, inc=1, device_id=(peer,), device_id_type=MESH)
    for peer in (mate, to_x, to_y):
        greet(peer)
    nxt = lax.rem(chip + 1, chips) * 2 + core
    prv = lax.rem(chip + chips - 1, chips) * 2 + core
    greet(nxt)
    greet(prv)
    spot_in_layer = lax.rem(me, PLANE)
    greet(lax.rem(z + 1, layers) * PLANE + spot_in_layer)
    greet(lax.rem(z + layers - 1, layers) * PLANE + spot_in_layer)
    pl.semaphore_wait(barrier, 7)

    ins = (qkv, out, fc1, fc2)
    held = (h_qkv, h_out, h_fc1, h_fc2)
    outs = (o_qkv, o_out, o_fc1, o_fc2)
    blocks = (b_qkv, b_out, b_fc1, b_fc2)
    for a in range(4):
        remote(ins[a], held[a].at[core], pair_send.at[a], pair_recv.at[a], mate).start()
        pltpu.make_async_copy(ins[a], held[a].at[core], own_sem.at[a]).start()

    def pair_wait(a):
        pltpu.make_async_copy(ins[a], held[a].at[core], own_sem.at[a]).wait()
        remote(ins[a], held[a].at[1 - core], pair_send.at[a], pair_recv.at[a], mate).wait_recv()

    def build(a):
        half = ROWS[a] // 2
        w = WIDE[a]
        wide[0:half, 0:w] = held[a][0].astype(jnp.float32)
        wide[half:2 * half, 0:w] = held[a][1].astype(jnp.float32)
        blocks[a][...] = wide[0:2 * half, 0:w].reshape(half // 4, 8, w).astype(jnp.bfloat16)

    def build_fc2():
        wide[0:135, 0:D] = held[3][0].astype(jnp.float32)
        lead = wide[134:135, 0:D] + held[3][1, 0:1].astype(jnp.float32)
        wide[134:135, 0:D] = lead
        wide[135:269, 0:D] = held[3][1].astype(jnp.float32)[1:135]
        ahead[...] = wide[0:48, 0:D].astype(jnp.bfloat16)
        remote(ahead, ahead_in, ahead_sem.at[0], ahead_sem.at[1], prv).start()
    def finish_fc2():
        remote(ahead, ahead_in, ahead_sem.at[0], ahead_sem.at[1], prv).wait_recv()
        more = ahead_in[...].astype(jnp.float32)
        wide[269:269 + 48, 0:D] = jnp.where(chip + 1 < chips, more, 0.0)
        moved = pltpu.roll(wide[0:320, 0:D], 320 - 3 * chip, axis=0)[0:272]
        b_fc2[...] = moved.reshape(34, 8, D).astype(jnp.bfloat16)

    def spot(p, m, c):
        a, *cuts = PIECES[p]
        at, rows = cuts[c]
        return outs[a].at[pl.ds(m * TILES[a] + at, rows)]

    levels = [(d, s) for d in range(layers) for s in ((0,) if d == 0 else (-1, 1))]
    plane = lax.rem(chip, 4)
    corners = (plane, plane + 1 - 2 * x, plane + 2 - 4 * y, 3 - plane)

    def there(d, s):
        return (z - d >= 0) if s < 0 else (z + d < layers)

    def also(yes, go):
        if yes is None:
            go()
        else:
            pl.when(yes)(go)

    def level(d, s, go):
        also(None if d == 0 else there(d, s), go)

    def run(c):
        def cut(p):
            a, *cuts = PIECES[p]
            return blocks[a].at[pl.ds(*cuts[c])]

        def hops(p, src, m, slot, ways):
            for w in ways:
                if w == 2:
                    remote(src, spot(p, m, c), pair_out.at[p, slot], pair_in.at[p, m], mate).start()
                else:
                    remote(src, spot(p, m, c), hop_send.at[p, slot, w], ici_recv.at[p, m], (to_x, to_y)[w]).start()

        def along(p, src, m, slot, up, act):
            def go():
                d = remote(src, spot(p, m, c), z_send.at[p, slot, up], ici_recv.at[p, m], me + PLANE if up else me - PLANE)
                act(d)
            pl.when((z + 1 < layers) if up else (z > 0))(go)

        def arrived(p, m):
            s = spot(p, m, c)
            pltpu.make_async_copy(s, s, ici_recv.at[p, m]).wait()
            return s

        start = lambda d: d.start()
        finish = lambda d: d.wait_send()

        def event(p, g, act):
            n = len(levels)
            if g == 0:
                hops(p, cut(p), chip, 0, (0, 1))
                for up in (0, 1):
                    along(p, cut(p), chip, 0, up, start)
            for i, (d, s) in enumerate(levels):
                zz = z + s * d
                if d >= 1 and d == g:
                    def go():
                        m = zz * 4 + corners[0]
                        src = arrived(p, m)
                        along(p, src, m, i, int(s < 0), start)
                        hops(p, src, m, i, (0, 1, 2))
                    level(d, s, go)
                if d + 1 == g:
                    def go():
                        m = zz * 4 + corners[1]
                        hops(p, arrived(p, m), m, n + i, (1, 2) if c == 0 else (2,))
                        m = zz * 4 + corners[2]
                        hops(p, arrived(p, m), m, 2 * n + i, (2,) if c == 0 else (0, 2))
                    level(d, s, go)
                if d + 2 == g:
                    def go():
                        m = zz * 4 + corners[3]
                        hops(p, arrived(p, m), m, 3 * n + i, (2,))
                    level(d, s, go)

        launched = {0: 0, 1: 1, 2: 2, 3: 3}
        made = -1
        count = len(PIECES)
        last = STRIDE * (count - 1) + layers + 1
        for t in range(last + 1):
            for p in range(count):
                g = t - STRIDE * p
                if 0 <= g <= layers + 1:
                    a = PIECES[p][0]
                    if g == 0 and a > made:
                        made = a
                        pair_wait(a)
                        if a < 3:
                            build(a)
                        else:
                            build_fc2()
                            finish_fc2()
                        pltpu.make_async_copy(blocks[a], outs[a].at[pl.ds(chip * TILES[a], TILES[a])], own_sem.at[a]).start()
                    event(p, g, start)
        for p in range(count):
            for k in range(4):
                for d, s in levels:
                    if k == 0 and d == 0:
                        continue
                    def go():
                        m = (z + s * d) * 4 + corners[k]
                        q = spot(p, m, 1 - c)
                        pltpu.make_async_copy(q, q, pair_in.at[p, m]).wait()
                    level(d, s, go)
        n = len(levels)
        for p in range(count):
            src = cut(p)
            def sent(sem):
                pltpu.make_async_copy(src, src, sem).wait()
            for i, (d, s) in enumerate(levels):
                def go():
                    sent(hop_send.at[p, i, 0])
                    sent(hop_send.at[p, i, 1])
                    if c == 0:
                        sent(hop_send.at[p, n + i, 1])
                    else:
                        sent(hop_send.at[p, 2 * n + i, 0])
                    for k in range(4):
                        if k or d:
                            sent(pair_out.at[p, k * n + i])
                    for up in (0, 1):
                        if d == 0 or up == int(s < 0):
                            pl.when((z + 1 < layers) if up else (z > 0))(lambda: sent(z_send.at[p, i, up]))
                level(d, s, go)
        for a in range(4):
            remote(ins[a], held[a].at[core], pair_send.at[a], pair_recv.at[a], mate).wait_send()
            pltpu.make_async_copy(blocks[a], outs[a].at[pl.ds(chip * TILES[a], TILES[a])], own_sem.at[a]).wait()
        remote(ahead, ahead_in, ahead_sem.at[0], ahead_sem.at[1], prv).wait_send()

    for c in (0, 1):
        @pl.when(core == c)
        def _():
            run(c)

def gather(n, qkv, out, fc1, fc2):
    layers = n // PLANE
    core = lax.rem(lax.axis_index("dp"), 2)
    qkv = qkv.reshape(108, D)
    out = out.reshape(36, D)
    fc1 = jnp.pad(fc1.reshape(36, FF), ((0, 0), (0, FP - FF)))
    half = jnp.zeros((576,), fc2.dtype)
    fc2 = jnp.where(core == 0, jnp.concatenate([fc2, half]), jnp.concatenate([half, fc2])).reshape(135, D)
    chips = 4 * layers
    slots = 2 * layers - 1
    count = len(PIECES)
    dma = pltpu.SemaphoreType.DMA
    return pl.pallas_call(
        functools.partial(gather_kernel, layers),
        out_shape=[jax.ShapeDtypeStruct((TILES[a] * chips, 8, WIDE[a]), jnp.bfloat16) for a in range(4)],
        in_specs=[pl.BlockSpec(memory_space=pl.ANY)] * 4,
        out_specs=[pl.BlockSpec(memory_space=pl.ANY)] * 4,
        scratch_shapes=[
            pltpu.VMEM((2, 108, D), jnp.bfloat16),
            pltpu.VMEM((2, 36, D), jnp.bfloat16),
            pltpu.VMEM((2, 36, FP), jnp.bfloat16),
            pltpu.VMEM((2, 135, D), jnp.bfloat16),
            pltpu.VMEM((48, D), jnp.bfloat16),
            pltpu.VMEM((48, D), jnp.bfloat16),
            pltpu.VMEM((320, FP), jnp.float32),
            pltpu.VMEM((27, 8, D), jnp.bfloat16),
            pltpu.VMEM((9, 8, D), jnp.bfloat16),
            pltpu.VMEM((9, 8, FP), jnp.bfloat16),
            pltpu.VMEM((34, 8, D), jnp.bfloat16),
            dma((4,)), dma((4,)), dma((2,)), dma((4,)), dma((count, slots, 2)),
            dma((count, 3 * slots, 2)), dma((count, 4 * slots)), dma((count, chips)), dma((count, chips)),
        ],
        compiler_params=pltpu.CompilerParams(collective_id=0, has_side_effects=True, vmem_limit_bytes=40 << 20),
        name="gather_weights",
    )(qkv, out, fc1, fc2)


def frozen(qkv, out, fc1, fc2):
    n = lax.axis_size("dp")
    if n == 4 * PLANE:
        w_qkv, w_out, w_fc1, w_fc2 = gather(n, qkv, out, fc1, fc2)
        return (w_qkv.reshape(3, D, D), w_out.reshape(D, D), w_fc1.reshape(D, FP), w_fc2.reshape(FP, D))
    qkv, out, fc1, fc2 = (lax.all_gather(v, "dp", axis=0, tiled=True) for v in (qkv, out, fc1, fc2))
    return (
        qkv.reshape(3, D, D),
        out.reshape(D, D),
        jnp.pad(fc1.reshape(D, FF), ((0, 0), (0, FP - FF))),
        jnp.pad(fc2.reshape(FF, D), ((0, FP - FF), (0, 0))),
    )


ROWS_HERE = 256
SIDE = 3
SPAN = 2 * SIDE + 1
LANES = 128
COLS = 384
STEP = 256
LOG2E = 1.4426950408889634
HIDE = -1e30


def mm(left, right):
    return jnp.dot(left, right, preferred_element_type=jnp.float32)


def mm_t(left, right):
    return lax.dot_general(left, right, (((1,), (1,)), ((), ())), preferred_element_type=jnp.float32)


def t_mm(left, right):
    return lax.dot_general(left, right, (((0,), (0,)), ((), ())), preferred_element_type=jnp.float32)


def moments(rows):
    center = rows - jnp.mean(rows, axis=-1, keepdims=True)
    return center, lax.rsqrt(jnp.mean(center * center, axis=-1, keepdims=True) + epsilon)


def shares_image(low, high):
    return (low * ROWS_HERE + ROWS_HERE - 1) // IMG >= (high * ROWS_HERE) // IMG


def met(me, n, k):
    other = me + k
    inside = (other >= 0) & (other < n)
    low, high = (me, other) if k > 0 else (other, me)
    return inside & shares_image(low, high)


def reach(me, n):
    first = jnp.int32(SIDE)
    last = jnp.int32(SIDE)
    for k in range(1, SIDE + 1):
        first = first - met(me, n, -k).astype(jnp.int32)
        last = last + met(me, n, k).astype(jnp.int32)
    return first, last


def slots_of(place, me):
    first = (me * ROWS_HERE) // IMG
    edge = first * IMG
    inside = jnp.where(place < edge + IMG, 0, 1)
    return jnp.where((place >= edge) & (place < edge + 2 * IMG), inside, -1)


def chosen_columns(adapters, images, me, block):
    shape = (ROWS_HERE, LANES)
    place = (me + block - SIDE) * ROWS_HERE + lax.broadcasted_iota(jnp.int32, shape, 0)
    column = lax.broadcasted_iota(jnp.int32, shape, 1)
    first = (me * ROWS_HERE) // IMG
    second = jnp.minimum(first + 1, images - 1)
    adapter = jnp.where(slots_of(place, me) == 0, adapters[first], adapters[second])
    return ((column >= adapter * RANK) & (column < adapter * RANK + RANK)).astype(jnp.float32)


def same_image(me, keys_block, query_block):
    shape = (ROWS_HERE, ROWS_HERE)
    key = (me + keys_block - SIDE) * ROWS_HERE + lax.broadcasted_iota(jnp.int32, shape, 0)
    query = (me + query_block - SIDE) * ROWS_HERE + lax.broadcasted_iota(jnp.int32, shape, 1)
    one = slots_of(key, me)
    return jnp.where((one == slots_of(query, me)) & (one >= 0), 0.0, HIDE)


def forward_kernel(n, images, tokens, w_qkv, w_out, w_fc1, w_fc2, gain, bias, fbias, qkv_down, qkv_up, out_down, out_up,
                   ff_down, fc1_up, fc2_down, fc2_up, adapters,
                   output, normed1, low_qkv, qt, kv, lse, mixed_t, mixed, low_out, resid, normed2, low_fc1, pre, low_fc2,
                   xs, v_qkv, v_out, v_fc1, v_fc2, tmp, shade, acc, act, x_send, x_recv, w_sem, fc1_sem, fc2_sem):
    me = lax.axis_index("dp")
    pltpu.make_async_copy(w_qkv, v_qkv, w_sem.at[0]).start()
    pltpu.make_async_copy(w_out, v_out, w_sem.at[1]).start()
    near = [k for k in range(-SIDE, SIDE + 1) if k]
    barrier = pltpu.get_barrier_semaphore()
    total = jnp.int32(0)
    for k in near:
        yes = met(me, n, k)
        total = total + yes.astype(jnp.int32)

        @pl.when(yes)
        def _():
            pl.semaphore_signal(barrier, inc=1, device_id=(me + k,), device_id_type=MESH)

    pl.semaphore_wait(barrier, total)

    def shift(i, k):
        return remote(tokens, xs.at[SIDE - k], x_send.at[i], x_recv.at[SIDE - k], me + k)

    for i, k in enumerate(near):
        @pl.when(met(me, n, k))
        def _():
            shift(i, k).start()
    xs[SIDE] = tokens[...]
    for i, k in enumerate(near):
        @pl.when(met(me, n, k))
        def _():
            pltpu.make_async_copy(xs.at[SIDE + k], xs.at[SIDE + k], x_recv.at[SIDE + k]).wait()
    begin, end = reach(me, n)

    pltpu.make_async_copy(w_qkv, v_qkv, w_sem.at[0]).wait()

    def project(j, carry):
        center, inv = moments(xs[j].astype(jnp.float32))
        n1 = (center * inv * gain[0:1] + bias[0:1]).astype(jnp.bfloat16)
        select = chosen_columns(adapters, images, me, j)
        @pl.when(j == SIDE)
        def _():
            normed1[...] = n1
        for p in range(3):
            low = (select * mm(n1, qkv_down[p])).astype(jnp.bfloat16)
            @pl.when(j == SIDE)
            def _():
                low_qkv[p] = low
            for c in range(0, D, COLS):
                y = mm(n1, v_qkv[p * D:(p + 1) * D, c:c + COLS]) + mm(low, qkv_up[p, :, c:c + COLS])
                if p != 1:
                    y = y + bias[(1, 0, 2)[p]:(1, 0, 2)[p] + 1, c:c + COLS]
                tmp[:, c:c + COLS] = y
            if p == 0:
                qt[j] = tmp[...].T.reshape(HEADS, HEAD_DIM, ROWS_HERE).astype(jnp.bfloat16)
            else:
                for h in range(HEADS):
                    kv[p - 1, j, h] = tmp[:, h * HEAD_DIM:(h + 1) * HEAD_DIM].astype(jnp.bfloat16)
        shade[j] = same_image(me, j, SIDE)
        return carry

    lax.fori_loop(begin, end + 1, project, 0)
    factor = HEAD_DIM ** (-0.5) * LOG2E

    def one_head(h, carry):
        q = qt[SIDE, h]

        def one_block(j, state):
            top, total, o = state
            s = mm(kv[0, j, h], q) * factor + shade[j]
            new = jnp.maximum(top, jnp.max(s, axis=0, keepdims=True))
            fade = jnp.exp2(top - new)
            p = jnp.exp2(s - new)
            total = total * fade + jnp.sum(p, axis=0, keepdims=True)
            o = o * fade + t_mm(kv[1, j, h], p.astype(jnp.bfloat16))
            return new, total, o

        start = (jnp.full((1, ROWS_HERE), HIDE, jnp.float32), jnp.zeros((1, ROWS_HERE), jnp.float32),
                 jnp.zeros((HEAD_DIM, ROWS_HERE), jnp.float32))
        top, total, o = lax.fori_loop(begin, end + 1, one_block, start)
        mixed_t[h] = o / total
        lse[h] = top + jnp.log2(total)
        return carry

    lax.fori_loop(0, HEADS, one_head, 0)
    att = mixed_t[...].reshape(D, ROWS_HERE).T.astype(jnp.bfloat16)
    mixed[...] = att
    select = chosen_columns(adapters, images, me, SIDE)
    pltpu.make_async_copy(w_out, v_out, w_sem.at[1]).wait()
    low = (select * mm(att, out_down[...])).astype(jnp.bfloat16)
    low_out[...] = low
    for c in range(0, D, COLS):
        s = slice(c, c + COLS)
        resid[:, s] = tokens[:, s].astype(jnp.float32) + mm(att, v_out[:, s]) + bias[3:4, s] + mm(low, out_up[:, s])
    center, inv = moments(resid[...])
    n2 = (center * inv * gain[1:2] + bias[4:5]).astype(jnp.bfloat16)
    normed2[...] = n2
    low1 = (select * mm(n2, ff_down[...])).astype(jnp.bfloat16)
    low_fc1[...] = low1

    def fetch1(i):
        slot = lax.rem(i, 2)
        cols = pl.ds(pl.multiple_of(i * STEP, STEP), STEP)
        return pltpu.make_async_copy(w_fc1.at[:, cols], v_fc1.at[slot], fc1_sem.at[slot])

    def fetch(i):
        slot = lax.rem(i, 2)
        rows = pl.ds(pl.multiple_of(i * STEP, STEP), STEP)
        return pltpu.make_async_copy(w_fc2.at[rows, :], v_fc2.at[slot], fc2_sem.at[slot])

    fetch1(0).start()
    fetch(0).start()
    acc[...] = jnp.zeros_like(acc)

    def feed(i, carry):
        @pl.when(i + 1 < FP // STEP)
        def _():
            fetch1(i + 1).start()
        fetch1(i).wait()
        s = pl.ds(pl.multiple_of(i * STEP, STEP), STEP)
        y = mm(n2, v_fc1[lax.rem(i, 2)]) + fbias[:, s] + mm(low1, fc1_up[:, s])
        pre[:, s] = y
        a = (0.5 * y * (1.0 + jnp.tanh(0.7978845608028654 * (y + 0.044715 * y * y * y)))).astype(jnp.bfloat16)
        act[:, s] = a
        acc[...] += mm(a, fc2_down[s, :])
        return carry

    lax.fori_loop(0, FP // STEP, feed, 0)
    low2 = (select * acc[...]).astype(jnp.bfloat16)
    low_fc2[...] = low2
    for c in range(0, D, COLS):
        s = slice(c, c + COLS)
        tmp[:, s] = resid[:, s] + bias[5:6, s] + mm(low2, fc2_up[:, s])

    def close(i, carry):
        @pl.when(i + 1 < FP // STEP)
        def _():
            fetch(i + 1).start()
        fetch(i).wait()
        s = pl.ds(pl.multiple_of(i * STEP, STEP), STEP)
        tmp[...] += mm(act[:, s], v_fc2[lax.rem(i, 2)])
        return carry

    lax.fori_loop(0, FP // STEP, close, 0)
    output[...] = tmp[...].astype(jnp.bfloat16)
    for i, k in enumerate(near):
        @pl.when(met(me, n, k))
        def _():
            shift(i, k).wait_send()


def forward(n, tokens, w_qkv, w_out, w_fc1, w_fc2, gain, bias, fbias, qkv_down, qkv_up, out_down, out_up, ff_down, fc1_up,
            fc2_down, fc2_up, adapters):
    bf, f32 = jnp.bfloat16, jnp.float32
    r = ROWS_HERE
    outs = [
        ((r, D), bf), ((r, D), bf), ((3, r, LANES), bf), ((SPAN, HEADS, HEAD_DIM, r), bf), ((2, SPAN, HEADS, r, HEAD_DIM), bf),
        ((HEADS, 1, r), f32), ((HEADS, HEAD_DIM, r), f32), ((r, D), bf), ((r, LANES), bf), ((r, D), f32), ((r, D), bf),
        ((r, LANES), bf), ((r, FP), f32), ((r, LANES), bf),
    ]
    vmem = pl.BlockSpec(memory_space=pltpu.VMEM)
    away = pl.BlockSpec(memory_space=pl.ANY)
    dma = pltpu.SemaphoreType.DMA
    return pl.pallas_call(
        functools.partial(forward_kernel, n, adapters.shape[0]),
        out_shape=[jax.ShapeDtypeStruct(*o) for o in outs],
        in_specs=[vmem] + [away] * 4 + [vmem] * 11 + [pl.BlockSpec(memory_space=pltpu.SMEM)],
        out_specs=[vmem] * len(outs),
        scratch_shapes=[
            pltpu.VMEM((SPAN, r, D), bf), pltpu.VMEM((3 * D, D), bf), pltpu.VMEM((D, D), bf), pltpu.VMEM((2, D, STEP), bf),
            pltpu.VMEM((2, STEP, D), bf), pltpu.VMEM((r, D), f32), pltpu.VMEM((SPAN, r, r), f32),
            pltpu.VMEM((r, LANES), f32), pltpu.VMEM((r, FP), bf), dma((6,)), dma((SPAN,)), dma((2,)), dma((2,)), dma((2,)),
        ],
        compiler_params=pltpu.CompilerParams(collective_id=1, has_side_effects=True, vmem_limit_bytes=63 << 20),
        name="layer_forward",
    )(tokens, w_qkv, w_out, w_fc1, w_fc2, gain, bias, fbias, qkv_down, qkv_up, out_down, out_up, ff_down, fc1_up, fc2_down,
      fc2_up, adapters)


def norm_back(center, inv, gain_row, grad):
    u = center * inv
    g = grad * gain_row
    return inv * (g - jnp.mean(g, axis=-1, keepdims=True) - u * jnp.mean(g * u, axis=-1, keepdims=True))


def backward_kernel(n, images, cotangent, tokens, w_qkv, w_out, w_fc1, w_fc2, gain, bias, qkv_down, qkv_up, out_down, out_up,
                    ff_down, fc1_up, fc2_down, fc2_up, adapters,
                    normed1, low_qkv, qt, kv, lse, mixed_t, mixed, low_out, resid, normed2, low_fc1, pre, low_fc2,
                    grad_tokens, g_qkv_down, g_qkv_up, g_out_down, g_out_up, g_ff_down, g_fc1_up, g_fc2_down, g_fc2_up,
                    v_qkv, v_out, v_fc1, v_fc2, v_kv, own_kv, wide, dres, acc, dat, stat, dq, dk, dv,
                    send, recv, w_sem, fc1_sem, fc2_sem, kv_sem):
    me = lax.axis_index("dp")
    own = pltpu.make_async_copy(kv.at[:, SIDE], own_kv, w_sem.at[0])
    own.start()
    get_out = pltpu.make_async_copy(w_out, v_out, w_sem.at[1])
    get_out.start()
    get_qkv = pltpu.make_async_copy(w_qkv, v_qkv, w_sem.at[2])
    get_qkv.start()

    def fetch1(i):
        slot = lax.rem(i, 2)
        cols = pl.ds(pl.multiple_of(i * STEP, STEP), STEP)
        return pltpu.make_async_copy(w_fc1.at[:, cols], v_fc1.at[slot], fc1_sem.at[slot])

    def fetch2(i):
        slot = lax.rem(i, 2)
        rows = pl.ds(pl.multiple_of(i * STEP, STEP), STEP)
        return pltpu.make_async_copy(w_fc2.at[rows, :], v_fc2.at[slot], fc2_sem.at[slot])

    fetch1(0).start()
    fetch2(0).start()
    near = [k for k in range(-SIDE, SIDE + 1) if k]
    barrier = pltpu.get_barrier_semaphore()
    total = jnp.int32(0)
    for k in near:
        yes = met(me, n, k)
        total = total + yes.astype(jnp.int32)

        @pl.when(yes)
        def _():
            pl.semaphore_signal(barrier, inc=1, device_id=(me + k,), device_id_type=MESH)

    begin, end = reach(me, n)
    bf = jnp.bfloat16
    select = chosen_columns(adapters, images, me, SIDE)
    e = cotangent[...]
    g_fc2_up[...] = t_mm(low_fc2[...], e)
    glow2 = (select * mm_t(e, fc2_up[...])).astype(bf)
    acc[...] = jnp.zeros_like(acc)
    wide[...] = jnp.zeros_like(wide)
    low1 = low_fc1[...]

    def feed(i, carry):
        @pl.when(i + 1 < FP // STEP)
        def _():
            fetch1(i + 1).start()
            fetch2(i + 1).start()
        fetch1(i).wait()
        fetch2(i).wait()
        slot = lax.rem(i, 2)
        s = pl.ds(pl.multiple_of(i * STEP, STEP), STEP)
        y = pre[:, s]
        t = jnp.tanh(0.7978845608028654 * (y + 0.044715 * y * y * y))
        half = 0.5 * (1.0 + t)
        a = (y * half).astype(bf)
        slope = half + 0.5 * y * (1.0 - t * t) * (0.7978845608028654 * (1.0 + 3.0 * 0.044715 * y * y))
        g_fc2_down[s, :] = t_mm(a, glow2)
        g = mm_t(e, v_fc2[slot]) + mm_t(glow2, fc2_down[s, :])
        gp = (g * slope).astype(bf)
        g_fc1_up[:, s] = t_mm(low1, gp)
        acc[...] += mm_t(gp, fc1_up[:, s])
        wide[...] += mm_t(gp, v_fc1[slot])
        return carry

    lax.fori_loop(0, FP // STEP, feed, 0)
    glow1 = (select * acc[...]).astype(bf)
    g_ff_down[...] = t_mm(normed2[...], glow1)
    center, inv = moments(resid[...])
    dres[...] = e.astype(jnp.float32) + norm_back(center, inv, gain[1:2], wide[...] + mm_t(glow1, ff_down[...]))
    gb = dres[...].astype(bf)
    g_out_up[...] = t_mm(low_out[...], gb)
    glow = (select * mm_t(gb, out_up[...])).astype(bf)
    g_out_down[...] = t_mm(mixed[...], glow)
    get_out.wait()
    for c in range(0, D, COLS):
        wide[:, c:c + COLS] = mm_t(gb, v_out[c:c + COLS, :]) + mm_t(glow, out_down[c:c + COLS, :])
    da = wide[...].T.reshape(HEADS, HEAD_DIM, ROWS_HERE).astype(bf)
    dat[SIDE] = da
    delta = jnp.sum(da.astype(jnp.float32) * mixed_t[...], axis=1, keepdims=True)
    stat[SIDE, :, 0:1, :] = lse[...]
    stat[SIDE, :, 1:2, :] = delta

    pl.semaphore_wait(barrier, total)

    def shift(i, k, what):
        ref = (dat, stat)[what]
        return remote(ref.at[SIDE], ref.at[SIDE - k], send.at[what, i], recv.at[what, SIDE - k], me + k)

    for i, k in enumerate(near):
        @pl.when(met(me, n, k))
        def _():
            shift(i, k, 0).start()
            shift(i, k, 1).start()

    factor = HEAD_DIM ** (-0.5) * LOG2E
    dq[...] = jnp.zeros_like(dq)

    def block(h, keys, vals, q, d, st, shade, which):
        s = mm(keys, q) * factor + shade
        p = jnp.exp2(s - st[0:1])
        ds = (p * (mm(vals, d) - st[1:2])).astype(bf)
        if which != 2:
            dq[h] += t_mm(keys, ds)
        if which == 0:
            dk[h] = mm_t(q, ds)
            dv[h] = mm_t(d, p.astype(bf))
        if which == 2:
            dk[h] += mm_t(q, ds)
            dv[h] += mm_t(d, p.astype(bf))

    own.wait()
    shade = same_image(me, SIDE, SIDE)

    def own_head(h, carry):
        block(h, own_kv[0, h], own_kv[1, h], qt[SIDE, h], dat[SIDE, h], stat[SIDE, h], shade, 0)
        return carry

    def get_kv(j):
        slot = lax.rem(j, 2)
        return pltpu.make_async_copy(kv.at[:, j], v_kv.at[slot], kv_sem.at[slot])

    get_kv(begin).start()
    lax.fori_loop(0, HEADS, own_head, 0)

    def pass_one(j, carry):
        @pl.when(j < end)
        def _():
            get_kv(j + 1).start()
        get_kv(j).wait()

        @pl.when(j != SIDE)
        def _():
            shade = same_image(me, j, SIDE)
            slot = lax.rem(j, 2)

            def head(h, carry):
                block(h, v_kv[slot, 0, h], v_kv[slot, 1, h], qt[SIDE, h], dat[SIDE, h], stat[SIDE, h], shade, 1)
                return carry

            lax.fori_loop(0, HEADS, head, 0)
        return carry

    lax.fori_loop(begin, end + 1, pass_one, 0)
    for i, k in enumerate(near):
        @pl.when(met(me, n, k))
        def _():
            for what, ref in enumerate((dat, stat)):
                pltpu.make_async_copy(ref.at[SIDE + k], ref.at[SIDE + k], recv.at[what, SIDE + k]).wait()

    def pass_two(j, carry):
        @pl.when(j != SIDE)
        def _():
            shade = same_image(me, SIDE, j)

            def head(h, carry):
                block(h, own_kv[0, h], own_kv[1, h], qt[j, h], dat[j, h], stat[j, h], shade, 2)
                return carry

            lax.fori_loop(0, HEADS, head, 0)
        return carry

    lax.fori_loop(begin, end + 1, pass_two, 0)
    get_qkv.wait()
    n1 = normed1[...]
    for p, source in enumerate((dq, dk, dv)):
        value = source[...] * HEAD_DIM ** (-0.5) if p < 2 else source[...]
        g = value.reshape(D, ROWS_HERE).T.astype(bf)
        g_qkv_up[p * LANES:(p + 1) * LANES, :] = t_mm(low_qkv[p], g)
        glow = (select * mm_t(g, qkv_up[p])).astype(bf)
        g_qkv_down[p * D:(p + 1) * D, :] = t_mm(n1, glow)
        for c in range(0, D, COLS):
            s = slice(c, c + COLS)
            y = mm_t(g, v_qkv[p * D + c:p * D + c + COLS, :]) + mm_t(glow, qkv_down[p, s, :])
            wide[:, s] = y if p == 0 else wide[:, s] + y
    center, inv = moments(tokens[...].astype(jnp.float32))
    grad_tokens[...] = (dres[...] + norm_back(center, inv, gain[0:1], wide[...])).astype(bf)
    for i, k in enumerate(near):
        @pl.when(met(me, n, k))
        def _():
            shift(i, k, 0).wait_send()
            shift(i, k, 1).wait_send()


def backward(n, cotangent, tokens, w_qkv, w_out, w_fc1, w_fc2, gain, bias, qkv_down, qkv_up, out_down, out_up, ff_down, fc1_up,
             fc2_down, fc2_up, adapters, saved):
    bf, f32 = jnp.bfloat16, jnp.float32
    r = ROWS_HERE
    outs = [((r, D), bf), ((3 * D, LANES), f32), ((3 * LANES, D), f32), ((D, LANES), f32), ((LANES, D), f32), ((D, LANES), f32),
            ((LANES, FP), f32), ((FP, LANES), f32), ((LANES, D), f32)]
    vmem = pl.BlockSpec(memory_space=pltpu.VMEM)
    away = pl.BlockSpec(memory_space=pl.ANY)
    dma = pltpu.SemaphoreType.DMA
    heads = (HEADS, HEAD_DIM, r)
    return pl.pallas_call(
        functools.partial(backward_kernel, n, adapters.shape[0]),
        out_shape=[jax.ShapeDtypeStruct(*o) for o in outs],
        in_specs=[vmem] * 2 + [away] * 4 + [vmem] * 10 + [pl.BlockSpec(memory_space=pltpu.SMEM)] + [vmem] * 3 + [away] + [vmem] * 9,
        out_specs=[vmem] * len(outs),
        scratch_shapes=[
            pltpu.VMEM((3 * D, D), bf), pltpu.VMEM((D, D), bf), pltpu.VMEM((2, D, STEP), bf), pltpu.VMEM((2, STEP, D), bf),
            pltpu.VMEM((2, 2, HEADS, r, HEAD_DIM), bf), pltpu.VMEM((2, HEADS, r, HEAD_DIM), bf),
            pltpu.VMEM((r, D), f32), pltpu.VMEM((r, D), f32), pltpu.VMEM((r, LANES), f32),
            pltpu.VMEM((SPAN,) + heads, bf), pltpu.VMEM((SPAN, HEADS, 8, r), f32),
            pltpu.VMEM(heads, f32), pltpu.VMEM(heads, f32), pltpu.VMEM(heads, f32),
            dma((2, 6)), dma((2, SPAN)), dma((3,)), dma((2,)), dma((2,)), dma((2,)),
        ],
        compiler_params=pltpu.CompilerParams(collective_id=2, has_side_effects=True, vmem_limit_bytes=63 << 20),
        name="layer_backward",
    )(cotangent, tokens, w_qkv, w_out, w_fc1, w_fc2, gain, bias, qkv_down, qkv_up, out_down, out_up, ff_down, fc1_up, fc2_down,
      fc2_up, adapters, *saved)


def local(
    tokens,
    qkv_weights,
    out_weights,
    fc1_weights,
    fc2_weights,
    ln_gain,
    bias_model,
    first_feedforward_bias,
    qkv_down,
    qkv_up,
    out_down,
    out_up,
    first_feedforward_down,
    fc1_up,
    fc2_down,
    fc2_up,
    adapter_of_image,
    cotangent,
):
    n = lax.axis_size("dp")
    w_qkv, w_out, w_fc1, w_fc2 = frozen(qkv_weights, out_weights, fc1_weights, fc2_weights)
    w_qkv = w_qkv.reshape(3 * D, D)
    tail = FP - FF
    fbias = jnp.pad(first_feedforward_bias, (0, tail))[None]
    fc1_up = jnp.pad(fc1_up, ((0, 0), (0, tail)))
    fc2_down = jnp.pad(fc2_down, ((0, tail), (0, 0)))
    factors = (qkv_down, qkv_up, out_down, out_up, first_feedforward_down, fc1_up, fc2_down, fc2_up, adapter_of_image)
    output, *saved = forward(n, tokens, w_qkv, w_out, w_fc1, w_fc2, ln_gain, bias_model, fbias, *factors)
    grad_tokens, *grads = backward(n, cotangent, tokens, w_qkv, w_out, w_fc1, w_fc2, ln_gain, bias_model, *factors, saved)
    grads[5] = grads[5][:, :FF]
    grads[6] = grads[6][:FF]
    summed = [lax.psum_scatter(g.reshape(-1), "dp", scatter_dimension=0, tiled=True) for g in grads]
    return (output, grad_tokens, *summed)


def solution(mesh):
    return jax.shard_map(
        local,
        mesh=mesh,
        in_specs=(P("dp", None),) + (P("dp"),) * 4 + (P(),) * 12 + (P("dp", None),),
        out_specs=(P("dp", None),) * 2 + (P("dp"),) * 8,
        check_vma=False,
    )
```

```python
import functools

import jax
import jax.numpy as jnp
from jax import lax
from jax.experimental import pallas as pl
from jax.experimental.pallas import tpu as pltpu
from jax.sharding import PartitionSpec as P

D = 1152
HEADS = 16
HEAD_DIM = 72
FF = 4304
FP = 4352
IMG = 729
RANK = 16
ADAPTERS = 8
epsilon = 1e-06


MESH = pl.DeviceIdType.MESH
PLANE = 8
STRIDE = 1
ROWS = (216, 72, 72, 272)
WIDE = (D, D, FP, D)
TILES = tuple(rows // 8 for rows in ROWS)
PIECES = (
    (0, (0, 14), (14, 13)),
    (1, (0, 5), (5, 4)),
    (2, (0, 4), (4, 5)),
    (3, (0, 17), (17, 17)),
)


def remote(src, dst, send, recv, to):
    return pltpu.make_async_remote_copy(src_ref=src, dst_ref=dst, send_sem=send, recv_sem=recv, device_id=(to,), device_id_type=MESH)

def gather_kernel(layers, qkv, out, fc1, fc2, o_qkv, o_out, o_fc1, o_fc2,
                  h_qkv, h_out, h_fc1, h_fc2, ahead, ahead_in, wide, b_qkv, b_out, b_fc1, b_fc2,
                  pair_send, pair_recv, ahead_sem, own_sem, z_send, hop_send, pair_out, ici_recv, pair_in):
    me = lax.axis_index("dp")
    core = lax.rem(me, 2)
    x = lax.rem(me // 2, 2)
    y = lax.rem(me // 4, 2)
    z = me // PLANE
    chip = me // 2
    chips = 4 * layers
    mate = me + 1 - 2 * core
    to_x = me + 2 - 4 * x
    to_y = me + 4 - 8 * y
    barrier = pltpu.get_barrier_semaphore()
    def greet(peer):
        pl.semaphore_signal(barrier, inc=1, device_id=(peer,), device_id_type=MESH)
    for peer in (mate, to_x, to_y):
        greet(peer)
    nxt = lax.rem(chip + 1, chips) * 2 + core
    prv = lax.rem(chip + chips - 1, chips) * 2 + core
    greet(nxt)
    greet(prv)
    spot_in_layer = lax.rem(me, PLANE)
    greet(lax.rem(z + 1, layers) * PLANE + spot_in_layer)
    greet(lax.rem(z + layers - 1, layers) * PLANE + spot_in_layer)
    pl.semaphore_wait(barrier, 7)

    ins = (qkv, out, fc1, fc2)
    held = (h_qkv, h_out, h_fc1, h_fc2)
    outs = (o_qkv, o_out, o_fc1, o_fc2)
    blocks = (b_qkv, b_out, b_fc1, b_fc2)
    for a in range(4):
        remote(ins[a], held[a].at[core], pair_send.at[a], pair_recv.at[a], mate).start()
        pltpu.make_async_copy(ins[a], held[a].at[core], own_sem.at[a]).start()

    def pair_wait(a):
        pltpu.make_async_copy(ins[a], held[a].at[core], own_sem.at[a]).wait()
        remote(ins[a], held[a].at[1 - core], pair_send.at[a], pair_recv.at[a], mate).wait_recv()

    def build(a):
        half = ROWS[a] // 2
        w = WIDE[a]
        wide[0:half, 0:w] = held[a][0].astype(jnp.float32)
        wide[half:2 * half, 0:w] = held[a][1].astype(jnp.float32)
        blocks[a][...] = wide[0:2 * half, 0:w].reshape(half // 4, 8, w).astype(jnp.bfloat16)

    def build_fc2():
        wide[0:135, 0:D] = held[3][0].astype(jnp.float32)
        lead = wide[134:135, 0:D] + held[3][1, 0:1].astype(jnp.float32)
        wide[134:135, 0:D] = lead
        wide[135:269, 0:D] = held[3][1].astype(jnp.float32)[1:135]
        ahead[...] = wide[0:48, 0:D].astype(jnp.bfloat16)
        remote(ahead, ahead_in, ahead_sem.at[0], ahead_sem.at[1], prv).start()
    def finish_fc2():
        remote(ahead, ahead_in, ahead_sem.at[0], ahead_sem.at[1], prv).wait_recv()
        more = ahead_in[...].astype(jnp.float32)
        wide[269:269 + 48, 0:D] = jnp.where(chip + 1 < chips, more, 0.0)
        moved = pltpu.roll(wide[0:320, 0:D], 320 - 3 * chip, axis=0)[0:272]
        b_fc2[...] = moved.reshape(34, 8, D).astype(jnp.bfloat16)

    def spot(p, m, c):
        a, *cuts = PIECES[p]
        at, rows = cuts[c]
        return outs[a].at[pl.ds(m * TILES[a] + at, rows)]

    levels = [(d, s) for d in range(layers) for s in ((0,) if d == 0 else (-1, 1))]
    plane = lax.rem(chip, 4)
    corners = (plane, plane + 1 - 2 * x, plane + 2 - 4 * y, 3 - plane)

    def there(d, s):
        return (z - d >= 0) if s < 0 else (z + d < layers)

    def also(yes, go):
        if yes is None:
            go()
        else:
            pl.when(yes)(go)

    def level(d, s, go):
        also(None if d == 0 else there(d, s), go)

    def run(c):
        def cut(p):
            a, *cuts = PIECES[p]
            return blocks[a].at[pl.ds(*cuts[c])]

        def hops(p, src, m, slot, ways):
            for w in ways:
                if w == 2:
                    remote(src, spot(p, m, c), pair_out.at[p, slot], pair_in.at[p, m], mate).start()
                else:
                    remote(src, spot(p, m, c), hop_send.at[p, slot, w], ici_recv.at[p, m], (to_x, to_y)[w]).start()

        def along(p, src, m, slot, up, act):
            def go():
                d = remote(src, spot(p, m, c), z_send.at[p, slot, up], ici_recv.at[p, m], me + PLANE if up else me - PLANE)
                act(d)
            pl.when((z + 1 < layers) if up else (z > 0))(go)

        def arrived(p, m):
            s = spot(p, m, c)
            pltpu.make_async_copy(s, s, ici_recv.at[p, m]).wait()
            return s

        start = lambda d: d.start()
        finish = lambda d: d.wait_send()

        def event(p, g, act):
            n = len(levels)
            if g == 0:
                hops(p, cut(p), chip, 0, (0, 1))
                for up in (0, 1):
                    along(p, cut(p), chip, 0, up, start)
            for i, (d, s) in enumerate(levels):
                zz = z + s * d
                if d >= 1 and d == g:
                    def go():
                        m = zz * 4 + corners[0]
                        src = arrived(p, m)
                        along(p, src, m, i, int(s < 0), start)
                        hops(p, src, m, i, (0, 1, 2))
                    level(d, s, go)
                if d + 1 == g:
                    def go():
                        m = zz * 4 + corners[1]
                        hops(p, arrived(p, m), m, n + i, (1, 2) if c == 0 else (2,))
                        m = zz * 4 + corners[2]
                        hops(p, arrived(p, m), m, 2 * n + i, (2,) if c == 0 else (0, 2))
                    level(d, s, go)
                if d + 2 == g:
                    def go():
                        m = zz * 4 + corners[3]
                        hops(p, arrived(p, m), m, 3 * n + i, (2,))
                    level(d, s, go)

        launched = {0: 0, 1: 1, 2: 2, 3: 3}
        made = -1
        count = len(PIECES)
        last = STRIDE * (count - 1) + layers + 1
        for t in range(last + 1):
            for p in range(count):
                g = t - STRIDE * p
                if 0 <= g <= layers + 1:
                    a = PIECES[p][0]
                    if g == 0 and a > made:
                        made = a
                        pair_wait(a)
                        if a < 3:
                            build(a)
                        else:
                            build_fc2()
                            finish_fc2()
                        pltpu.make_async_copy(blocks[a], outs[a].at[pl.ds(chip * TILES[a], TILES[a])], own_sem.at[a]).start()
                    event(p, g, start)
        for p in range(count):
            for k in range(4):
                for d, s in levels:
                    if k == 0 and d == 0:
                        continue
                    def go():
                        m = (z + s * d) * 4 + corners[k]
                        q = spot(p, m, 1 - c)
                        pltpu.make_async_copy(q, q, pair_in.at[p, m]).wait()
                    level(d, s, go)
        n = len(levels)
        for p in range(count):
            src = cut(p)
            def sent(sem):
                pltpu.make_async_copy(src, src, sem).wait()
            for i, (d, s) in enumerate(levels):
                def go():
                    sent(hop_send.at[p, i, 0])
                    sent(hop_send.at[p, i, 1])
                    if c == 0:
                        sent(hop_send.at[p, n + i, 1])
                    else:
                        sent(hop_send.at[p, 2 * n + i, 0])
                    for k in range(4):
                        if k or d:
                            sent(pair_out.at[p, k * n + i])
                    for up in (0, 1):
                        if d == 0 or up == int(s < 0):
                            pl.when((z + 1 < layers) if up else (z > 0))(lambda: sent(z_send.at[p, i, up]))
                level(d, s, go)
        for a in range(4):
            remote(ins[a], held[a].at[core], pair_send.at[a], pair_recv.at[a], mate).wait_send()
            pltpu.make_async_copy(blocks[a], outs[a].at[pl.ds(chip * TILES[a], TILES[a])], own_sem.at[a]).wait()
        remote(ahead, ahead_in, ahead_sem.at[0], ahead_sem.at[1], prv).wait_send()

    for c in (0, 1):
        @pl.when(core == c)
        def _():
            run(c)

def gather(n, qkv, out, fc1, fc2):
    layers = n // PLANE
    core = lax.rem(lax.axis_index("dp"), 2)
    qkv = qkv.reshape(108, D)
    out = out.reshape(36, D)
    fc1 = jnp.pad(fc1.reshape(36, FF), ((0, 0), (0, FP - FF)))
    half = jnp.zeros((576,), fc2.dtype)
    fc2 = jnp.where(core == 0, jnp.concatenate([fc2, half]), jnp.concatenate([half, fc2])).reshape(135, D)
    chips = 4 * layers
    slots = 2 * layers - 1
    count = len(PIECES)
    dma = pltpu.SemaphoreType.DMA
    return pl.pallas_call(
        functools.partial(gather_kernel, layers),
        out_shape=[jax.ShapeDtypeStruct((TILES[a] * chips, 8, WIDE[a]), jnp.bfloat16) for a in range(4)],
        in_specs=[pl.BlockSpec(memory_space=pl.ANY)] * 4,
        out_specs=[pl.BlockSpec(memory_space=pl.ANY)] * 4,
        scratch_shapes=[
            pltpu.VMEM((2, 108, D), jnp.bfloat16),
            pltpu.VMEM((2, 36, D), jnp.bfloat16),
            pltpu.VMEM((2, 36, FP), jnp.bfloat16),
            pltpu.VMEM((2, 135, D), jnp.bfloat16),
            pltpu.VMEM((48, D), jnp.bfloat16),
            pltpu.VMEM((48, D), jnp.bfloat16),
            pltpu.VMEM((320, FP), jnp.float32),
            pltpu.VMEM((27, 8, D), jnp.bfloat16),
            pltpu.VMEM((9, 8, D), jnp.bfloat16),
            pltpu.VMEM((9, 8, FP), jnp.bfloat16),
            pltpu.VMEM((34, 8, D), jnp.bfloat16),
            dma((4,)), dma((4,)), dma((2,)), dma((4,)), dma((count, slots, 2)),
            dma((count, 3 * slots, 2)), dma((count, 4 * slots)), dma((count, chips)), dma((count, chips)),
        ],
        compiler_params=pltpu.CompilerParams(collective_id=0, has_side_effects=True, vmem_limit_bytes=40 << 20),
        name="gather_weights",
    )(qkv, out, fc1, fc2)


def frozen(qkv, out, fc1, fc2):
    n = lax.axis_size("dp")
    if n == 4 * PLANE:
        w_qkv, w_out, w_fc1, w_fc2 = gather(n, qkv, out, fc1, fc2)
        return (w_qkv.reshape(3, D, D), w_out.reshape(D, D), w_fc1.reshape(D, FP), w_fc2.reshape(FP, D))
    qkv, out, fc1, fc2 = (lax.all_gather(v, "dp", axis=0, tiled=True) for v in (qkv, out, fc1, fc2))
    return (
        qkv.reshape(3, D, D),
        out.reshape(D, D),
        jnp.pad(fc1.reshape(D, FF), ((0, 0), (0, FP - FF))),
        jnp.pad(fc2.reshape(FF, D), ((0, FP - FF), (0, 0))),
    )


ROWS_HERE = 256
SIDE = 3
SPAN = 2 * SIDE + 1
LANES = 128
COLS = 384
STEP = 256
LOG2E = 1.4426950408889634
HIDE = -1e30


def mm(left, right):
    return jnp.dot(left, right, preferred_element_type=jnp.float32)


def mm_t(left, right):
    return lax.dot_general(left, right, (((1,), (1,)), ((), ())), preferred_element_type=jnp.float32)


def t_mm(left, right):
    return lax.dot_general(left, right, (((0,), (0,)), ((), ())), preferred_element_type=jnp.float32)


def moments(rows):
    center = rows - jnp.mean(rows, axis=-1, keepdims=True)
    return center, lax.rsqrt(jnp.mean(center * center, axis=-1, keepdims=True) + epsilon)


def shares_image(low, high):
    return (low * ROWS_HERE + ROWS_HERE - 1) // IMG >= (high * ROWS_HERE) // IMG


def met(me, n, k):
    other = me + k
    inside = (other >= 0) & (other < n)
    low, high = (me, other) if k > 0 else (other, me)
    return inside & shares_image(low, high)


def reach(me, n):
    first = jnp.int32(SIDE)
    last = jnp.int32(SIDE)
    for k in range(1, SIDE + 1):
        first = first - met(me, n, -k).astype(jnp.int32)
        last = last + met(me, n, k).astype(jnp.int32)
    return first, last


def slots_of(place, me):
    first = (me * ROWS_HERE) // IMG
    edge = first * IMG
    inside = jnp.where(place < edge + IMG, 0, 1)
    return jnp.where((place >= edge) & (place < edge + 2 * IMG), inside, -1)


def chosen_columns(adapters, images, me, block):
    shape = (ROWS_HERE, LANES)
    place = (me + block - SIDE) * ROWS_HERE + lax.broadcasted_iota(jnp.int32, shape, 0)
    column = lax.broadcasted_iota(jnp.int32, shape, 1)
    first = (me * ROWS_HERE) // IMG
    second = jnp.minimum(first + 1, images - 1)
    adapter = jnp.where(slots_of(place, me) == 0, adapters[first], adapters[second])
    return ((column >= adapter * RANK) & (column < adapter * RANK + RANK)).astype(jnp.float32)


def same_image(me, keys_block, query_block):
    shape = (ROWS_HERE, ROWS_HERE)
    key = (me + keys_block - SIDE) * ROWS_HERE + lax.broadcasted_iota(jnp.int32, shape, 0)
    query = (me + query_block - SIDE) * ROWS_HERE + lax.broadcasted_iota(jnp.int32, shape, 1)
    one = slots_of(key, me)
    return jnp.where((one == slots_of(query, me)) & (one >= 0), 0.0, HIDE)


def forward_kernel(n, images, tokens, w_qkv, w_out, w_fc1, w_fc2, gain, bias, fbias, qkv_down, qkv_up, out_down, out_up,
                   ff_down, fc1_up, fc2_down, fc2_up, adapters,
                   output, normed1, low_qkv, qt, kv, lse, mixed_t, mixed, low_out, resid, normed2, low_fc1, pre, low_fc2,
                   xs, v_qkv, v_out, v_fc1, v_fc2, tmp, shade, acc, act, x_send, x_recv, w_sem, fc1_sem, fc2_sem):
    me = lax.axis_index("dp")
    pltpu.make_async_copy(w_qkv, v_qkv, w_sem.at[0]).start()
    pltpu.make_async_copy(w_out, v_out, w_sem.at[1]).start()
    near = [k for k in range(-SIDE, SIDE + 1) if k]
    barrier = pltpu.get_barrier_semaphore()
    total = jnp.int32(0)
    for k in near:
        yes = met(me, n, k)
        total = total + yes.astype(jnp.int32)

        @pl.when(yes)
        def _():
            pl.semaphore_signal(barrier, inc=1, device_id=(me + k,), device_id_type=MESH)

    pl.semaphore_wait(barrier, total)

    def shift(i, k):
        return remote(tokens, xs.at[SIDE - k], x_send.at[i], x_recv.at[SIDE - k], me + k)

    for i, k in enumerate(near):
        @pl.when(met(me, n, k))
        def _():
            shift(i, k).start()
    xs[SIDE] = tokens[...]
    for i, k in enumerate(near):
        @pl.when(met(me, n, k))
        def _():
            pltpu.make_async_copy(xs.at[SIDE + k], xs.at[SIDE + k], x_recv.at[SIDE + k]).wait()
    begin, end = reach(me, n)

    pltpu.make_async_copy(w_qkv, v_qkv, w_sem.at[0]).wait()

    def project(j, carry):
        center, inv = moments(xs[j].astype(jnp.float32))
        n1 = (center * inv * gain[0:1] + bias[0:1]).astype(jnp.bfloat16)
        select = chosen_columns(adapters, images, me, j)
        @pl.when(j == SIDE)
        def _():
            normed1[...] = n1
        for p in range(3):
            low = (select * mm(n1, qkv_down[p])).astype(jnp.bfloat16)
            @pl.when(j == SIDE)
            def _():
                low_qkv[p] = low
            for c in range(0, D, COLS):
                y = mm(n1, v_qkv[p * D:(p + 1) * D, c:c + COLS]) + mm(low, qkv_up[p, :, c:c + COLS])
                if p != 1:
                    y = y + bias[(1, 0, 2)[p]:(1, 0, 2)[p] + 1, c:c + COLS]
                tmp[:, c:c + COLS] = y
            if p == 0:
                qt[j] = tmp[...].T.reshape(HEADS, HEAD_DIM, ROWS_HERE).astype(jnp.bfloat16)
            else:
                for h in range(HEADS):
                    kv[p - 1, j, h] = tmp[:, h * HEAD_DIM:(h + 1) * HEAD_DIM].astype(jnp.bfloat16)
        shade[j] = same_image(me, j, SIDE)
        return carry

    lax.fori_loop(begin, end + 1, project, 0)
    factor = HEAD_DIM ** (-0.5) * LOG2E

    def one_head(h, carry):
        q = qt[SIDE, h]

        def one_block(j, state):
            top, total, o = state
            s = mm(kv[0, j, h], q) * factor + shade[j]
            new = jnp.maximum(top, jnp.max(s, axis=0, keepdims=True))
            fade = jnp.exp2(top - new)
            p = jnp.exp2(s - new)
            total = total * fade + jnp.sum(p, axis=0, keepdims=True)
            o = o * fade + t_mm(kv[1, j, h], p.astype(jnp.bfloat16))
            return new, total, o

        start = (jnp.full((1, ROWS_HERE), HIDE, jnp.float32), jnp.zeros((1, ROWS_HERE), jnp.float32),
                 jnp.zeros((HEAD_DIM, ROWS_HERE), jnp.float32))
        top, total, o = lax.fori_loop(begin, end + 1, one_block, start)
        mixed_t[h] = o / total
        lse[h] = top + jnp.log2(total)
        return carry

    lax.fori_loop(0, HEADS, one_head, 0)
    att = mixed_t[...].reshape(D, ROWS_HERE).T.astype(jnp.bfloat16)
    mixed[...] = att
    select = chosen_columns(adapters, images, me, SIDE)
    pltpu.make_async_copy(w_out, v_out, w_sem.at[1]).wait()
    low = (select * mm(att, out_down[...])).astype(jnp.bfloat16)
    low_out[...] = low
    for c in range(0, D, COLS):
        s = slice(c, c + COLS)
        resid[:, s] = tokens[:, s].astype(jnp.float32) + mm(att, v_out[:, s]) + bias[3:4, s] + mm(low, out_up[:, s])
    center, inv = moments(resid[...])
    n2 = (center * inv * gain[1:2] + bias[4:5]).astype(jnp.bfloat16)
    normed2[...] = n2
    low1 = (select * mm(n2, ff_down[...])).astype(jnp.bfloat16)
    low_fc1[...] = low1

    def fetch1(i):
        slot = lax.rem(i, 2)
        cols = pl.ds(pl.multiple_of(i * STEP, STEP), STEP)
        return pltpu.make_async_copy(w_fc1.at[:, cols], v_fc1.at[slot], fc1_sem.at[slot])

    def fetch(i):
        slot = lax.rem(i, 2)
        rows = pl.ds(pl.multiple_of(i * STEP, STEP), STEP)
        return pltpu.make_async_copy(w_fc2.at[rows, :], v_fc2.at[slot], fc2_sem.at[slot])

    fetch1(0).start()
    fetch(0).start()
    acc[...] = jnp.zeros_like(acc)

    def feed(i, carry):
        @pl.when(i + 1 < FP // STEP)
        def _():
            fetch1(i + 1).start()
        fetch1(i).wait()
        s = pl.ds(pl.multiple_of(i * STEP, STEP), STEP)
        y = mm(n2, v_fc1[lax.rem(i, 2)]) + fbias[:, s] + mm(low1, fc1_up[:, s])
        pre[:, s] = y
        a = (0.5 * y * (1.0 + jnp.tanh(0.7978845608028654 * (y + 0.044715 * y * y * y)))).astype(jnp.bfloat16)
        act[:, s] = a
        acc[...] += mm(a, fc2_down[s, :])
        return carry

    lax.fori_loop(0, FP // STEP, feed, 0)
    low2 = (select * acc[...]).astype(jnp.bfloat16)
    low_fc2[...] = low2
    for c in range(0, D, COLS):
        s = slice(c, c + COLS)
        tmp[:, s] = resid[:, s] + bias[5:6, s] + mm(low2, fc2_up[:, s])

    def close(i, carry):
        @pl.when(i + 1 < FP // STEP)
        def _():
            fetch(i + 1).start()
        fetch(i).wait()
        s = pl.ds(pl.multiple_of(i * STEP, STEP), STEP)
        tmp[...] += mm(act[:, s], v_fc2[lax.rem(i, 2)])
        return carry

    lax.fori_loop(0, FP // STEP, close, 0)
    output[...] = tmp[...].astype(jnp.bfloat16)
    for i, k in enumerate(near):
        @pl.when(met(me, n, k))
        def _():
            shift(i, k).wait_send()


def forward(n, tokens, w_qkv, w_out, w_fc1, w_fc2, gain, bias, fbias, qkv_down, qkv_up, out_down, out_up, ff_down, fc1_up,
            fc2_down, fc2_up, adapters):
    bf, f32 = jnp.bfloat16, jnp.float32
    r = ROWS_HERE
    outs = [
        ((r, D), bf), ((r, D), bf), ((3, r, LANES), bf), ((SPAN, HEADS, HEAD_DIM, r), bf), ((2, SPAN, HEADS, r, HEAD_DIM), bf),
        ((HEADS, 1, r), f32), ((HEADS, HEAD_DIM, r), f32), ((r, D), bf), ((r, LANES), bf), ((r, D), f32), ((r, D), bf),
        ((r, LANES), bf), ((r, FP), f32), ((r, LANES), bf),
    ]
    vmem = pl.BlockSpec(memory_space=pltpu.VMEM)
    away = pl.BlockSpec(memory_space=pl.ANY)
    dma = pltpu.SemaphoreType.DMA
    return pl.pallas_call(
        functools.partial(forward_kernel, n, adapters.shape[0]),
        out_shape=[jax.ShapeDtypeStruct(*o) for o in outs],
        in_specs=[vmem] + [away] * 4 + [vmem] * 11 + [pl.BlockSpec(memory_space=pltpu.SMEM)],
        out_specs=[vmem] * len(outs),
        scratch_shapes=[
            pltpu.VMEM((SPAN, r, D), bf), pltpu.VMEM((3 * D, D), bf), pltpu.VMEM((D, D), bf), pltpu.VMEM((2, D, STEP), bf),
            pltpu.VMEM((2, STEP, D), bf), pltpu.VMEM((r, D), f32), pltpu.VMEM((SPAN, r, r), f32),
            pltpu.VMEM((r, LANES), f32), pltpu.VMEM((r, FP), bf), dma((6,)), dma((SPAN,)), dma((2,)), dma((2,)), dma((2,)),
        ],
        compiler_params=pltpu.CompilerParams(collective_id=1, has_side_effects=True, vmem_limit_bytes=63 << 20),
        name="layer_forward",
    )(tokens, w_qkv, w_out, w_fc1, w_fc2, gain, bias, fbias, qkv_down, qkv_up, out_down, out_up, ff_down, fc1_up, fc2_down,
      fc2_up, adapters)
CHIPS = 16
SLOTS = 2 * RANK
DOWN = (3 * D, D, D, FP)


def norm_back(center, inv, gain_row, grad):
    u = center * inv
    g = grad * gain_row
    return inv * (g - jnp.mean(g, axis=-1, keepdims=True) - u * jnp.mean(g * u, axis=-1, keepdims=True))


def backward_kernel(n, images, cotangent, tokens, w_qkv, w_out, w_fc1, w_fc2, gain, bias, qkv_down, qkv_up, out_down, out_up,
                    ff_down, fc1_up, fc2_down, fc2_up, adapters,
                    normed1, low_qkv, qt, kv, lse, mixed_t, mixed, low_out, resid, normed2, low_fc1, pre, low_fc2,
                    grad_tokens, *rest):
    reduce = n == 4 * PLANE
    count = 8 if reduce else len(DOWN) + 1
    results, rest = rest[:count], rest[count:]
    (v_qkv, v_out, v_fc1, v_fc2, v_kv, own_kv, wide, dres, acc, dat, stat, dq, dk, dv,
     send, recv, w_sem, fc1_sem, fc2_sem, kv_sem, v_pre, pre_sem), rest = rest[:22], rest[22:]
    if reduce:
        (ups, *downs), rest = rest[:5], rest[5:]
        packed, mate_in, going, coming, final, mate_sem, far_send, far_recv, last_sem = (
            rest[0:2], rest[2:6], rest[6:10], rest[10:14], rest[14:22], *rest[22:26])
    else:
        ups, *downs = results
    g_qkv, g_out, g_ff, g_fc2 = downs
    me = lax.axis_index("dp")
    core = lax.rem(me, 2)
    chip = me // 2
    mate = me + 1 - 2 * core
    own = pltpu.make_async_copy(kv.at[:, SIDE], own_kv, w_sem.at[0])
    own.start()
    get_out = pltpu.make_async_copy(w_out, v_out, w_sem.at[1])
    get_out.start()

    def fetch_qkv(t):
        rows = pl.ds(t * COLS, COLS)
        return pltpu.make_async_copy(w_qkv.at[rows, :], v_qkv.at[t % 2], w_sem.at[2 + t % 2])

    fetch_qkv(0).start()

    def fetch1(i):
        slot = lax.rem(i, 2)
        cols = pl.ds(pl.multiple_of(i * STEP, STEP), STEP)
        return pltpu.make_async_copy(w_fc1.at[:, cols], v_fc1.at[slot], fc1_sem.at[slot])

    def fetch2(i):
        slot = lax.rem(i, 2)
        rows = pl.ds(pl.multiple_of(i * STEP, STEP), STEP)
        return pltpu.make_async_copy(w_fc2.at[rows, :], v_fc2.at[slot], fc2_sem.at[slot])

    def fetch_pre(i):
        slot = lax.rem(i, 2)
        cols = pl.ds(pl.multiple_of(i * STEP, STEP), STEP)
        return pltpu.make_async_copy(pre.at[:, cols], v_pre.at[slot], pre_sem.at[slot])

    fetch1(0).start()
    fetch2(0).start()
    fetch_pre(0).start()
    near = [k for k in range(-SIDE, SIDE + 1) if k]
    barrier = pltpu.get_barrier_semaphore()
    total = jnp.int32(0)
    for k in near:
        yes = met(me, n, k)
        total = total + yes.astype(jnp.int32)

        @pl.when(yes)
        def _():
            pl.semaphore_signal(barrier, inc=1, device_id=(me + k,), device_id_type=MESH)

    if reduce:
        for k in range(1, CHIPS):
            pl.semaphore_signal(barrier, inc=1, device_id=(lax.rem(me + 2 * k, n),), device_id_type=MESH)
        pl.semaphore_signal(barrier, inc=1, device_id=(mate,), device_id_type=MESH)
        total = total + CHIPS
    begin, end = reach(me, n)
    bf = jnp.bfloat16
    select = chosen_columns(adapters, images, me, SIDE)

    def narrow(glow):
        if not reduce:
            return glow
        first = (chip * 2 * ROWS_HERE) // IMG
        shape = (LANES, SLOTS)
        lane = lax.broadcasted_iota(jnp.int32, shape, 1)
        late = lane >= RANK
        adapter = jnp.where(late, adapters[jnp.minimum(first + 1, images - 1)], adapters[first])
        pick = lax.broadcasted_iota(jnp.int32, shape, 0) == adapter * RANK + lane - jnp.where(late, RANK, 0)
        place = me * ROWS_HERE + lax.broadcasted_iota(jnp.int32, (ROWS_HERE, SLOTS), 0)
        mine = (place >= (first + 1) * IMG) == (lax.broadcasted_iota(jnp.int32, (ROWS_HERE, SLOTS), 1) >= RANK)
        return jnp.where(mine, mm(glow, pick.astype(bf)), 0.0).astype(bf)

    def put_up(at, value):
        ups[:, :, at] = value.reshape(CHIPS, 8, value.shape[-1])

    e = cotangent[...]
    put_up(slice(0, D), t_mm(low_fc2[...], e))
    glow2 = (select * mm_t(e, fc2_up[...])).astype(bf)
    acc[...] = jnp.zeros_like(acc)
    wide[...] = jnp.zeros_like(wide)
    low1 = low_fc1[...]
    glow2n = narrow(glow2)

    def feed(i, carry):
        @pl.when(i + 1 < FP // STEP)
        def _():
            fetch1(i + 1).start()
            fetch2(i + 1).start()
            fetch_pre(i + 1).start()
        fetch_pre(i).wait()
        fetch1(i).wait()
        fetch2(i).wait()
        slot = lax.rem(i, 2)
        s = pl.ds(pl.multiple_of(i * STEP, STEP), STEP)
        y = v_pre[slot]
        t = jnp.tanh(0.7978845608028654 * (y + 0.044715 * y * y * y))
        half = 0.5 * (1.0 + t)
        a = (y * half).astype(bf)
        slope = half + 0.5 * y * (1.0 - t * t) * (0.7978845608028654 * (1.0 + 3.0 * 0.044715 * y * y))
        g_fc2[:, s] = t_mm(glow2n, a)
        g = mm_t(e, v_fc2[slot]) + mm_t(glow2, fc2_down[s, :])
        gp = (g * slope).astype(bf)
        put_up(pl.ds(pl.multiple_of(D + i * STEP, LANES), STEP), t_mm(low1, gp))
        acc[...] += mm_t(gp, fc1_up[:, s])
        wide[...] += mm_t(gp, v_fc1[slot])
        return carry

    lax.fori_loop(0, FP // STEP, feed, 0)
    glow1 = (select * acc[...]).astype(bf)
    g_ff[...] = t_mm(narrow(glow1), normed2[...])
    center, inv = moments(resid[...])
    dres[...] = e.astype(jnp.float32) + norm_back(center, inv, gain[1:2], wide[...] + mm_t(glow1, ff_down[...]))
    gb = dres[...].astype(bf)
    put_up(slice(D + FP, 2 * D + FP), t_mm(low_out[...], gb))
    glow = (select * mm_t(gb, out_up[...])).astype(bf)
    g_out[...] = t_mm(narrow(glow), mixed[...])
    get_out.wait()
    for c in range(0, D, COLS):
        wide[:, c:c + COLS] = mm_t(gb, v_out[c:c + COLS, :]) + mm_t(glow, out_down[c:c + COLS, :])
    da = wide[...].T.reshape(HEADS, HEAD_DIM, ROWS_HERE).astype(bf)
    dat[SIDE] = da
    delta = jnp.sum(da.astype(jnp.float32) * mixed_t[...], axis=1, keepdims=True)
    stat[SIDE, :, 0:1, :] = lse[...]
    stat[SIDE, :, 1:2, :] = delta

    pl.semaphore_wait(barrier, total)

    half = CHIPS // 2
    early = 2 * D + FP
    if reduce:
        upper = (ups.at[:, :, 0:early], ups.at[:, :, early:early + 3 * D])

        def source(i):
            return upper[i // 2] if i % 2 == 0 else packed[i // 2]

        def to_mate(i):
            return remote(source(i).at[pl.ds(half * (1 - core), half)], mate_in[i], mate_sem.at[0, i], mate_sem.at[1, i], mate)

        def to_chip(i, k):
            return remote(going[i].at[k], coming[i].at[chip], far_send.at[i, k], far_recv.at[i, chip], 2 * (half * core + k) + core)

        def pass_on(i):
            to_mate(i).wait_recv()

            def one(k, carry):
                going[i][k] = (source(i)[half * core + k] + mate_in[i][k]).astype(bf)

                @pl.when(half * core + k != chip)
                def _():
                    to_chip(i, k).start()
                return carry

            lax.fori_loop(0, half, one, 0)

            @pl.when(core == chip // half)
            def _():
                coming[i][chip] = going[i][chip - half * core]

        def gathered(i):
            for k in range(CHIPS):
                @pl.when(chip != k)
                def _():
                    pltpu.make_async_copy(coming[i].at[k], coming[i].at[k], far_recv.at[i, k]).wait()

        def add_up(i):
            gathered(i)
            return lax.fori_loop(1, CHIPS, lambda k, sofar: sofar + coming[i][k].astype(jnp.float32), coming[i][0].astype(jnp.float32))

        def add_down(i):
            gathered(i)
            shape = (LANES, SLOTS)
            lane = lax.broadcasted_iota(jnp.int32, shape, 1)
            late = lane >= RANK
            sofar = None
            for k in range(CHIPS):
                first = (k * 2 * ROWS_HERE) // IMG
                adapter = jnp.where(late, adapters[min(first + 1, images - 1)], adapters[first])
                pick = lax.broadcasted_iota(jnp.int32, shape, 0) == adapter * RANK + lane - jnp.where(late, RANK, 0)
                part = mm(pick.astype(bf), coming[i][k])
                sofar = part if k == 0 else sofar + part
            return sofar.T

        def flat_rows(ref, start, rows):
            for t in range(D // LANES):
                ref[pl.ds(start * (D // LANES) + t, rows.shape[0], stride=D // LANES), :] = rows[:, t * LANES:(t + 1) * LANES]

        def hand_out(which):
            for r in which:
                results[r][...] = final[r][core]
                remote(final[r].at[1 - core], results[r], last_sem.at[0, r], last_sem.at[1, r], mate).start()

        (f_qkv_down, f_qkv_up, f_out_down, f_out_up, f_ff_down, f_fc1_up, f_fc2_down, f_fc2_up) = final

        def finish_early():
            v = add_up(0)
            for q in range(2):
                flat_rows(f_fc2_up.at[q], 0, v[4 * q:4 * q + 4, 0:D])
                f_fc1_up[q] = v[4 * q:4 * q + 4, D:D + FP]
                flat_rows(f_out_up.at[q], 0, v[4 * q:4 * q + 4, D + FP:2 * D + FP])
            v = add_down(1)
            f_fc2_down[0] = v[0:135]
            turned = pltpu.roll(v, 64, axis=1)
            left = lax.broadcasted_iota(jnp.int32, (135, LANES), 1) < 64
            f_fc2_down[1] = jnp.where(left, turned[134:269], turned[135:270])
            for q in range(2):
                f_ff_down[q] = v[384 + 36 * q:420 + 36 * q]
                f_out_down[q] = v[512 + 36 * q:548 + 36 * q]
            hand_out((2, 3, 4, 5, 6, 7))

        def finish_late():
            v = add_up(2)
            flat_rows(f_qkv_up.at[0], 0, v[:, 0:D])
            flat_rows(f_qkv_up.at[0], 8, v[0:4, D:2 * D])
            flat_rows(f_qkv_up.at[1], 0, v[4:8, D:2 * D])
            flat_rows(f_qkv_up.at[1], 4, v[:, 2 * D:3 * D])
            v = add_down(3)
            for q in range(2):
                f_qkv_down[q] = v[108 * q:108 * q + 108]
            hand_out((0, 1))

        for m in range(CHIPS):
            packed[0][m, :, 0:269] = g_fc2[:, 269 * m:269 * m + 269]
            packed[0][m, :, 384:456] = g_ff[:, 72 * m:72 * m + 72]
            packed[0][m, :, 512:584] = g_out[:, 72 * m:72 * m + 72]
        to_mate(0).start()
        to_mate(1).start()

    def shift(i, k, what):
        ref = (dat, stat)[what]
        return remote(ref.at[SIDE], ref.at[SIDE - k], send.at[what, i], recv.at[what, SIDE - k], me + k)

    for i, k in enumerate(near):
        @pl.when(met(me, n, k))
        def _():
            shift(i, k, 0).start()
            shift(i, k, 1).start()

    factor = HEAD_DIM ** (-0.5) * LOG2E
    dq[...] = jnp.zeros_like(dq)

    def block(h, keys, vals, q, d, st, shade, which):
        s = mm(keys, q) * factor + shade
        p = jnp.exp2(s - st[0:1])
        ds = (p * (mm(vals, d) - st[1:2])).astype(bf)
        if which != 2:
            dq[h] += t_mm(keys, ds)
        if which == 0:
            dk[h] = mm_t(q, ds)
            dv[h] = mm_t(d, p.astype(bf))
        if which == 2:
            dk[h] += mm_t(q, ds)
            dv[h] += mm_t(d, p.astype(bf))

    own.wait()
    shade = same_image(me, SIDE, SIDE)

    def own_head(h, carry):
        block(h, own_kv[0, h], own_kv[1, h], qt[SIDE, h], dat[SIDE, h], stat[SIDE, h], shade, 0)
        return carry

    def get_kv(j):
        slot = lax.rem(j, 2)
        return pltpu.make_async_copy(kv.at[:, j], v_kv.at[slot], kv_sem.at[slot])

    get_kv(begin).start()
    lax.fori_loop(0, HEADS, own_head, 0)
    if reduce:
        pass_on(0)
        pass_on(1)

    def pass_one(j, carry):
        @pl.when(j < end)
        def _():
            get_kv(j + 1).start()
        get_kv(j).wait()

        @pl.when(j != SIDE)
        def _():
            shade = same_image(me, j, SIDE)
            slot = lax.rem(j, 2)

            def head(h, carry):
                block(h, v_kv[slot, 0, h], v_kv[slot, 1, h], qt[SIDE, h], dat[SIDE, h], stat[SIDE, h], shade, 1)
                return carry

            lax.fori_loop(0, HEADS, head, 0)
        return carry

    lax.fori_loop(begin, end + 1, pass_one, 0)
    for i, k in enumerate(near):
        @pl.when(met(me, n, k))
        def _():
            for what, ref in enumerate((dat, stat)):
                pltpu.make_async_copy(ref.at[SIDE + k], ref.at[SIDE + k], recv.at[what, SIDE + k]).wait()

    def pass_two(j, carry):
        @pl.when(j != SIDE)
        def _():
            shade = same_image(me, SIDE, j)

            def head(h, carry):
                block(h, own_kv[0, h], own_kv[1, h], qt[j, h], dat[j, h], stat[j, h], shade, 2)
                return carry

            lax.fori_loop(0, HEADS, head, 0)
        return carry

    lax.fori_loop(begin, end + 1, pass_two, 0)
    n1 = normed1[...]
    grads = []
    for p, total_grad in enumerate((dq, dk, dv)):
        value = total_grad[...] * HEAD_DIM ** (-0.5) if p < 2 else total_grad[...]
        g = value.reshape(D, ROWS_HERE).T.astype(bf)
        rows = t_mm(low_qkv[p], g)
        for t in range(LANES // 8):
            at = p * (LANES // 8) + t
            ups[at // 3, :, early + at % 3 * D:early + at % 3 * D + D] = rows[8 * t:8 * t + 8]
        glow = (select * mm_t(g, qkv_up[p])).astype(bf)
        g_qkv[:, p * D:(p + 1) * D] = t_mm(narrow(glow), n1)
        grads.append((g, glow))
    if reduce:
        for m in range(CHIPS):
            packed[1][m, :, 0:216] = g_qkv[:, 216 * m:216 * m + 216]
        to_mate(2).start()
        to_mate(3).start()
    for p, (g, glow) in enumerate(grads):
        for c in range(0, D, COLS):
            s = slice(c, c + COLS)
            t = (p * D + c) // COLS
            if t + 1 < 3 * D // COLS:
                fetch_qkv(t + 1).start()
            fetch_qkv(t).wait()
            y = mm_t(g, v_qkv[t % 2]) + mm_t(glow, qkv_down[p, s, :])
            wide[:, s] = y if p == 0 else wide[:, s] + y
        if reduce and p == 0:
            pass_on(2)
            pass_on(3)
    center, inv = moments(tokens[...].astype(jnp.float32))
    grad_tokens[...] = (dres[...] + norm_back(center, inv, gain[0:1], wide[...])).astype(bf)
    for i, k in enumerate(near):
        @pl.when(met(me, n, k))
        def _():
            shift(i, k, 0).wait_send()
            shift(i, k, 1).wait_send()
    if reduce:
        reducer = core == chip // half

        @pl.when(reducer)
        def _():
            finish_early()
            finish_late()
            for r in range(8):
                remote(final[r].at[1 - core], results[r], last_sem.at[0, r], last_sem.at[1, r], mate).wait_send()

        @pl.when(jnp.logical_not(reducer))
        def _():
            for r in range(8):
                pltpu.make_async_copy(results[r], results[r], last_sem.at[1, r]).wait()

        for i in range(4):
            to_mate(i).wait_send()
            for k in range(half):
                @pl.when(half * core + k != chip)
                def _():
                    to_chip(i, k).wait_send()


def backward(n, cotangent, tokens, w_qkv, w_out, w_fc1, w_fc2, gain, bias, qkv_down, qkv_up, out_down, out_up, ff_down, fc1_up,
             fc2_down, fc2_up, adapters, saved):
    bf, f32 = jnp.bfloat16, jnp.float32
    r = ROWS_HERE
    reduce = n == 4 * PLANE
    deep = SLOTS if reduce else LANES
    partial = [((CHIPS, 8, 5 * D + FP), f32)] + [((deep, w), f32) for w in DOWN]
    shares = [(108, LANES), (108, LANES), (36, LANES), (36, LANES), (36, LANES), (4, FP), (135, LANES), (36, LANES)]
    outs = [((r, D), bf)] + ([(s, f32) for s in shares] if reduce else partial)
    more = []
    if reduce:
        half = CHIPS // 2
        up, down = (2 * D + FP, 3 * D), (640, 256)
        more = [pltpu.VMEM(*v) for v in partial]
        more += [pltpu.VMEM((CHIPS, SLOTS, w), f32) for w in down]
        for rows, kind in ((half, f32), (half, bf), (CHIPS, bf)):
            for w, v in zip(up, down):
                more += [pltpu.VMEM((rows, 8, w), kind), pltpu.VMEM((rows, SLOTS, v), kind)]
        more += [pltpu.VMEM((2,) + s, f32) for s in shares]
        dma = pltpu.SemaphoreType.DMA
        more += [dma((2, 4)), dma((4, half)), dma((4, CHIPS)), dma((2, 8))]
    vmem = pl.BlockSpec(memory_space=pltpu.VMEM)
    away = pl.BlockSpec(memory_space=pl.ANY)
    dma = pltpu.SemaphoreType.DMA
    heads = (HEADS, HEAD_DIM, r)
    return pl.pallas_call(
        functools.partial(backward_kernel, n, adapters.shape[0]),
        out_shape=[jax.ShapeDtypeStruct(*o) for o in outs],
        in_specs=[vmem] * 2 + [away] * 4 + [vmem] * 10 + [pl.BlockSpec(memory_space=pltpu.SMEM)] + [vmem] * 3 + [away] + [vmem] * 7 + [away, vmem],
        out_specs=[vmem] * len(outs),
        scratch_shapes=[
            pltpu.VMEM((2, COLS, D), bf), pltpu.VMEM((D, D), bf), pltpu.VMEM((2, D, STEP), bf), pltpu.VMEM((2, STEP, D), bf),
            pltpu.VMEM((2, 2, HEADS, r, HEAD_DIM), bf), pltpu.VMEM((2, HEADS, r, HEAD_DIM), bf),
            pltpu.VMEM((r, D), f32), pltpu.VMEM((r, D), f32), pltpu.VMEM((r, LANES), f32),
            pltpu.VMEM((SPAN,) + heads, bf), pltpu.VMEM((SPAN, HEADS, 8, r), f32),
            pltpu.VMEM(heads, f32), pltpu.VMEM(heads, f32), pltpu.VMEM(heads, f32),
            dma((2, 6)), dma((2, SPAN)), dma((4,)), dma((2,)), dma((2,)), dma((2,)),
            pltpu.VMEM((2, r, STEP), f32), dma((2,)),
        ] + more,
        compiler_params=pltpu.CompilerParams(collective_id=2, has_side_effects=True, vmem_limit_bytes=63 << 20),
        name="layer_backward",
    )(cotangent, tokens, w_qkv, w_out, w_fc1, w_fc2, gain, bias, qkv_down, qkv_up, out_down, out_up, ff_down, fc1_up, fc2_down,
      fc2_up, adapters, *saved)


def local(
    tokens,
    qkv_weights,
    out_weights,
    fc1_weights,
    fc2_weights,
    ln_gain,
    bias_model,
    first_feedforward_bias,
    qkv_down,
    qkv_up,
    out_down,
    out_up,
    first_feedforward_down,
    fc1_up,
    fc2_down,
    fc2_up,
    adapter_of_image,
    cotangent,
):
    n = lax.axis_size("dp")
    w_qkv, w_out, w_fc1, w_fc2 = frozen(qkv_weights, out_weights, fc1_weights, fc2_weights)
    w_qkv = w_qkv.reshape(3 * D, D)
    tail = FP - FF
    fbias = jnp.pad(first_feedforward_bias, (0, tail))[None]
    fc1_up = jnp.pad(fc1_up, ((0, 0), (0, tail)))
    fc2_down = jnp.pad(fc2_down, ((0, tail), (0, 0)))
    factors = (qkv_down, qkv_up, out_down, out_up, first_feedforward_down, fc1_up, fc2_down, fc2_up, adapter_of_image)
    output, *saved = forward(n, tokens, w_qkv, w_out, w_fc1, w_fc2, ln_gain, bias_model, fbias, *factors)
    grad_tokens, *grads = backward(n, cotangent, tokens, w_qkv, w_out, w_fc1, w_fc2, ln_gain, bias_model, *factors, saved)
    if n == 4 * PLANE:
        grads[5] = grads[5][:, :FF]
        summed = [g.reshape(-1) for g in grads]
        summed[6] = summed[6][: FF * LANES // n]
        return (output, grad_tokens, *summed)
    ups, g_qkv, g_out, g_ff, g_fc2 = grads
    early = 2 * D + FP
    g_up = ups[:, :, early:].reshape(CHIPS, 8, 3, D).transpose(0, 2, 1, 3)
    parts = (
        g_qkv.T,
        g_up,
        g_out.T,
        ups[:, :, D + FP : early],
        g_ff.T,
        ups[:, :, D : D + FF],
        g_fc2.T[:FF],
        ups[:, :, :D],
    )
    summed = [lax.psum_scatter(g.reshape(-1), "dp", scatter_dimension=0, tiled=True) for g in parts]
    return (output, grad_tokens, *summed)


def solution(mesh):
    return jax.shard_map(
        local,
        mesh=mesh,
        in_specs=(P("dp", None),) + (P("dp"),) * 4 + (P(),) * 12 + (P("dp", None),),
        out_specs=(P("dp", None),) * 2 + (P("dp"),) * 8,
        check_vma=False,
    )
```

```python
import functools

import jax
import jax.numpy as jnp
from jax import lax
from jax.experimental import pallas as pl
from jax.experimental.pallas import tpu as pltpu
from jax.sharding import PartitionSpec as P

D = 1152
HEADS = 16
HEAD_DIM = 72
FF = 4304
FP = 4352
IMG = 729
RANK = 16
ADAPTERS = 8
epsilon = 1e-06


MESH = pl.DeviceIdType.MESH
PLANE = 8
ROWS = (216, 72, 72, 272)
WIDE = (D, D, FP, D)
TILES = tuple(rows // 8 for rows in ROWS)
def remote(src, dst, send, recv, to):
    return pltpu.make_async_remote_copy(src_ref=src, dst_ref=dst, send_sem=send, recv_sem=recv, device_id=(to,), device_id_type=MESH)

PIECES = (
    (0, (0, 14), (14, 13)),
    (1, (0, 5), (5, 4)),
    (2, (0, 4), (4, 5)),
    (3, (0, 8), (17, 8)),
    (3, (8, 9), (25, 9)),
)
FLAT = (1, 4)
START = (0, 1, 2, 3, 4)


class Carrier:
    def __init__(self, layers, ins, outs, scratch):
        (self.held, self.ahead, self.ahead_in, self.wide, self.tall, self.blocks, self.pair_send, self.pair_recv, self.ahead_sem,
         self.own_sem, self.z_send, self.hop_send, self.pair_out, self.ici_recv, self.pair_in) = scratch
        self.layers, self.ins, self.outs = layers, ins, outs
        me = self.me = lax.axis_index("dp")
        self.core = lax.rem(me, 2)
        x = lax.rem(me // 2, 2)
        y = lax.rem(me // 4, 2)
        self.z = me // PLANE
        self.chip = me // 2
        self.chips = 4 * layers
        self.mate = me + 1 - 2 * self.core
        self.to_x = me + 2 - 4 * x
        self.to_y = me + 4 - 8 * y
        self.nxt = lax.rem(self.chip + 1, self.chips) * 2 + self.core
        self.prv = lax.rem(self.chip + self.chips - 1, self.chips) * 2 + self.core
        self.levels = [(d, s) for d in range(layers) for s in ((0,) if d == 0 else (-1, 1))]
        plane = lax.rem(self.chip, 4)
        self.corners = (plane, plane + 1 - 2 * x, plane + 2 - 4 * y, 3 - plane)
        self.made = -1
        last = layers + 1
        self.queue = sorted((START[p] + step, p, step) for p in range(len(PIECES)) for step in range(last + 1))

    def greet(self, barrier):
        spot = lax.rem(self.me, PLANE)
        up = lax.rem(self.z + 1, self.layers) * PLANE + spot
        down = lax.rem(self.z + self.layers - 1, self.layers) * PLANE + spot
        peers = (self.mate, self.to_x, self.to_y, self.nxt, self.prv, up, down)
        for peer in peers:
            pl.semaphore_signal(barrier, inc=1, device_id=(peer,), device_id_type=MESH)
        return len(peers)

    def pair(self, a):
        return remote(self.ins[a], self.held[a].at[self.core], self.pair_send.at[a], self.pair_recv.at[a], self.mate)

    def keep(self, a):
        return pltpu.make_async_copy(self.ins[a], self.held[a].at[self.core], self.own_sem.at[a])

    def lay(self, a):
        whole = self.outs[a].at[pl.ds(self.chip * TILES[a], TILES[a])]
        return pltpu.make_async_copy(self.blocks[a], whole, self.own_sem.at[a])

    def look_ahead(self):
        return remote(self.ahead, self.ahead_in, self.ahead_sem.at[0], self.ahead_sem.at[1], self.prv)

    def begin(self):
        for a in range(4):
            self.pair(a).start()
            self.keep(a).start()

    def build(self, a):
        self.keep(a).wait()
        remote(self.ins[a], self.held[a].at[1 - self.core], self.pair_send.at[a], self.pair_recv.at[a], self.mate).wait_recv()
        half, w, held = ROWS[a] // 2, WIDE[a], self.held[a]
        if a < 3:
            rows = self.wide if a == 2 else self.tall
            rows[0:half, 0:w] = held[0].astype(jnp.float32)
            rows[half:2 * half, 0:w] = held[1].astype(jnp.float32)
            self.blocks[a][...] = rows[0:2 * half, 0:w].reshape(half // 4, 8, w).astype(jnp.bfloat16)
        else:
            tall = self.tall
            tall[0:135, :] = held[0].astype(jnp.float32)
            tall[134:135, :] = tall[134:135, :] + held[1, 0:1].astype(jnp.float32)
            tall[135:269, :] = held[1].astype(jnp.float32)[1:135]
            self.ahead[...] = tall[0:48, :].astype(jnp.bfloat16)
            self.look_ahead().start()
            self.look_ahead().wait_recv()
            tall[269:317, :] = jnp.where(self.chip + 1 < self.chips, self.ahead_in[...].astype(jnp.float32), 0.0)
            moved = pltpu.roll(tall[...], 320 - 3 * self.chip, axis=0)[0:272]
            self.blocks[3][...] = moved.reshape(34, 8, D).astype(jnp.bfloat16)
        self.lay(a).start()

    def spot(self, p, m, c):
        a, *cuts = PIECES[p]
        at, rows = cuts[c]
        return self.outs[a].at[pl.ds(m * TILES[a] + at, rows)]

    def level(self, d, s, go):
        if d == 0:
            go()
        else:
            pl.when((self.z - d >= 0) if s < 0 else (self.z + d < self.layers))(go)

    def cut(self, p, c):
        a, *cuts = PIECES[p]
        return self.blocks[a].at[pl.ds(*cuts[c])]

    def hops(self, p, src, m, c, slot, ways):
        for w in ways:
            if w == 2:
                remote(src, self.spot(p, m, c), self.pair_out.at[p, slot], self.pair_in.at[p, m], self.mate).start()
            else:
                to = (self.to_x, self.to_y)[w]
                remote(src, self.spot(p, m, c), self.hop_send.at[p, slot, w], self.ici_recv.at[p, m], to).start()

    def along(self, p, src, m, c, slot, up):
        def go():
            to = self.me + PLANE if up else self.me - PLANE
            remote(src, self.spot(p, m, c), self.z_send.at[p, slot, up], self.ici_recv.at[p, m], to).start()
        pl.when((self.z + 1 < self.layers) if up else (self.z > 0))(go)

    def arrived(self, p, m, c):
        s = self.spot(p, m, c)
        pltpu.make_async_copy(s, s, self.ici_recv.at[p, m]).wait()
        return s

    def flat_event(self, p, step, c):
        count = len(self.levels)
        if step == 0:
            self.hops(p, self.cut(p, c), self.chip, c, 0, (0, 1))
        for k in range(4):
            for i, (d, s) in enumerate(self.levels):
                if (0, 1, 1, 2)[k] + d != step:
                    continue
                def go():
                    m = (self.z + s * d) * 4 + self.corners[k]
                    own = k == 0 and d == 0
                    src = self.cut(p, c) if own else self.arrived(p, m, c)
                    slot = k * count + i
                    ways = () if own else (2,)
                    if d == 0 and k == 1 + c:
                        ways = (1 - c, 2)
                    for up in (0, 1):
                        if d == 0 or up == int(s < 0):
                            self.along(p, src, m, c, slot, up)
                    self.hops(p, src, m, c, slot, ways)
                self.level(d, s, go)

    def event(self, p, step, c):
        if p in FLAT:
            return self.flat_event(p, step, c)
        count = len(self.levels)
        if step == 0:
            self.hops(p, self.cut(p, c), self.chip, c, 0, (0, 1))
            for up in (0, 1):
                self.along(p, self.cut(p, c), self.chip, c, 0, up)
        for i, (d, s) in enumerate(self.levels):
            zz = self.z + s * d
            if d >= 1 and d == step:
                def go():
                    m = zz * 4 + self.corners[0]
                    src = self.arrived(p, m, c)
                    self.along(p, src, m, c, i, int(s < 0))
                    self.hops(p, src, m, c, i, (0, 1, 2))
                self.level(d, s, go)
            if d + 1 == step:
                def go():
                    m = zz * 4 + self.corners[1]
                    self.hops(p, self.arrived(p, m, c), m, c, count + i, (1, 2) if c == 0 else (2,))
                    m = zz * 4 + self.corners[2]
                    self.hops(p, self.arrived(p, m, c), m, c, 2 * count + i, (2,) if c == 0 else (0, 2))
                self.level(d, s, go)
            if d + 2 == step:
                def go():
                    m = zz * 4 + self.corners[3]
                    self.hops(p, self.arrived(p, m, c), m, c, 3 * count + i, (2,))
                self.level(d, s, go)

    def either(self, act):
        for c in (0, 1):
            pl.when(self.core == c)(lambda: act(c))

    def advance(self, steps=1):
        for _ in range(min(steps, len(self.queue))):
            _, p, step = self.queue.pop(0)
            if step == 0 and PIECES[p][0] > self.made:
                self.made = PIECES[p][0]
                self.build(self.made)
            self.either(lambda c: self.event(p, step, c))

    def ready(self, a):
        while any(PIECES[p][0] == a for _, p, _ in self.queue):
            self.advance()

        def act(c):
            for p, piece in enumerate(PIECES):
                if piece[0] != a:
                    continue
                for k in range(4):
                    for d, s in self.levels:
                        if k or d:
                            def go():
                                m = (self.z + s * d) * 4 + self.corners[k]
                                q = self.spot(p, m, 1 - c)
                                pltpu.make_async_copy(q, q, self.pair_in.at[p, m]).wait()
                            self.level(d, s, go)
        self.either(act)
        self.lay(a).wait()

    def end(self):
        count = len(self.levels)

        def act(c):
            for p in range(len(PIECES)):
                src = self.cut(p, c)

                def sent(sem):
                    pltpu.make_async_copy(src, src, sem).wait()
                for i, (d, s) in enumerate(self.levels):
                    def flat():
                        if d == 0:
                            sent(self.hop_send.at[p, 0, 0])
                            sent(self.hop_send.at[p, 0, 1])
                            sent(self.hop_send.at[p, (1 + c) * count, 1 - c])
                        for k in range(4):
                            if k or d:
                                sent(self.pair_out.at[p, k * count + i])
                            for up in (0, 1):
                                if d == 0 or up == int(s < 0):
                                    inside = (self.z + 1 < self.layers) if up else (self.z > 0)
                                    pl.when(inside)(lambda: sent(self.z_send.at[p, k * count + i, up]))

                    if p in FLAT:
                        self.level(d, s, flat)
                        continue

                    def go():
                        sent(self.hop_send.at[p, i, 0])
                        sent(self.hop_send.at[p, i, 1])
                        if c == 0:
                            sent(self.hop_send.at[p, count + i, 1])
                        else:
                            sent(self.hop_send.at[p, 2 * count + i, 0])
                        for k in range(4):
                            if k or d:
                                sent(self.pair_out.at[p, k * count + i])
                        for up in (0, 1):
                            if d == 0 or up == int(s < 0):
                                pl.when((self.z + 1 < self.layers) if up else (self.z > 0))(lambda: sent(self.z_send.at[p, i, up]))
                    self.level(d, s, go)
        self.either(act)
        for a in range(4):
            self.pair(a).wait_send()
        self.look_ahead().wait_send()


ROWS_HERE = 256
SIDE = 3
SPAN = 2 * SIDE + 1
LANES = 128
COLS = 384
STEP = 256
LOG2E = 1.4426950408889634
HIDE = -1e30


def mm(left, right):
    return jnp.dot(left, right, preferred_element_type=jnp.float32)


def mm_t(left, right):
    return lax.dot_general(left, right, (((1,), (1,)), ((), ())), preferred_element_type=jnp.float32)


def t_mm(left, right):
    return lax.dot_general(left, right, (((0,), (0,)), ((), ())), preferred_element_type=jnp.float32)


def moments(rows):
    center = rows - jnp.mean(rows, axis=-1, keepdims=True)
    return center, lax.rsqrt(jnp.mean(center * center, axis=-1, keepdims=True) + epsilon)


def shares_image(low, high):
    return (low * ROWS_HERE + ROWS_HERE - 1) // IMG >= (high * ROWS_HERE) // IMG


def met(me, n, k):
    other = me + k
    inside = (other >= 0) & (other < n)
    low, high = (me, other) if k > 0 else (other, me)
    return inside & shares_image(low, high)


def reach(me, n):
    first = jnp.int32(SIDE)
    last = jnp.int32(SIDE)
    for k in range(1, SIDE + 1):
        first = first - met(me, n, -k).astype(jnp.int32)
        last = last + met(me, n, k).astype(jnp.int32)
    return first, last


def slots_of(place, me):
    first = (me * ROWS_HERE) // IMG
    edge = first * IMG
    inside = jnp.where(place < edge + IMG, 0, 1)
    return jnp.where((place >= edge) & (place < edge + 2 * IMG), inside, -1)


def chosen_columns(adapters, images, me, block):
    shape = (ROWS_HERE, LANES)
    place = (me + block - SIDE) * ROWS_HERE + lax.broadcasted_iota(jnp.int32, shape, 0)
    column = lax.broadcasted_iota(jnp.int32, shape, 1)
    first = (me * ROWS_HERE) // IMG
    second = jnp.minimum(first + 1, images - 1)
    adapter = jnp.where(slots_of(place, me) == 0, adapters[first], adapters[second])
    return ((column >= adapter * RANK) & (column < adapter * RANK + RANK)).astype(jnp.float32)


def same_image(me, keys_block, query_block):
    shape = (ROWS_HERE, ROWS_HERE)
    key = (me + keys_block - SIDE) * ROWS_HERE + lax.broadcasted_iota(jnp.int32, shape, 0)
    query = (me + query_block - SIDE) * ROWS_HERE + lax.broadcasted_iota(jnp.int32, shape, 1)
    one = slots_of(key, me)
    return jnp.where((one == slots_of(query, me)) & (one >= 0), 0.0, HIDE)


class Spread:
    def __init__(self, me, n, kinds, send, recv):
        self.me, self.n, self.kinds, self.send, self.recv = me, n, kinds, send, recv
        self.out = 2 * lax.rem(me, 2) - 1
        self.mate = me - self.out

    def wants(self, device, other):
        low, high = jnp.minimum(device, other), jnp.maximum(device, other)
        return (low >= 0) & (high < self.n) & shares_image(low, high)

    def copy(self, what, i, src, block, to):
        own, held = self.kinds[what]
        at = SIDE + block - to
        return remote(src, held.at[at], self.send.at[what, i], self.recv.at[what, at], to)

    def direct(self):
        for i, step in enumerate((self.out, 3 * self.out, -2 * self.out)):
            yield i, self.me, self.me + step
        yield 3, self.me, self.mate

    def relayed(self):
        for i, step in ((4, self.out), (5, 2 * self.out)):
            yield i, self.me + step, self.mate

    def each(self, which, act):
        for i, block, to in which:
            def go():
                for what, (own, held) in enumerate(self.kinds):
                    src = own if i < 4 else held.at[SIDE + block - self.me]
                    act(what, block, self.copy(what, i, src, block, to))
            pl.when(self.wants(block, to))(go)

    def start(self):
        self.each(self.direct(), lambda what, block, copy: copy.start())

    def landed(self, what, at):
        ref = self.kinds[what][1].at[at]
        pltpu.make_async_copy(ref, ref, self.recv.at[what, at]).wait()

    def onward(self):
        def act(what, block, copy):
            self.landed(what, SIDE + block - self.me)
            copy.start()
        self.each(self.relayed(), act)

    def arrive(self):
        for step, relay in ((1, True), (2, True), (3, False), (-1, False), (-2, False), (-3, False)):
            block = self.me + step * self.out
            wanted = self.wants(self.me, block)
            if relay:
                wanted = wanted & jnp.logical_not(self.wants(block, self.mate))

            def go():
                for what in range(len(self.kinds)):
                    self.landed(what, SIDE + step * self.out)
            pl.when(wanted)(go)

    def end(self):
        self.each(self.direct(), lambda what, block, copy: copy.wait_send())
        self.each(self.relayed(), lambda what, block, copy: copy.wait_send())


def forward_kernel(n, images, tokens, in_qkv, in_out, in_fc1, in_fc2, gain, bias, fbias, qkv_down, qkv_up, out_down, out_up,
                   ff_down, fc1_up, fc2_down, fc2_up, adapters,
                   *rest):
    local_gather = n == 4 * PLANE
    shards = (in_qkv, in_out, in_fc1, in_fc2)
    weights, rest = (rest[:4], rest[4:]) if local_gather else (shards, rest)
    w_qkv, w_out, w_fc1, w_fc2 = weights
    (output, normed1, low_qkv, qt, kv, lse, mixed_t, mixed, low_out, resid, normed2, low_fc1, pre, low_fc2,
     xs, v_qkv, v_out, v_fc1, v_fc2, tmp, shade, acc, act, v_pre, x_send, x_recv, w_sem, fc1_sem, fc2_sem, pre_sem), rest = (
        rest[:30], rest[30:])
    me = lax.axis_index("dp")
    carrier = None
    if local_gather:
        carrier = Carrier(n // PLANE, shards, weights, (rest[:4],) + rest[4:8] + (rest[8:12],) + rest[12:])

    def advance(steps=1):
        if carrier:
            carrier.advance(steps)

    def ready(a):
        if carrier:
            carrier.ready(a)

    get_qkv = pltpu.make_async_copy(w_qkv, v_qkv, w_sem.at[0])
    get_out = pltpu.make_async_copy(w_out, v_out, w_sem.at[1])
    near = [k for k in range(-SIDE, SIDE + 1) if k]
    barrier = pltpu.get_barrier_semaphore()
    total = jnp.int32(0)
    for k in near:
        yes = met(me, n, k)
        total = total + yes.astype(jnp.int32)

        @pl.when(yes)
        def _():
            pl.semaphore_signal(barrier, inc=1, device_id=(me + k,), device_id_type=MESH)

    if carrier:
        total = total + carrier.greet(barrier)
    pl.semaphore_wait(barrier, total)
    if carrier:
        carrier.begin()
        advance(1)

    spread = Spread(me, n, [(tokens, xs)], x_send, x_recv)
    spread.start()
    xs[SIDE] = tokens[...]
    advance(1)
    spread.onward()
    begin, end = reach(me, n)
    for j in range(SPAN):
        shade[j] = same_image(me, j, SIDE)
    ready(0)
    get_qkv.start()
    advance(1)
    get_qkv.wait()
    m_qkv = v_qkv.reshape(3 * D, D)
    spread.arrive()

    def project(j, carry):
        center, inv = moments(xs[j].astype(jnp.float32))
        n1 = (center * inv * gain[0:1] + bias[0:1]).astype(jnp.bfloat16)
        select = chosen_columns(adapters, images, me, j)
        @pl.when(j == SIDE)
        def _():
            normed1[...] = n1
        for p in range(3):
            low = (select * mm(n1, qkv_down[p])).astype(jnp.bfloat16)
            @pl.when(j == SIDE)
            def _():
                low_qkv[p] = low
            for c in range(0, D, COLS):
                y = mm(n1, m_qkv[p * D:(p + 1) * D, c:c + COLS]) + mm(low, qkv_up[p, :, c:c + COLS])
                if p != 1:
                    y = y + bias[(1, 0, 2)[p]:(1, 0, 2)[p] + 1, c:c + COLS]
                tmp[:, c:c + COLS] = y
            if p == 0:
                qt[j] = tmp[...].T.reshape(HEADS, HEAD_DIM, ROWS_HERE).astype(jnp.bfloat16)
            else:
                for h in range(HEADS):
                    kv[p - 1, j, h] = tmp[:, h * HEAD_DIM:(h + 1) * HEAD_DIM].astype(jnp.bfloat16)
        return carry

    project(SIDE, 0)
    advance(1)
    lax.fori_loop(begin, jnp.int32(SIDE), project, 0)
    advance(2)
    lax.fori_loop(jnp.int32(SIDE + 1), end + 1, project, 0)
    advance(2)
    factor = HEAD_DIM ** (-0.5) * LOG2E

    def one_head(h, carry):
        q = qt[SIDE, h]

        def one_block(j, state):
            top, total, o = state
            s = mm(kv[0, j, h], q) * factor + shade[j]
            new = jnp.maximum(top, jnp.max(s, axis=0, keepdims=True))
            fade = jnp.exp2(top - new)
            p = jnp.exp2(s - new)
            total = total * fade + jnp.sum(p, axis=0, keepdims=True)
            o = o * fade + t_mm(kv[1, j, h], p.astype(jnp.bfloat16))
            return new, total, o

        start = (jnp.full((1, ROWS_HERE), HIDE, jnp.float32), jnp.zeros((1, ROWS_HERE), jnp.float32),
                 jnp.zeros((HEAD_DIM, ROWS_HERE), jnp.float32))
        top, total, o = lax.fori_loop(begin, end + 1, one_block, start)
        mixed_t[h] = o / total
        lse[h] = top + jnp.log2(total)
        return carry

    for h in range(0, HEADS, 4):
        lax.fori_loop(h, h + 4, one_head, 0)
        advance(1)
    ready(1)
    get_out.start()
    att = mixed_t[...].reshape(D, ROWS_HERE).T.astype(jnp.bfloat16)
    mixed[...] = att
    select = chosen_columns(adapters, images, me, SIDE)
    get_out.wait()
    m_out = v_out.reshape(D, D)
    low = (select * mm(att, out_down[...])).astype(jnp.bfloat16)
    low_out[...] = low
    for c in range(0, D, COLS):
        s = slice(c, c + COLS)
        resid[:, s] = tokens[:, s].astype(jnp.float32) + mm(att, m_out[:, s]) + bias[3:4, s] + mm(low, out_up[:, s])
    center, inv = moments(resid[...])
    n2 = (center * inv * gain[1:2] + bias[4:5]).astype(jnp.bfloat16)
    normed2[...] = n2
    low1 = (select * mm(n2, ff_down[...])).astype(jnp.bfloat16)
    low_fc1[...] = low1

    def fetch1(i):
        slot = lax.rem(i, 2)
        cols = pl.ds(pl.multiple_of(i * STEP, STEP), STEP)
        return pltpu.make_async_copy(w_fc1.at[:, :, cols], v_fc1.at[slot], fc1_sem.at[slot])

    def fetch(i):
        slot = lax.rem(i, 2)
        rows = pl.ds(i * (STEP // 8), STEP // 8)
        return pltpu.make_async_copy(w_fc2.at[rows], v_fc2.at[slot], fc2_sem.at[slot])

    ready(2)
    fetch1(0).start()
    acc[...] = jnp.zeros_like(acc)

    def keep_pre(i):
        slot = lax.rem(i, 2)
        cols = pl.ds(pl.multiple_of(i * STEP, STEP), STEP)
        return pltpu.make_async_copy(v_pre.at[slot], pre.at[:, cols], pre_sem.at[slot])

    def feed(i, carry):
        @pl.when(i + 1 < FP // STEP)
        def _():
            fetch1(i + 1).start()
        fetch1(i).wait()
        s = pl.ds(pl.multiple_of(i * STEP, STEP), STEP)
        y = mm(n2, v_fc1[lax.rem(i, 2)].reshape(D, STEP)) + fbias[:, s] + mm(low1, fc1_up[:, s])
        slot = lax.rem(i, 2)

        @pl.when(i > 1)
        def _():
            keep_pre(i - 2).wait()
        v_pre[slot] = y
        keep_pre(i).start()
        a = (0.5 * y * (1.0 + jnp.tanh(0.7978845608028654 * (y + 0.044715 * y * y * y)))).astype(jnp.bfloat16)
        act[:, s] = a
        acc[...] += mm(a, fc2_down[s, :])
        return carry

    lax.fori_loop(0, FP // STEP, feed, 0)
    low2 = (select * acc[...]).astype(jnp.bfloat16)
    low_fc2[...] = low2
    for c in range(0, D, COLS):
        s = slice(c, c + COLS)
        tmp[:, s] = resid[:, s] + bias[5:6, s] + mm(low2, fc2_up[:, s])

    ready(3)
    fetch(0).start()

    def close(i, carry):
        @pl.when(i + 1 < FP // STEP)
        def _():
            fetch(i + 1).start()
        fetch(i).wait()
        s = pl.ds(pl.multiple_of(i * STEP, STEP), STEP)
        tmp[...] += mm(act[:, s], v_fc2[lax.rem(i, 2)].reshape(STEP, D))
        return carry

    lax.fori_loop(0, FP // STEP, close, 0)
    output[...] = tmp[...].astype(jnp.bfloat16)
    keep_pre(FP // STEP - 2).wait()
    keep_pre(FP // STEP - 1).wait()
    if carrier:
        carrier.end()
    spread.end()


def forward(n, tokens, qkv, out, fc1, fc2, gain, bias, fbias, qkv_down, qkv_up, out_down, out_up, ff_down, fc1_up,
            fc2_down, fc2_up, adapters):
    bf, f32 = jnp.bfloat16, jnp.float32
    r = ROWS_HERE
    local_gather = n == 4 * PLANE
    full = [((16 * TILES[a], 8, WIDE[a]), bf) for a in range(4)]
    outs = [
        ((r, D), bf), ((r, D), bf), ((3, r, LANES), bf), ((SPAN, HEADS, HEAD_DIM, r), bf), ((2, SPAN, HEADS, r, HEAD_DIM), bf),
        ((HEADS, 1, r), f32), ((HEADS, HEAD_DIM, r), f32), ((r, D), bf), ((r, LANES), bf), ((r, D), f32), ((r, D), bf),
        ((r, LANES), bf), ((r, FP), f32), ((r, LANES), bf),
    ]
    vmem = pl.BlockSpec(memory_space=pltpu.VMEM)
    away = pl.BlockSpec(memory_space=pl.ANY)
    dma = pltpu.SemaphoreType.DMA
    scratch = [
        pltpu.VMEM((SPAN, r, D), bf), pltpu.VMEM(*full[0]), pltpu.VMEM(*full[1]), pltpu.VMEM((2, D // 8, 8, STEP), bf),
        pltpu.VMEM((2, STEP // 8, 8, D), bf), pltpu.VMEM((r, D), f32), pltpu.VMEM((SPAN, r, r), f32), pltpu.VMEM((r, LANES), f32),
        pltpu.VMEM((r, FP), bf), pltpu.VMEM((2, r, STEP), f32), dma((1, 6)), dma((1, SPAN)), dma((2,)), dma((2,)), dma((2,)), dma((2,)),
    ]
    if local_gather:
        layers = n // PLANE
        slots, pieces, chips = 2 * layers - 1, len(PIECES), 4 * layers
        scratch += [pltpu.VMEM((2,) + s, bf) for s in ((108, D), (36, D), (36, FP), (135, D))]
        scratch += [pltpu.VMEM((48, D), bf), pltpu.VMEM((48, D), bf), pltpu.VMEM((72, FP), f32), pltpu.VMEM((320, D), f32)]
        scratch += [pltpu.VMEM((TILES[a], 8, WIDE[a]), bf) for a in range(4)]
        scratch += [dma((4,)), dma((4,)), dma((2,)), dma((4,)), dma((pieces, 4 * slots, 2)), dma((pieces, 3 * slots, 2)),
                    dma((pieces, 4 * slots)), dma((pieces, chips)), dma((pieces, chips))]
    results = pl.pallas_call(
        functools.partial(forward_kernel, n, adapters.shape[0]),
        out_shape=[jax.ShapeDtypeStruct(*o) for o in (full if local_gather else []) + outs],
        in_specs=[vmem] + [away] * 4 + [vmem] * 11 + [pl.BlockSpec(memory_space=pltpu.SMEM)],
        out_specs=([away] * 4 if local_gather else []) + [vmem] * 12 + [away, vmem],
        scratch_shapes=scratch,
        compiler_params=pltpu.CompilerParams(collective_id=1, has_side_effects=True, vmem_limit_bytes=63 << 20),
        name="layer_forward",
    )(tokens, qkv, out, fc1, fc2, gain, bias, fbias, qkv_down, qkv_up, out_down, out_up, ff_down, fc1_up, fc2_down, fc2_up, adapters)
    return results if local_gather else (qkv, out, fc1, fc2, *results)


def shards_of(n, qkv, out, fc1, fc2):
    if n == 4 * PLANE:
        core = lax.rem(lax.axis_index("dp"), 2)
        half = jnp.zeros((D // 2,), fc2.dtype)
        fc2 = jnp.where(core == 0, jnp.concatenate([fc2, half]), jnp.concatenate([half, fc2]))
        return (qkv.reshape(108, D), out.reshape(36, D), jnp.pad(fc1.reshape(36, FF), ((0, 0), (0, FP - FF))), fc2.reshape(135, D))
    qkv, out, fc1, fc2 = (lax.all_gather(v, "dp", axis=0, tiled=True) for v in (qkv, out, fc1, fc2))
    return (
        qkv.reshape(3 * D // 8, 8, D),
        out.reshape(D // 8, 8, D),
        jnp.pad(fc1.reshape(D, FF), ((0, 0), (0, FP - FF))).reshape(D // 8, 8, FP),
        jnp.pad(fc2.reshape(FF, D), ((0, FP - FF), (0, 0))).reshape(FP // 8, 8, D),
    )
CHIPS = 16
SLOTS = 2 * RANK
DOWN = (3 * D, D, D, FP)


def norm_back(center, inv, gain_row, grad):
    u = center * inv
    g = grad * gain_row
    return inv * (g - jnp.mean(g, axis=-1, keepdims=True) - u * jnp.mean(g * u, axis=-1, keepdims=True))


def backward_kernel(n, images, cotangent, tokens, w_qkv, w_out, w_fc1, w_fc2, gain, bias, qkv_down, qkv_up, out_down, out_up,
                    ff_down, fc1_up, fc2_down, fc2_up, adapters,
                    normed1, low_qkv, qt, kv, lse, mixed_t, mixed, low_out, resid, normed2, low_fc1, pre, low_fc2,
                    grad_tokens, *rest):
    reduce = n == 4 * PLANE
    count = 8 if reduce else len(DOWN) + 1
    results, rest = rest[:count], rest[count:]
    (v_qkv, v_out, v_fc1, v_fc2, v_kv, own_kv, wide, dres, acc, dat, stat, dq, dk, dv,
     send, recv, w_sem, fc1_sem, fc2_sem, kv_sem, v_pre, pre_sem), rest = rest[:22], rest[22:]
    if reduce:
        (ups, *downs), rest = rest[:5], rest[5:]
        packed, mate_in, going, coming, final, mate_sem, far_send, far_recv, last_sem = (
            rest[0:2], rest[2:6], rest[6:10], rest[10:14], rest[14:22], *rest[22:26])
    else:
        ups, *downs = results
    g_qkv, g_out, g_ff, g_fc2 = downs
    me = lax.axis_index("dp")
    core = lax.rem(me, 2)
    chip = me // 2
    mate = me + 1 - 2 * core
    own = pltpu.make_async_copy(kv.at[:, SIDE], own_kv, w_sem.at[0])
    own.start()
    get_out = pltpu.make_async_copy(w_out, v_out, w_sem.at[1])
    get_out.start()

    def fetch_qkv(t):
        rows = pl.ds(t * COLS, COLS)
        return pltpu.make_async_copy(w_qkv.at[rows, :], v_qkv.at[t % 2], w_sem.at[2 + t % 2])

    fetch_qkv(0).start()

    def fetch1(i):
        slot = lax.rem(i, 2)
        cols = pl.ds(pl.multiple_of(i * STEP, STEP), STEP)
        return pltpu.make_async_copy(w_fc1.at[:, cols], v_fc1.at[slot], fc1_sem.at[slot])

    def fetch2(i):
        slot = lax.rem(i, 2)
        rows = pl.ds(pl.multiple_of(i * STEP, STEP), STEP)
        return pltpu.make_async_copy(w_fc2.at[rows, :], v_fc2.at[slot], fc2_sem.at[slot])

    def fetch_pre(i):
        slot = lax.rem(i, 2)
        cols = pl.ds(pl.multiple_of(i * STEP, STEP), STEP)
        return pltpu.make_async_copy(pre.at[:, cols], v_pre.at[slot], pre_sem.at[slot])

    fetch1(0).start()
    fetch2(0).start()
    fetch_pre(0).start()
    near = [k for k in range(-SIDE, SIDE + 1) if k]
    barrier = pltpu.get_barrier_semaphore()
    total = jnp.int32(0)
    for k in near:
        yes = met(me, n, k)
        total = total + yes.astype(jnp.int32)

        @pl.when(yes)
        def _():
            pl.semaphore_signal(barrier, inc=1, device_id=(me + k,), device_id_type=MESH)

    if reduce:
        for k in range(1, CHIPS):
            pl.semaphore_signal(barrier, inc=1, device_id=(lax.rem(me + 2 * k, n),), device_id_type=MESH)
        pl.semaphore_signal(barrier, inc=1, device_id=(mate,), device_id_type=MESH)
        total = total + CHIPS
    begin, end = reach(me, n)
    bf = jnp.bfloat16
    select = chosen_columns(adapters, images, me, SIDE)

    def narrow(glow):
        if not reduce:
            return glow
        first = (chip * 2 * ROWS_HERE) // IMG
        shape = (LANES, SLOTS)
        lane = lax.broadcasted_iota(jnp.int32, shape, 1)
        late = lane >= RANK
        adapter = jnp.where(late, adapters[jnp.minimum(first + 1, images - 1)], adapters[first])
        pick = lax.broadcasted_iota(jnp.int32, shape, 0) == adapter * RANK + lane - jnp.where(late, RANK, 0)
        place = me * ROWS_HERE + lax.broadcasted_iota(jnp.int32, (ROWS_HERE, SLOTS), 0)
        mine = (place >= (first + 1) * IMG) == (lax.broadcasted_iota(jnp.int32, (ROWS_HERE, SLOTS), 1) >= RANK)
        return jnp.where(mine, mm(glow, pick.astype(bf)), 0.0).astype(bf)

    def put_up(at, value):
        ups[:, :, at] = value.reshape(CHIPS, 8, value.shape[-1])

    e = cotangent[...]
    put_up(slice(0, D), t_mm(low_fc2[...], e))
    glow2 = (select * mm_t(e, fc2_up[...])).astype(bf)
    acc[...] = jnp.zeros_like(acc)
    wide[...] = jnp.zeros_like(wide)
    low1 = low_fc1[...]
    glow2n = narrow(glow2)

    def feed(i, carry):
        @pl.when(i + 1 < FP // STEP)
        def _():
            fetch1(i + 1).start()
            fetch2(i + 1).start()
            fetch_pre(i + 1).start()
        fetch_pre(i).wait()
        fetch1(i).wait()
        fetch2(i).wait()
        slot = lax.rem(i, 2)
        s = pl.ds(pl.multiple_of(i * STEP, STEP), STEP)
        y = v_pre[slot]
        t = jnp.tanh(0.7978845608028654 * (y + 0.044715 * y * y * y))
        half = 0.5 * (1.0 + t)
        a = (y * half).astype(bf)
        slope = half + 0.5 * y * (1.0 - t * t) * (0.7978845608028654 * (1.0 + 3.0 * 0.044715 * y * y))
        g_fc2[:, s] = t_mm(glow2n, a)
        g = mm_t(e, v_fc2[slot]) + mm_t(glow2, fc2_down[s, :])
        gp = (g * slope).astype(bf)
        put_up(pl.ds(pl.multiple_of(D + i * STEP, LANES), STEP), t_mm(low1, gp))
        acc[...] += mm_t(gp, fc1_up[:, s])
        wide[...] += mm_t(gp, v_fc1[slot])
        return carry

    lax.fori_loop(0, FP // STEP, feed, 0)
    glow1 = (select * acc[...]).astype(bf)
    g_ff[...] = t_mm(narrow(glow1), normed2[...])
    center, inv = moments(resid[...])
    dres[...] = e.astype(jnp.float32) + norm_back(center, inv, gain[1:2], wide[...] + mm_t(glow1, ff_down[...]))
    gb = dres[...].astype(bf)
    put_up(slice(D + FP, 2 * D + FP), t_mm(low_out[...], gb))
    glow = (select * mm_t(gb, out_up[...])).astype(bf)
    g_out[...] = t_mm(narrow(glow), mixed[...])
    get_out.wait()
    for c in range(0, D, COLS):
        wide[:, c:c + COLS] = mm_t(gb, v_out[c:c + COLS, :]) + mm_t(glow, out_down[c:c + COLS, :])
    da = wide[...].T.reshape(HEADS, HEAD_DIM, ROWS_HERE).astype(bf)
    dat[SIDE] = da
    delta = jnp.sum(da.astype(jnp.float32) * mixed_t[...], axis=1, keepdims=True)
    stat[SIDE, :, 0:1, :] = lse[...]
    stat[SIDE, :, 1:2, :] = delta

    pl.semaphore_wait(barrier, total)

    half = CHIPS // 2
    early = 2 * D + FP
    if reduce:
        upper = (ups.at[:, :, 0:early], ups.at[:, :, early:early + 3 * D])

        def source(i):
            return upper[i // 2] if i % 2 == 0 else packed[i // 2]

        def to_mate(i):
            return remote(source(i).at[pl.ds(half * (1 - core), half)], mate_in[i], mate_sem.at[0, i], mate_sem.at[1, i], mate)

        def to_chip(i, k):
            return remote(going[i].at[k], coming[i].at[chip], far_send.at[i, k], far_recv.at[i, chip], 2 * (half * core + k) + core)

        def pass_on(i):
            to_mate(i).wait_recv()

            def one(k, carry):
                going[i][k] = (source(i)[half * core + k] + mate_in[i][k]).astype(bf)

                @pl.when(half * core + k != chip)
                def _():
                    to_chip(i, k).start()
                return carry

            lax.fori_loop(0, half, one, 0)

            @pl.when(core == chip // half)
            def _():
                coming[i][chip] = going[i][chip - half * core]

        def gathered(i):
            for k in range(CHIPS):
                @pl.when(chip != k)
                def _():
                    pltpu.make_async_copy(coming[i].at[k], coming[i].at[k], far_recv.at[i, k]).wait()

        def add_up(i):
            gathered(i)
            return lax.fori_loop(1, CHIPS, lambda k, sofar: sofar + coming[i][k].astype(jnp.float32), coming[i][0].astype(jnp.float32))

        def add_down(i):
            gathered(i)
            shape = (LANES, SLOTS)
            lane = lax.broadcasted_iota(jnp.int32, shape, 1)
            late = lane >= RANK
            sofar = None
            for k in range(CHIPS):
                first = (k * 2 * ROWS_HERE) // IMG
                adapter = jnp.where(late, adapters[min(first + 1, images - 1)], adapters[first])
                pick = lax.broadcasted_iota(jnp.int32, shape, 0) == adapter * RANK + lane - jnp.where(late, RANK, 0)
                part = mm(pick.astype(bf), coming[i][k])
                sofar = part if k == 0 else sofar + part
            return sofar.T

        def flat_rows(ref, start, rows):
            for t in range(D // LANES):
                ref[pl.ds(start * (D // LANES) + t, rows.shape[0], stride=D // LANES), :] = rows[:, t * LANES:(t + 1) * LANES]

        def hand_out(which):
            for r in which:
                results[r][...] = final[r][core]
                remote(final[r].at[1 - core], results[r], last_sem.at[0, r], last_sem.at[1, r], mate).start()

        (f_qkv_down, f_qkv_up, f_out_down, f_out_up, f_ff_down, f_fc1_up, f_fc2_down, f_fc2_up) = final

        def finish_early():
            v = add_up(0)
            for q in range(2):
                flat_rows(f_fc2_up.at[q], 0, v[4 * q:4 * q + 4, 0:D])
                f_fc1_up[q] = v[4 * q:4 * q + 4, D:D + FP]
                flat_rows(f_out_up.at[q], 0, v[4 * q:4 * q + 4, D + FP:2 * D + FP])
            v = add_down(1)
            f_fc2_down[0] = v[0:135]
            turned = pltpu.roll(v, 64, axis=1)
            left = lax.broadcasted_iota(jnp.int32, (135, LANES), 1) < 64
            f_fc2_down[1] = jnp.where(left, turned[134:269], turned[135:270])
            for q in range(2):
                f_ff_down[q] = v[384 + 36 * q:420 + 36 * q]
                f_out_down[q] = v[512 + 36 * q:548 + 36 * q]
            hand_out((2, 3, 4, 5, 6, 7))

        def finish_late():
            v = add_up(2)
            flat_rows(f_qkv_up.at[0], 0, v[:, 0:D])
            flat_rows(f_qkv_up.at[0], 8, v[0:4, D:2 * D])
            flat_rows(f_qkv_up.at[1], 0, v[4:8, D:2 * D])
            flat_rows(f_qkv_up.at[1], 4, v[:, 2 * D:3 * D])
            v = add_down(3)
            for q in range(2):
                f_qkv_down[q] = v[108 * q:108 * q + 108]
            hand_out((0, 1))

        for m in range(CHIPS):
            packed[0][m, :, 0:269] = g_fc2[:, 269 * m:269 * m + 269]
            packed[0][m, :, 384:456] = g_ff[:, 72 * m:72 * m + 72]
            packed[0][m, :, 512:584] = g_out[:, 72 * m:72 * m + 72]
        to_mate(0).start()
        to_mate(1).start()

    def shift(i, k, what):
        ref = (dat, stat)[what]
        return remote(ref.at[SIDE], ref.at[SIDE - k], send.at[what, i], recv.at[what, SIDE - k], me + k)

    for i, k in enumerate(near):
        @pl.when(met(me, n, k))
        def _():
            shift(i, k, 0).start()
            shift(i, k, 1).start()

    factor = HEAD_DIM ** (-0.5) * LOG2E
    dq[...] = jnp.zeros_like(dq)

    def block(h, keys, vals, q, d, st, shade, which):
        s = mm(keys, q) * factor + shade
        p = jnp.exp2(s - st[0:1])
        ds = (p * (mm(vals, d) - st[1:2])).astype(bf)
        if which != 2:
            dq[h] += t_mm(keys, ds)
        if which == 0:
            dk[h] = mm_t(q, ds)
            dv[h] = mm_t(d, p.astype(bf))
        if which == 2:
            dk[h] += mm_t(q, ds)
            dv[h] += mm_t(d, p.astype(bf))

    own.wait()
    shade = same_image(me, SIDE, SIDE)

    def own_head(h, carry):
        block(h, own_kv[0, h], own_kv[1, h], qt[SIDE, h], dat[SIDE, h], stat[SIDE, h], shade, 0)
        return carry

    def get_kv(j):
        slot = lax.rem(j, 2)
        return pltpu.make_async_copy(kv.at[:, j], v_kv.at[slot], kv_sem.at[slot])

    get_kv(begin).start()
    lax.fori_loop(0, HEADS, own_head, 0)
    if reduce:
        pass_on(0)
        pass_on(1)

    def pass_one(j, carry):
        @pl.when(j < end)
        def _():
            get_kv(j + 1).start()
        get_kv(j).wait()

        @pl.when(j != SIDE)
        def _():
            shade = same_image(me, j, SIDE)
            slot = lax.rem(j, 2)

            def head(h, carry):
                block(h, v_kv[slot, 0, h], v_kv[slot, 1, h], qt[SIDE, h], dat[SIDE, h], stat[SIDE, h], shade, 1)
                return carry

            lax.fori_loop(0, HEADS, head, 0)
        return carry

    lax.fori_loop(begin, end + 1, pass_one, 0)
    for i, k in enumerate(near):
        @pl.when(met(me, n, k))
        def _():
            for what, ref in enumerate((dat, stat)):
                pltpu.make_async_copy(ref.at[SIDE + k], ref.at[SIDE + k], recv.at[what, SIDE + k]).wait()

    def pass_two(j, carry):
        @pl.when(j != SIDE)
        def _():
            shade = same_image(me, SIDE, j)

            def head(h, carry):
                block(h, own_kv[0, h], own_kv[1, h], qt[j, h], dat[j, h], stat[j, h], shade, 2)
                return carry

            lax.fori_loop(0, HEADS, head, 0)
        return carry

    lax.fori_loop(begin, end + 1, pass_two, 0)
    n1 = normed1[...]
    grads = []
    for p, total_grad in enumerate((dq, dk, dv)):
        value = total_grad[...] * HEAD_DIM ** (-0.5) if p < 2 else total_grad[...]
        g = value.reshape(D, ROWS_HERE).T.astype(bf)
        rows = t_mm(low_qkv[p], g)
        for t in range(LANES // 8):
            at = p * (LANES // 8) + t
            ups[at // 3, :, early + at % 3 * D:early + at % 3 * D + D] = rows[8 * t:8 * t + 8]
        glow = (select * mm_t(g, qkv_up[p])).astype(bf)
        g_qkv[:, p * D:(p + 1) * D] = t_mm(narrow(glow), n1)
        grads.append((g, glow))
    if reduce:
        for m in range(CHIPS):
            packed[1][m, :, 0:216] = g_qkv[:, 216 * m:216 * m + 216]
        to_mate(2).start()
        to_mate(3).start()
    for p, (g, glow) in enumerate(grads):
        for c in range(0, D, COLS):
            s = slice(c, c + COLS)
            t = (p * D + c) // COLS
            if t + 1 < 3 * D // COLS:
                fetch_qkv(t + 1).start()
            fetch_qkv(t).wait()
            y = mm_t(g, v_qkv[t % 2]) + mm_t(glow, qkv_down[p, s, :])
            wide[:, s] = y if p == 0 else wide[:, s] + y
        if reduce and p == 0:
            pass_on(2)
            pass_on(3)
    center, inv = moments(tokens[...].astype(jnp.float32))
    grad_tokens[...] = (dres[...] + norm_back(center, inv, gain[0:1], wide[...])).astype(bf)
    for i, k in enumerate(near):
        @pl.when(met(me, n, k))
        def _():
            shift(i, k, 0).wait_send()
            shift(i, k, 1).wait_send()
    if reduce:
        reducer = core == chip // half

        @pl.when(reducer)
        def _():
            finish_early()
            finish_late()
            for r in range(8):
                remote(final[r].at[1 - core], results[r], last_sem.at[0, r], last_sem.at[1, r], mate).wait_send()

        @pl.when(jnp.logical_not(reducer))
        def _():
            for r in range(8):
                pltpu.make_async_copy(results[r], results[r], last_sem.at[1, r]).wait()

        for i in range(4):
            to_mate(i).wait_send()
            for k in range(half):
                @pl.when(half * core + k != chip)
                def _():
                    to_chip(i, k).wait_send()


def backward(n, cotangent, tokens, w_qkv, w_out, w_fc1, w_fc2, gain, bias, qkv_down, qkv_up, out_down, out_up, ff_down, fc1_up,
             fc2_down, fc2_up, adapters, saved):
    bf, f32 = jnp.bfloat16, jnp.float32
    r = ROWS_HERE
    reduce = n == 4 * PLANE
    deep = SLOTS if reduce else LANES
    partial = [((CHIPS, 8, 5 * D + FP), f32)] + [((deep, w), f32) for w in DOWN]
    shares = [(108, LANES), (108, LANES), (36, LANES), (36, LANES), (36, LANES), (4, FP), (135, LANES), (36, LANES)]
    outs = [((r, D), bf)] + ([(s, f32) for s in shares] if reduce else partial)
    more = []
    if reduce:
        half = CHIPS // 2
        up, down = (2 * D + FP, 3 * D), (640, 256)
        more = [pltpu.VMEM(*v) for v in partial]
        more += [pltpu.VMEM((CHIPS, SLOTS, w), f32) for w in down]
        for rows, kind in ((half, f32), (half, bf), (CHIPS, bf)):
            for w, v in zip(up, down):
                more += [pltpu.VMEM((rows, 8, w), kind), pltpu.VMEM((rows, SLOTS, v), kind)]
        more += [pltpu.VMEM((2,) + s, f32) for s in shares]
        dma = pltpu.SemaphoreType.DMA
        more += [dma((2, 4)), dma((4, half)), dma((4, CHIPS)), dma((2, 8))]
    vmem = pl.BlockSpec(memory_space=pltpu.VMEM)
    away = pl.BlockSpec(memory_space=pl.ANY)
    dma = pltpu.SemaphoreType.DMA
    heads = (HEADS, HEAD_DIM, r)
    return pl.pallas_call(
        functools.partial(backward_kernel, n, adapters.shape[0]),
        out_shape=[jax.ShapeDtypeStruct(*o) for o in outs],
        in_specs=[vmem] * 2 + [away] * 4 + [vmem] * 10 + [pl.BlockSpec(memory_space=pltpu.SMEM)] + [vmem] * 3 + [away] + [vmem] * 7 + [away, vmem],
        out_specs=[vmem] * len(outs),
        scratch_shapes=[
            pltpu.VMEM((2, COLS, D), bf), pltpu.VMEM((D, D), bf), pltpu.VMEM((2, D, STEP), bf), pltpu.VMEM((2, STEP, D), bf),
            pltpu.VMEM((2, 2, HEADS, r, HEAD_DIM), bf), pltpu.VMEM((2, HEADS, r, HEAD_DIM), bf),
            pltpu.VMEM((r, D), f32), pltpu.VMEM((r, D), f32), pltpu.VMEM((r, LANES), f32),
            pltpu.VMEM((SPAN,) + heads, bf), pltpu.VMEM((SPAN, HEADS, 8, r), f32),
            pltpu.VMEM(heads, f32), pltpu.VMEM(heads, f32), pltpu.VMEM(heads, f32),
            dma((2, 6)), dma((2, SPAN)), dma((4,)), dma((2,)), dma((2,)), dma((2,)),
            pltpu.VMEM((2, r, STEP), f32), dma((2,)),
        ] + more,
        compiler_params=pltpu.CompilerParams(collective_id=2, has_side_effects=True, vmem_limit_bytes=63 << 20),
        name="layer_backward",
    )(cotangent, tokens, w_qkv, w_out, w_fc1, w_fc2, gain, bias, qkv_down, qkv_up, out_down, out_up, ff_down, fc1_up, fc2_down,
      fc2_up, adapters, *saved)


def local(
    tokens,
    qkv_weights,
    out_weights,
    fc1_weights,
    fc2_weights,
    ln_gain,
    bias_model,
    first_feedforward_bias,
    qkv_down,
    qkv_up,
    out_down,
    out_up,
    first_feedforward_down,
    fc1_up,
    fc2_down,
    fc2_up,
    adapter_of_image,
    cotangent,
):
    n = lax.axis_size("dp")
    shards = shards_of(n, qkv_weights, out_weights, fc1_weights, fc2_weights)
    tail = FP - FF
    fbias = jnp.pad(first_feedforward_bias, (0, tail))[None]
    fc1_up = jnp.pad(fc1_up, ((0, 0), (0, tail)))
    fc2_down = jnp.pad(fc2_down, ((0, tail), (0, 0)))
    factors = (qkv_down, qkv_up, out_down, out_up, first_feedforward_down, fc1_up, fc2_down, fc2_up, adapter_of_image)
    results = forward(n, tokens, *shards, ln_gain, bias_model, fbias, *factors)
    weights, output, saved = results[:4], results[4], results[5:]
    weights = [w.reshape(-1, w.shape[-1]) for w in weights]
    grad_tokens, *grads = backward(n, cotangent, tokens, *weights, ln_gain, bias_model, *factors, saved)
    if n == 4 * PLANE:
        grads[5] = grads[5][:, :FF]
        summed = [g.reshape(-1) for g in grads]
        summed[6] = summed[6][: FF * LANES // n]
        return (output, grad_tokens, *summed)
    ups, g_qkv, g_out, g_ff, g_fc2 = grads
    early = 2 * D + FP
    g_up = ups[:, :, early:].reshape(CHIPS, 8, 3, D).transpose(0, 2, 1, 3)
    parts = (
        g_qkv.T,
        g_up,
        g_out.T,
        ups[:, :, D + FP : early],
        g_ff.T,
        ups[:, :, D : D + FF],
        g_fc2.T[:FF],
        ups[:, :, :D],
    )
    summed = [lax.psum_scatter(g.reshape(-1), "dp", scatter_dimension=0, tiled=True) for g in parts]
    return (output, grad_tokens, *summed)


def solution(mesh):
    return jax.shard_map(
        local,
        mesh=mesh,
        in_specs=(P("dp", None),) + (P("dp"),) * 4 + (P(),) * 12 + (P("dp", None),),
        out_specs=(P("dp", None),) * 2 + (P("dp"),) * 8,
        check_vma=False,
    )
```

```python
import functools

import jax
import jax.numpy as jnp
from jax import lax
from jax.experimental import pallas as pl
from jax.experimental.pallas import tpu as pltpu
from jax.sharding import PartitionSpec as P

D = 1152
HEADS = 16
HEAD_DIM = 72
FF = 4304
FP = 4352
IMG = 729
RANK = 16
ADAPTERS = 8
epsilon = 1e-06


MESH = pl.DeviceIdType.MESH
PLANE = 8
ROWS = (216, 72, 72, 272)
WIDE = (D, D, FP, D)
TILES = tuple(rows // 8 for rows in ROWS)
def remote(src, dst, send, recv, to):
    return pltpu.make_async_remote_copy(src_ref=src, dst_ref=dst, send_sem=send, recv_sem=recv, device_id=(to,), device_id_type=MESH)

PIECES = (
    (0, (0, 14), (14, 13)),
    (1, (0, 5), (5, 4)),
    (2, (0, 4), (4, 5)),
    (3, (0, 8), (17, 8)),
    (3, (8, 9), (25, 9)),
)
FLAT = (1, 4)
START = (0, 1, 2, 3, 4)


class Carrier:
    def __init__(self, layers, ins, outs, scratch):
        (self.held, self.ahead, self.ahead_in, self.wide, self.tall, self.blocks, self.pair_send, self.pair_recv, self.ahead_sem,
         self.own_sem, self.z_send, self.hop_send, self.pair_out, self.ici_recv, self.pair_in) = scratch
        self.layers, self.ins, self.outs = layers, ins, outs
        me = self.me = lax.axis_index("dp")
        self.core = lax.rem(me, 2)
        x = lax.rem(me // 2, 2)
        y = lax.rem(me // 4, 2)
        self.z = me // PLANE
        self.chip = me // 2
        self.chips = 4 * layers
        self.mate = me + 1 - 2 * self.core
        self.to_x = me + 2 - 4 * x
        self.to_y = me + 4 - 8 * y
        self.nxt = lax.rem(self.chip + 1, self.chips) * 2 + self.core
        self.prv = lax.rem(self.chip + self.chips - 1, self.chips) * 2 + self.core
        self.levels = [(d, s) for d in range(layers) for s in ((0,) if d == 0 else (-1, 1))]
        plane = lax.rem(self.chip, 4)
        self.corners = (plane, plane + 1 - 2 * x, plane + 2 - 4 * y, 3 - plane)
        self.made = -1
        last = layers + 1
        self.queue = sorted((START[p] + step, p, step) for p in range(len(PIECES)) for step in range(last + 1))

    def greet(self, barrier):
        spot = lax.rem(self.me, PLANE)
        up = lax.rem(self.z + 1, self.layers) * PLANE + spot
        down = lax.rem(self.z + self.layers - 1, self.layers) * PLANE + spot
        peers = (self.mate, self.to_x, self.to_y, self.nxt, self.prv, up, down)
        for peer in peers:
            pl.semaphore_signal(barrier, inc=1, device_id=(peer,), device_id_type=MESH)
        return len(peers)

    def pair(self, a):
        return remote(self.ins[a], self.held[a].at[self.core], self.pair_send.at[a], self.pair_recv.at[a], self.mate)

    def keep(self, a):
        return pltpu.make_async_copy(self.ins[a], self.held[a].at[self.core], self.own_sem.at[a])

    def lay(self, a):
        whole = self.outs[a].at[pl.ds(self.chip * TILES[a], TILES[a])]
        return pltpu.make_async_copy(self.blocks[a], whole, self.own_sem.at[a])

    def look_ahead(self):
        return remote(self.ahead, self.ahead_in, self.ahead_sem.at[0], self.ahead_sem.at[1], self.prv)

    def begin(self):
        for a in range(4):
            self.pair(a).start()
            self.keep(a).start()

    def build(self, a):
        self.keep(a).wait()
        remote(self.ins[a], self.held[a].at[1 - self.core], self.pair_send.at[a], self.pair_recv.at[a], self.mate).wait_recv()
        half, w, held = ROWS[a] // 2, WIDE[a], self.held[a]
        if a < 3:
            rows = self.wide if a == 2 else self.tall
            rows[0:half, 0:w] = held[0].astype(jnp.float32)
            rows[half:2 * half, 0:w] = held[1].astype(jnp.float32)
            self.blocks[a][...] = rows[0:2 * half, 0:w].reshape(half // 4, 8, w).astype(jnp.bfloat16)
        else:
            tall = self.tall
            tall[0:135, :] = held[0].astype(jnp.float32)
            tall[134:135, :] = tall[134:135, :] + held[1, 0:1].astype(jnp.float32)
            tall[135:269, :] = held[1].astype(jnp.float32)[1:135]
            self.ahead[...] = tall[0:48, :].astype(jnp.bfloat16)
            self.look_ahead().start()
            self.look_ahead().wait_recv()
            tall[269:317, :] = jnp.where(self.chip + 1 < self.chips, self.ahead_in[...].astype(jnp.float32), 0.0)
            moved = pltpu.roll(tall[...], 320 - 3 * self.chip, axis=0)[0:272]
            self.blocks[3][...] = moved.reshape(34, 8, D).astype(jnp.bfloat16)
        self.lay(a).start()

    def spot(self, p, m, c):
        a, *cuts = PIECES[p]
        at, rows = cuts[c]
        return self.outs[a].at[pl.ds(m * TILES[a] + at, rows)]

    def level(self, d, s, go):
        if d == 0:
            go()
        else:
            pl.when((self.z - d >= 0) if s < 0 else (self.z + d < self.layers))(go)

    def cut(self, p, c):
        a, *cuts = PIECES[p]
        return self.blocks[a].at[pl.ds(*cuts[c])]

    def hops(self, p, src, m, c, slot, ways):
        for w in ways:
            if w == 2:
                remote(src, self.spot(p, m, c), self.pair_out.at[p, slot], self.pair_in.at[p, m], self.mate).start()
            else:
                to = (self.to_x, self.to_y)[w]
                remote(src, self.spot(p, m, c), self.hop_send.at[p, slot, w], self.ici_recv.at[p, m], to).start()

    def along(self, p, src, m, c, slot, up):
        def go():
            to = self.me + PLANE if up else self.me - PLANE
            remote(src, self.spot(p, m, c), self.z_send.at[p, slot, up], self.ici_recv.at[p, m], to).start()
        pl.when((self.z + 1 < self.layers) if up else (self.z > 0))(go)

    def arrived(self, p, m, c):
        s = self.spot(p, m, c)
        pltpu.make_async_copy(s, s, self.ici_recv.at[p, m]).wait()
        return s

    def flat_event(self, p, step, c):
        count = len(self.levels)
        if step == 0:
            self.hops(p, self.cut(p, c), self.chip, c, 0, (0, 1))
        for k in range(4):
            for i, (d, s) in enumerate(self.levels):
                if (0, 1, 1, 2)[k] + d != step:
                    continue
                def go():
                    m = (self.z + s * d) * 4 + self.corners[k]
                    own = k == 0 and d == 0
                    src = self.cut(p, c) if own else self.arrived(p, m, c)
                    slot = k * count + i
                    ways = () if own else (2,)
                    if d == 0 and k == 1 + c:
                        ways = (1 - c, 2)
                    for up in (0, 1):
                        if d == 0 or up == int(s < 0):
                            self.along(p, src, m, c, slot, up)
                    self.hops(p, src, m, c, slot, ways)
                self.level(d, s, go)

    def event(self, p, step, c):
        if p in FLAT:
            return self.flat_event(p, step, c)
        count = len(self.levels)
        if step == 0:
            self.hops(p, self.cut(p, c), self.chip, c, 0, (0, 1))
            for up in (0, 1):
                self.along(p, self.cut(p, c), self.chip, c, 0, up)
        for i, (d, s) in enumerate(self.levels):
            zz = self.z + s * d
            if d >= 1 and d == step:
                def go():
                    m = zz * 4 + self.corners[0]
                    src = self.arrived(p, m, c)
                    self.along(p, src, m, c, i, int(s < 0))
                    self.hops(p, src, m, c, i, (0, 1, 2))
                self.level(d, s, go)
            if d + 1 == step:
                def go():
                    m = zz * 4 + self.corners[1]
                    self.hops(p, self.arrived(p, m, c), m, c, count + i, (1, 2) if c == 0 else (2,))
                    m = zz * 4 + self.corners[2]
                    self.hops(p, self.arrived(p, m, c), m, c, 2 * count + i, (2,) if c == 0 else (0, 2))
                self.level(d, s, go)
            if d + 2 == step:
                def go():
                    m = zz * 4 + self.corners[3]
                    self.hops(p, self.arrived(p, m, c), m, c, 3 * count + i, (2,))
                self.level(d, s, go)

    def either(self, act):
        for c in (0, 1):
            pl.when(self.core == c)(lambda: act(c))

    def advance(self, steps=1):
        for _ in range(min(steps, len(self.queue))):
            _, p, step = self.queue.pop(0)
            if step == 0 and PIECES[p][0] > self.made:
                self.made = PIECES[p][0]
                self.build(self.made)
            self.either(lambda c: self.event(p, step, c))

    def ready(self, a):
        while any(PIECES[p][0] == a for _, p, _ in self.queue):
            self.advance()

        def act(c):
            for p, piece in enumerate(PIECES):
                if piece[0] != a:
                    continue
                for k in range(4):
                    for d, s in self.levels:
                        if k or d:
                            def go():
                                m = (self.z + s * d) * 4 + self.corners[k]
                                q = self.spot(p, m, 1 - c)
                                pltpu.make_async_copy(q, q, self.pair_in.at[p, m]).wait()
                            self.level(d, s, go)
        self.either(act)
        self.lay(a).wait()

    def end(self):
        count = len(self.levels)

        def act(c):
            for p in range(len(PIECES)):
                src = self.cut(p, c)

                def sent(sem):
                    pltpu.make_async_copy(src, src, sem).wait()
                for i, (d, s) in enumerate(self.levels):
                    def flat():
                        if d == 0:
                            sent(self.hop_send.at[p, 0, 0])
                            sent(self.hop_send.at[p, 0, 1])
                            sent(self.hop_send.at[p, (1 + c) * count, 1 - c])
                        for k in range(4):
                            if k or d:
                                sent(self.pair_out.at[p, k * count + i])
                            for up in (0, 1):
                                if d == 0 or up == int(s < 0):
                                    inside = (self.z + 1 < self.layers) if up else (self.z > 0)
                                    pl.when(inside)(lambda: sent(self.z_send.at[p, k * count + i, up]))

                    if p in FLAT:
                        self.level(d, s, flat)
                        continue

                    def go():
                        sent(self.hop_send.at[p, i, 0])
                        sent(self.hop_send.at[p, i, 1])
                        if c == 0:
                            sent(self.hop_send.at[p, count + i, 1])
                        else:
                            sent(self.hop_send.at[p, 2 * count + i, 0])
                        for k in range(4):
                            if k or d:
                                sent(self.pair_out.at[p, k * count + i])
                        for up in (0, 1):
                            if d == 0 or up == int(s < 0):
                                pl.when((self.z + 1 < self.layers) if up else (self.z > 0))(lambda: sent(self.z_send.at[p, i, up]))
                    self.level(d, s, go)
        self.either(act)
        for a in range(4):
            self.pair(a).wait_send()
        self.look_ahead().wait_send()


ROWS_HERE = 256
SIDE = 3
SPAN = 2 * SIDE + 1
LANES = 128
COLS = 384
STEP = 256
TOGETHER = 8
LOG2E = 1.4426950408889634
HIDE = -1e30


def mm(left, right):
    return jnp.dot(left, right, preferred_element_type=jnp.float32)


def mm_t(left, right):
    return lax.dot_general(left, right, (((1,), (1,)), ((), ())), preferred_element_type=jnp.float32)


def t_mm(left, right):
    return lax.dot_general(left, right, (((0,), (0,)), ((), ())), preferred_element_type=jnp.float32)


def moments(rows):
    center = rows - jnp.mean(rows, axis=-1, keepdims=True)
    return center, lax.rsqrt(jnp.mean(center * center, axis=-1, keepdims=True) + epsilon)


def shares_image(low, high):
    return (low * ROWS_HERE + ROWS_HERE - 1) // IMG >= (high * ROWS_HERE) // IMG


def met(me, n, k):
    other = me + k
    inside = (other >= 0) & (other < n)
    low, high = (me, other) if k > 0 else (other, me)
    return inside & shares_image(low, high)


def reach(me, n):
    first = jnp.int32(SIDE)
    last = jnp.int32(SIDE)
    for k in range(1, SIDE + 1):
        first = first - met(me, n, -k).astype(jnp.int32)
        last = last + met(me, n, k).astype(jnp.int32)
    return first, last


def slots_of(place, me):
    first = (me * ROWS_HERE) // IMG
    edge = first * IMG
    inside = jnp.where(place < edge + IMG, 0, 1)
    return jnp.where((place >= edge) & (place < edge + 2 * IMG), inside, -1)


def chosen_columns(adapters, images, me, block):
    shape = (ROWS_HERE, LANES)
    place = (me + block - SIDE) * ROWS_HERE + lax.broadcasted_iota(jnp.int32, shape, 0)
    column = lax.broadcasted_iota(jnp.int32, shape, 1)
    first = (me * ROWS_HERE) // IMG
    second = jnp.minimum(first + 1, images - 1)
    adapter = jnp.where(slots_of(place, me) == 0, adapters[first], adapters[second])
    return ((column >= adapter * RANK) & (column < adapter * RANK + RANK)).astype(jnp.float32)


def same_image(me, keys_block, query_block):
    shape = (ROWS_HERE, ROWS_HERE)
    key = (me + keys_block - SIDE) * ROWS_HERE + lax.broadcasted_iota(jnp.int32, shape, 0)
    query = (me + query_block - SIDE) * ROWS_HERE + lax.broadcasted_iota(jnp.int32, shape, 1)
    one = slots_of(key, me)
    return jnp.where((one == slots_of(query, me)) & (one >= 0), 0.0, HIDE)


class Spread:
    def __init__(self, me, n, kinds, send, recv):
        self.me, self.n, self.kinds, self.send, self.recv = me, n, kinds, send, recv
        self.out = 2 * lax.rem(me, 2) - 1
        self.mate = me - self.out

    def wants(self, device, other):
        low, high = jnp.minimum(device, other), jnp.maximum(device, other)
        return (low >= 0) & (high < self.n) & shares_image(low, high)

    def copy(self, what, i, src, block, to):
        own, held = self.kinds[what]
        at = SIDE + block - to
        return remote(src, held.at[at], self.send.at[what, i], self.recv.at[what, at], to)

    def direct(self):
        for i, step in enumerate((self.out, 3 * self.out, -2 * self.out)):
            yield i, self.me, self.me + step
        yield 3, self.me, self.mate

    def relayed(self):
        for i, step in ((4, self.out), (5, 2 * self.out)):
            yield i, self.me + step, self.mate

    def each(self, which, act):
        for i, block, to in which:
            def go():
                for what, (own, held) in enumerate(self.kinds):
                    src = own if i < 4 else held.at[SIDE + block - self.me]
                    act(what, block, self.copy(what, i, src, block, to))
            pl.when(self.wants(block, to))(go)

    def start(self):
        self.each(self.direct(), lambda what, block, copy: copy.start())

    def landed(self, what, at):
        ref = self.kinds[what][1].at[at]
        pltpu.make_async_copy(ref, ref, self.recv.at[what, at]).wait()

    def onward(self):
        def act(what, block, copy):
            self.landed(what, SIDE + block - self.me)
            copy.start()
        self.each(self.relayed(), act)

    def arrive(self):
        for step, relay in ((1, True), (2, True), (3, False), (-1, False), (-2, False), (-3, False)):
            block = self.me + step * self.out
            wanted = self.wants(self.me, block)
            if relay:
                wanted = wanted & jnp.logical_not(self.wants(block, self.mate))

            def go():
                for what in range(len(self.kinds)):
                    self.landed(what, SIDE + step * self.out)
            pl.when(wanted)(go)

    def end(self):
        self.each(self.direct(), lambda what, block, copy: copy.wait_send())
        self.each(self.relayed(), lambda what, block, copy: copy.wait_send())


def forward_kernel(n, images, tokens, in_qkv, in_out, in_fc1, in_fc2, gain, bias, fbias, qkv_down, qkv_up, out_down, out_up,
                   ff_down, fc1_up, fc2_down, fc2_up, adapters,
                   *rest):
    local_gather = n == 4 * PLANE
    shards = (in_qkv, in_out, in_fc1, in_fc2)
    weights, rest = (rest[:4], rest[4:]) if local_gather else (shards, rest)
    w_qkv, w_out, w_fc1, w_fc2 = weights
    (output, normed1, low_qkv, qt, kv, lse, mixed_t, mixed, low_out, resid, normed2, low_fc1, pre, low_fc2,
     xs, v_qkv, v_out, v_fc1, v_fc2, tmp, shade, acc, act, v_pre, x_send, x_recv, w_sem, fc1_sem, fc2_sem, pre_sem), rest = (
        rest[:30], rest[30:])
    me = lax.axis_index("dp")
    carrier = None
    if local_gather:
        carrier = Carrier(n // PLANE, shards, weights, (rest[:4],) + rest[4:8] + (rest[8:12],) + rest[12:])

    def advance(steps=1):
        if carrier:
            carrier.advance(steps)

    def ready(a):
        if carrier:
            carrier.ready(a)

    get_qkv = pltpu.make_async_copy(w_qkv, v_qkv, w_sem.at[0])
    get_out = pltpu.make_async_copy(w_out, v_out, w_sem.at[1])
    near = [k for k in range(-SIDE, SIDE + 1) if k]
    barrier = pltpu.get_barrier_semaphore()
    total = jnp.int32(0)
    for k in near:
        yes = met(me, n, k)
        total = total + yes.astype(jnp.int32)

        @pl.when(yes)
        def _():
            pl.semaphore_signal(barrier, inc=1, device_id=(me + k,), device_id_type=MESH)

    if carrier:
        total = total + carrier.greet(barrier)
    pl.semaphore_wait(barrier, total)
    if carrier:
        carrier.begin()
        advance(1)

    spread = Spread(me, n, [(tokens, xs)], x_send, x_recv)
    spread.start()
    xs[SIDE] = tokens[...]
    advance(1)
    spread.onward()
    begin, end = reach(me, n)
    for j in range(SPAN):
        shade[j] = same_image(me, j, SIDE)
    ready(0)
    get_qkv.start()
    advance(1)
    get_qkv.wait()
    m_qkv = v_qkv.reshape(3 * D, D)
    spread.arrive()

    def project(j, carry):
        center, inv = moments(xs[j].astype(jnp.float32))
        n1 = (center * inv * gain[0:1] + bias[0:1]).astype(jnp.bfloat16)
        select = chosen_columns(adapters, images, me, j)
        @pl.when(j == SIDE)
        def _():
            normed1[...] = n1
        for p in range(3):
            low = (select * mm(n1, qkv_down[p])).astype(jnp.bfloat16)
            @pl.when(j == SIDE)
            def _():
                low_qkv[p] = low
            for c in range(0, D, COLS):
                y = mm(n1, m_qkv[p * D:(p + 1) * D, c:c + COLS]) + mm(low, qkv_up[p, :, c:c + COLS])
                if p != 1:
                    y = y + bias[(1, 0, 2)[p]:(1, 0, 2)[p] + 1, c:c + COLS]
                tmp[:, c:c + COLS] = y
            if p == 0:
                qt[j] = tmp[...].T.reshape(HEADS, HEAD_DIM, ROWS_HERE).astype(jnp.bfloat16)
            else:
                for h in range(HEADS):
                    kv[p - 1, j, h] = tmp[:, h * HEAD_DIM:(h + 1) * HEAD_DIM].astype(jnp.bfloat16)
        return carry

    project(SIDE, 0)
    advance(1)
    lax.fori_loop(begin, jnp.int32(SIDE), project, 0)
    advance(2)
    lax.fori_loop(jnp.int32(SIDE + 1), end + 1, project, 0)
    advance(2)
    factor = HEAD_DIM ** (-0.5) * LOG2E

    def some_heads(group, carry):
        heads = [group * 4 + i for i in range(4)]
        queries = [qt[SIDE, h] for h in heads]

        def one_block(j, state):
            after = []
            for h, q, (top, total, o) in zip(heads, queries, state):
                s = mm(kv[0, j, h], q) * factor + shade[j]
                new = jnp.maximum(top, jnp.max(s, axis=0, keepdims=True))
                fade = jnp.exp2(top - new)
                p = jnp.exp2(s - new)
                total = total * fade + jnp.sum(p, axis=0, keepdims=True)
                o = o * fade + t_mm(kv[1, j, h], p.astype(jnp.bfloat16))
                after.append((new, total, o))
            return tuple(after)

        start = (jnp.full((1, ROWS_HERE), HIDE, jnp.float32), jnp.zeros((1, ROWS_HERE), jnp.float32),
                 jnp.zeros((HEAD_DIM, ROWS_HERE), jnp.float32))
        for h, (top, total, o) in zip(heads, lax.fori_loop(begin, end + 1, one_block, (start,) * 4)):
            mixed_t[h] = o / total
            lse[h] = top + jnp.log2(total)
        return carry

    for h in range(0, HEADS, 4):
        lax.fori_loop(h // 4, h // 4 + 1, some_heads, 0)
        advance(1)
    ready(1)
    get_out.start()
    att = mixed_t[...].reshape(D, ROWS_HERE).T.astype(jnp.bfloat16)
    mixed[...] = att
    select = chosen_columns(adapters, images, me, SIDE)
    get_out.wait()
    m_out = v_out.reshape(D, D)
    low = (select * mm(att, out_down[...])).astype(jnp.bfloat16)
    low_out[...] = low
    for c in range(0, D, COLS):
        s = slice(c, c + COLS)
        resid[:, s] = tokens[:, s].astype(jnp.float32) + mm(att, m_out[:, s]) + bias[3:4, s] + mm(low, out_up[:, s])
    center, inv = moments(resid[...])
    n2 = (center * inv * gain[1:2] + bias[4:5]).astype(jnp.bfloat16)
    normed2[...] = n2
    low1 = (select * mm(n2, ff_down[...])).astype(jnp.bfloat16)
    low_fc1[...] = low1

    def fetch1(i):
        slot = lax.rem(i, 2)
        cols = pl.ds(pl.multiple_of(i * STEP, STEP), STEP)
        return pltpu.make_async_copy(w_fc1.at[:, :, cols], v_fc1.at[slot], fc1_sem.at[slot])

    def fetch(i):
        slot = lax.rem(i, 2)
        rows = pl.ds(i * (STEP // 8), STEP // 8)
        return pltpu.make_async_copy(w_fc2.at[rows], v_fc2.at[slot], fc2_sem.at[slot])

    ready(2)
    fetch1(0).start()
    acc[...] = jnp.zeros_like(acc)

    def keep_pre(i):
        slot = lax.rem(i, 2)
        cols = pl.ds(pl.multiple_of(i * STEP, STEP), STEP)
        return pltpu.make_async_copy(v_pre.at[slot], pre.at[:, cols], pre_sem.at[slot])

    def feed(i, carry):
        @pl.when(i + 1 < FP // STEP)
        def _():
            fetch1(i + 1).start()
        fetch1(i).wait()
        s = pl.ds(pl.multiple_of(i * STEP, STEP), STEP)
        y = mm(n2, v_fc1[lax.rem(i, 2)].reshape(D, STEP)) + fbias[:, s] + mm(low1, fc1_up[:, s])
        slot = lax.rem(i, 2)

        @pl.when(i > 1)
        def _():
            keep_pre(i - 2).wait()
        v_pre[slot] = y
        keep_pre(i).start()
        a = (0.5 * y * (1.0 + jnp.tanh(0.7978845608028654 * (y + 0.044715 * y * y * y)))).astype(jnp.bfloat16)
        act[:, s] = a
        acc[...] += mm(a, fc2_down[s, :])
        return carry

    lax.fori_loop(0, FP // STEP, feed, 0)
    low2 = (select * acc[...]).astype(jnp.bfloat16)
    low_fc2[...] = low2
    for c in range(0, D, COLS):
        s = slice(c, c + COLS)
        tmp[:, s] = resid[:, s] + bias[5:6, s] + mm(low2, fc2_up[:, s])

    ready(3)
    fetch(0).start()

    def close(i, carry):
        @pl.when(i + 1 < FP // STEP)
        def _():
            fetch(i + 1).start()
        fetch(i).wait()
        s = pl.ds(pl.multiple_of(i * STEP, STEP), STEP)
        tmp[...] += mm(act[:, s], v_fc2[lax.rem(i, 2)].reshape(STEP, D))
        return carry

    lax.fori_loop(0, FP // STEP, close, 0)
    output[...] = tmp[...].astype(jnp.bfloat16)
    keep_pre(FP // STEP - 2).wait()
    keep_pre(FP // STEP - 1).wait()
    if carrier:
        carrier.end()
    spread.end()


def forward(n, tokens, qkv, out, fc1, fc2, gain, bias, fbias, qkv_down, qkv_up, out_down, out_up, ff_down, fc1_up,
            fc2_down, fc2_up, adapters):
    bf, f32 = jnp.bfloat16, jnp.float32
    r = ROWS_HERE
    local_gather = n == 4 * PLANE
    full = [((16 * TILES[a], 8, WIDE[a]), bf) for a in range(4)]
    outs = [
        ((r, D), bf), ((r, D), bf), ((3, r, LANES), bf), ((SPAN, HEADS, HEAD_DIM, r), bf), ((2, SPAN, HEADS, r, HEAD_DIM), bf),
        ((HEADS, 1, r), f32), ((HEADS, HEAD_DIM, r), f32), ((r, D), bf), ((r, LANES), bf), ((r, D), f32), ((r, D), bf),
        ((r, LANES), bf), ((r, FP), f32), ((r, LANES), bf),
    ]
    vmem = pl.BlockSpec(memory_space=pltpu.VMEM)
    away = pl.BlockSpec(memory_space=pl.ANY)
    dma = pltpu.SemaphoreType.DMA
    scratch = [
        pltpu.VMEM((SPAN, r, D), bf), pltpu.VMEM(*full[0]), pltpu.VMEM(*full[1]), pltpu.VMEM((2, D // 8, 8, STEP), bf),
        pltpu.VMEM((2, STEP // 8, 8, D), bf), pltpu.VMEM((r, D), f32), pltpu.VMEM((SPAN, r, r), f32), pltpu.VMEM((r, LANES), f32),
        pltpu.VMEM((r, FP), bf), pltpu.VMEM((2, r, STEP), f32), dma((1, 6)), dma((1, SPAN)), dma((2,)), dma((2,)), dma((2,)), dma((2,)),
    ]
    if local_gather:
        layers = n // PLANE
        slots, pieces, chips = 2 * layers - 1, len(PIECES), 4 * layers
        scratch += [pltpu.VMEM((2,) + s, bf) for s in ((108, D), (36, D), (36, FP), (135, D))]
        scratch += [pltpu.VMEM((48, D), bf), pltpu.VMEM((48, D), bf), pltpu.VMEM((72, FP), f32), pltpu.VMEM((320, D), f32)]
        scratch += [pltpu.VMEM((TILES[a], 8, WIDE[a]), bf) for a in range(4)]
        scratch += [dma((4,)), dma((4,)), dma((2,)), dma((4,)), dma((pieces, 4 * slots, 2)), dma((pieces, 3 * slots, 2)),
                    dma((pieces, 4 * slots)), dma((pieces, chips)), dma((pieces, chips))]
    results = pl.pallas_call(
        functools.partial(forward_kernel, n, adapters.shape[0]),
        out_shape=[jax.ShapeDtypeStruct(*o) for o in (full if local_gather else []) + outs],
        in_specs=[vmem] + [away] * 4 + [vmem] * 11 + [pl.BlockSpec(memory_space=pltpu.SMEM)],
        out_specs=([away] * 4 if local_gather else []) + [vmem] * 12 + [away, vmem],
        scratch_shapes=scratch,
        compiler_params=pltpu.CompilerParams(collective_id=1, has_side_effects=True, vmem_limit_bytes=63 << 20),
        name="layer_forward",
    )(tokens, qkv, out, fc1, fc2, gain, bias, fbias, qkv_down, qkv_up, out_down, out_up, ff_down, fc1_up, fc2_down, fc2_up, adapters)
    return results if local_gather else (qkv, out, fc1, fc2, *results)


def shards_of(n, qkv, out, fc1, fc2):
    if n == 4 * PLANE:
        core = lax.rem(lax.axis_index("dp"), 2)
        half = jnp.zeros((D // 2,), fc2.dtype)
        fc2 = jnp.where(core == 0, jnp.concatenate([fc2, half]), jnp.concatenate([half, fc2]))
        return (qkv.reshape(108, D), out.reshape(36, D), jnp.pad(fc1.reshape(36, FF), ((0, 0), (0, FP - FF))), fc2.reshape(135, D))
    qkv, out, fc1, fc2 = (lax.all_gather(v, "dp", axis=0, tiled=True) for v in (qkv, out, fc1, fc2))
    return (
        qkv.reshape(3 * D // 8, 8, D),
        out.reshape(D // 8, 8, D),
        jnp.pad(fc1.reshape(D, FF), ((0, 0), (0, FP - FF))).reshape(D // 8, 8, FP),
        jnp.pad(fc2.reshape(FF, D), ((0, FP - FF), (0, 0))).reshape(FP // 8, 8, D),
    )
CUT = 256
CHIPS = 16
SLOTS = 2 * RANK
DOWN = (3 * D, D, D, FP)


def norm_back(center, inv, gain_row, grad):
    u = center * inv
    g = grad * gain_row
    return inv * (g - jnp.mean(g, axis=-1, keepdims=True) - u * jnp.mean(g * u, axis=-1, keepdims=True))


def backward_kernel(n, images, cotangent, tokens, w_qkv, w_out, w_fc1, w_fc2, gain, bias, qkv_down, qkv_up, out_down, out_up,
                    ff_down, fc1_up, fc2_down, fc2_up, adapters,
                    normed1, low_qkv, qt, kv, lse, mixed_t, mixed, low_out, resid, normed2, low_fc1, pre, low_fc2,
                    grad_tokens, *rest):
    reduce = n == 4 * PLANE
    count = 8 if reduce else len(DOWN) + 1
    results, rest = rest[:count], rest[count:]
    (v_qkv, v_out, v_fc1, v_fc2, v_kv, own_kv, wide, dres, acc, dat, stat, dq, dk, dv,
     send, recv, w_sem, fc1_sem, fc2_sem, kv_sem, v_pre, pre_sem), rest = rest[:22], rest[22:]
    if reduce:
        (ups, *downs), rest = rest[:5], rest[5:]
        packed, mate_in, going, coming, final, mate_sem, far_send, far_recv, last_sem = (
            rest[0:2], rest[2:6], rest[6:10], rest[10:14], rest[14:22], *rest[22:26])
    else:
        ups, *downs = results
    g_qkv, g_out, g_ff, g_fc2 = downs
    me = lax.axis_index("dp")
    core = lax.rem(me, 2)
    chip = me // 2
    mate = me + 1 - 2 * core
    own = pltpu.make_async_copy(kv.at[:, SIDE], own_kv, w_sem.at[0])
    own.start()
    get_out = pltpu.make_async_copy(w_out, v_out, w_sem.at[1])
    get_out.start()

    def fetch_qkv(t):
        rows = pl.ds(t * COLS, COLS)
        return pltpu.make_async_copy(w_qkv.at[rows, :], v_qkv.at[t % 2], w_sem.at[2 + t % 2])

    fetch_qkv(0).start()

    def fetch1(i):
        slot = lax.rem(i, 2)
        cols = pl.ds(pl.multiple_of(i * STEP, STEP), STEP)
        return pltpu.make_async_copy(w_fc1.at[:, cols], v_fc1.at[slot], fc1_sem.at[slot])

    def fetch2(i):
        slot = lax.rem(i, 2)
        rows = pl.ds(pl.multiple_of(i * STEP, STEP), STEP)
        return pltpu.make_async_copy(w_fc2.at[rows, :], v_fc2.at[slot], fc2_sem.at[slot])

    def fetch_pre(i):
        slot = lax.rem(i, 2)
        cols = pl.ds(pl.multiple_of(i * STEP, STEP), STEP)
        return pltpu.make_async_copy(pre.at[:, cols], v_pre.at[slot], pre_sem.at[slot])

    fetch1(0).start()
    fetch2(0).start()
    fetch_pre(0).start()
    near = [k for k in range(-SIDE, SIDE + 1) if k]
    barrier = pltpu.get_barrier_semaphore()
    total = jnp.int32(0)
    for k in near:
        yes = met(me, n, k)
        total = total + yes.astype(jnp.int32)

        @pl.when(yes)
        def _():
            pl.semaphore_signal(barrier, inc=1, device_id=(me + k,), device_id_type=MESH)

    if reduce:
        for k in range(1, CHIPS):
            pl.semaphore_signal(barrier, inc=1, device_id=(lax.rem(me + 2 * k, n),), device_id_type=MESH)
        pl.semaphore_signal(barrier, inc=1, device_id=(mate,), device_id_type=MESH)
        total = total + CHIPS
    begin, end = reach(me, n)
    bf = jnp.bfloat16
    select = chosen_columns(adapters, images, me, SIDE)

    def narrow(glow):
        if not reduce:
            return glow
        first = (chip * 2 * ROWS_HERE) // IMG
        shape = (LANES, SLOTS)
        lane = lax.broadcasted_iota(jnp.int32, shape, 1)
        late = lane >= RANK
        adapter = jnp.where(late, adapters[jnp.minimum(first + 1, images - 1)], adapters[first])
        pick = lax.broadcasted_iota(jnp.int32, shape, 0) == adapter * RANK + lane - jnp.where(late, RANK, 0)
        place = me * ROWS_HERE + lax.broadcasted_iota(jnp.int32, (ROWS_HERE, SLOTS), 0)
        mine = (place >= (first + 1) * IMG) == (lax.broadcasted_iota(jnp.int32, (ROWS_HERE, SLOTS), 1) >= RANK)
        return jnp.where(mine, mm(glow, pick.astype(bf)), 0.0).astype(bf)

    def put_up(at, value):
        ups[:, :, at] = value.reshape(CHIPS, 8, value.shape[-1])

    e = cotangent[...]
    put_up(slice(0, D), t_mm(low_fc2[...], e))
    glow2 = (select * mm_t(e, fc2_up[...])).astype(bf)
    acc[...] = jnp.zeros_like(acc)
    wide[...] = jnp.zeros_like(wide)
    low1 = low_fc1[...]
    glow2n = narrow(glow2)

    def feed(i, carry):
        @pl.when(i + 1 < FP // STEP)
        def _():
            fetch1(i + 1).start()
            fetch2(i + 1).start()
            fetch_pre(i + 1).start()
        fetch_pre(i).wait()
        fetch1(i).wait()
        fetch2(i).wait()
        slot = lax.rem(i, 2)
        s = pl.ds(pl.multiple_of(i * STEP, STEP), STEP)
        y = v_pre[slot]
        t = jnp.tanh(0.7978845608028654 * (y + 0.044715 * y * y * y))
        half = 0.5 * (1.0 + t)
        a = (y * half).astype(bf)
        slope = half + 0.5 * y * (1.0 - t * t) * (0.7978845608028654 * (1.0 + 3.0 * 0.044715 * y * y))
        g_fc2[:, s] = t_mm(glow2n, a)
        g = mm_t(e, v_fc2[slot]) + mm_t(glow2, fc2_down[s, :])
        gp = (g * slope).astype(bf)
        put_up(pl.ds(pl.multiple_of(D + i * STEP, LANES), STEP), t_mm(low1, gp))
        acc[...] += mm_t(gp, fc1_up[:, s])
        wide[...] += mm_t(gp, v_fc1[slot])
        return carry

    lax.fori_loop(0, FP // STEP, feed, 0)
    glow1 = (select * acc[...]).astype(bf)
    g_ff[...] = t_mm(narrow(glow1), normed2[...])
    center, inv = moments(resid[...])
    dres[...] = e.astype(jnp.float32) + norm_back(center, inv, gain[1:2], wide[...] + mm_t(glow1, ff_down[...]))
    gb = dres[...].astype(bf)
    put_up(slice(D + FP, 2 * D + FP), t_mm(low_out[...], gb))
    glow = (select * mm_t(gb, out_up[...])).astype(bf)
    g_out[...] = t_mm(narrow(glow), mixed[...])
    get_out.wait()
    for c in range(0, D, COLS):
        wide[:, c:c + COLS] = mm_t(gb, v_out[c:c + COLS, :]) + mm_t(glow, out_down[c:c + COLS, :])
    da = wide[...].T.reshape(HEADS, HEAD_DIM, ROWS_HERE).astype(bf)
    dat[SIDE] = da
    delta = jnp.sum(da.astype(jnp.float32) * mixed_t[...], axis=1, keepdims=True)
    stat[SIDE, 0] = lse[...].reshape(HEADS, ROWS_HERE)
    stat[SIDE, 1] = delta.reshape(HEADS, ROWS_HERE)

    pl.semaphore_wait(barrier, total)

    half = CHIPS // 2
    early = 2 * D + FP
    if reduce:
        upper = (ups.at[:, :, 0:early], ups.at[:, :, early:early + 3 * D])

        def source(i):
            return upper[i // 2] if i % 2 == 0 else packed[i // 2]

        def to_mate(i):
            return remote(source(i).at[pl.ds(half * (1 - core), half)], mate_in[i], mate_sem.at[0, i], mate_sem.at[1, i], mate)

        def to_chip(i, k):
            return remote(going[i].at[k], coming[i].at[chip], far_send.at[i, k], far_recv.at[i, chip], 2 * (half * core + k) + core)

        def pass_on(i):
            to_mate(i).wait_recv()

            def one(k, carry):
                going[i][k] = (source(i)[half * core + k] + mate_in[i][k]).astype(bf)

                @pl.when(half * core + k != chip)
                def _():
                    to_chip(i, k).start()
                return carry

            lax.fori_loop(0, half, one, 0)

            @pl.when(core == chip // half)
            def _():
                coming[i][chip] = going[i][chip - half * core]

        def gathered(i):
            for k in range(CHIPS):
                @pl.when(chip != k)
                def _():
                    pltpu.make_async_copy(coming[i].at[k], coming[i].at[k], far_recv.at[i, k]).wait()

        def add_up(i):
            gathered(i)
            return lax.fori_loop(1, CHIPS, lambda k, sofar: sofar + coming[i][k].astype(jnp.float32), coming[i][0].astype(jnp.float32))

        def add_down(i):
            gathered(i)
            shape = (LANES, SLOTS)
            lane = lax.broadcasted_iota(jnp.int32, shape, 1)
            late = lane >= RANK
            sofar = None
            for k in range(CHIPS):
                first = (k * 2 * ROWS_HERE) // IMG
                adapter = jnp.where(late, adapters[min(first + 1, images - 1)], adapters[first])
                pick = lax.broadcasted_iota(jnp.int32, shape, 0) == adapter * RANK + lane - jnp.where(late, RANK, 0)
                part = mm(pick.astype(bf), coming[i][k])
                sofar = part if k == 0 else sofar + part
            return sofar.T

        def flat_rows(ref, start, rows):
            for t in range(D // LANES):
                ref[pl.ds(start * (D // LANES) + t, rows.shape[0], stride=D // LANES), :] = rows[:, t * LANES:(t + 1) * LANES]

        def hand_out(which):
            for r in which:
                results[r][...] = final[r][core]
                remote(final[r].at[1 - core], results[r], last_sem.at[0, r], last_sem.at[1, r], mate).start()

        (f_qkv_down, f_qkv_up, f_out_down, f_out_up, f_ff_down, f_fc1_up, f_fc2_down, f_fc2_up) = final

        def finish_early():
            v = add_up(0)
            for q in range(2):
                flat_rows(f_fc2_up.at[q], 0, v[4 * q:4 * q + 4, 0:D])
                f_fc1_up[q] = v[4 * q:4 * q + 4, D:D + FP]
                flat_rows(f_out_up.at[q], 0, v[4 * q:4 * q + 4, D + FP:2 * D + FP])
            v = add_down(1)
            f_fc2_down[0] = v[0:135]
            turned = pltpu.roll(v, 64, axis=1)
            left = lax.broadcasted_iota(jnp.int32, (135, LANES), 1) < 64
            f_fc2_down[1] = jnp.where(left, turned[134:269], turned[135:270])
            for q in range(2):
                f_ff_down[q] = v[384 + 36 * q:420 + 36 * q]
                f_out_down[q] = v[512 + 36 * q:548 + 36 * q]
            hand_out((2, 3, 4, 5, 6, 7))

        def finish_late():
            v = add_up(2)
            flat_rows(f_qkv_up.at[0], 0, v[:, 0:D])
            flat_rows(f_qkv_up.at[0], 8, v[0:4, D:2 * D])
            flat_rows(f_qkv_up.at[1], 0, v[4:8, D:2 * D])
            flat_rows(f_qkv_up.at[1], 4, v[:, 2 * D:3 * D])
            v = add_down(3)
            for q in range(2):
                f_qkv_down[q] = v[108 * q:108 * q + 108]
            hand_out((0, 1))

        for m in range(CHIPS):
            packed[0][m, :, 0:269] = g_fc2[:, 269 * m:269 * m + 269]
            packed[0][m, :, 384:456] = g_ff[:, 72 * m:72 * m + 72]
            packed[0][m, :, 512:584] = g_out[:, 72 * m:72 * m + 72]
        to_mate(0).start()
        to_mate(1).start()

    spread = Spread(me, n, [(dat.at[SIDE], dat), (stat.at[SIDE], stat)], send, recv)
    spread.start()
    factor = HEAD_DIM ** (-0.5) * LOG2E

    parts = ROWS_HERE // CUT

    def stats(j, group):
        both = [stat[j, i, pl.ds(pl.multiple_of(group * TOGETHER, TOGETHER), TOGETHER), :] for i in (0, 1)]
        return [(both[0][i:i + 1], both[1][i:i + 1]) for i in range(TOGETHER)]

    def blocks(heads, keys, vals, q, d, st, shade, which):
        add_q, add_k, add_v = [], [], []
        for i in range(len(heads)):
            more_q, more_k, more_v = None, [], []
            for c in range(parts):
                rows = slice(c * CUT, (c + 1) * CUT)
                s = mm(keys[i][rows], q[i]) * factor + shade[rows]
                p = jnp.exp2(s - st[i][0])
                ds = (p * (mm(vals[i][rows], d[i]) - st[i][1])).astype(bf)
                if which != 2:
                    y = t_mm(keys[i][rows], ds)
                    more_q = y if more_q is None else more_q + y
                if which != 1:
                    more_k.append(mm_t(q[i], ds))
                    more_v.append(mm_t(d[i], p.astype(bf)))
            add_q.append(more_q)
            add_k.append(jnp.concatenate(more_k, axis=1) if more_k else None)
            add_v.append(jnp.concatenate(more_v, axis=1) if more_v else None)
        if which == 1:
            add_q = [a + dq[h] for h, a in zip(heads, add_q)]
        if which == 2:
            add_k = [a + dk[h] for h, a in zip(heads, add_k)]
            add_v = [a + dv[h] for h, a in zip(heads, add_v)]
        for i, h in enumerate(heads):
            if which != 2:
                dq[h] = add_q[i]
            if which != 1:
                dk[h] = add_k[i]
                dv[h] = add_v[i]

    own.wait()
    shade = same_image(me, SIDE, SIDE)

    def own_head(group, carry):
        heads = [group * TOGETHER + i for i in range(TOGETHER)]
        blocks(heads, [own_kv[0, h] for h in heads], [own_kv[1, h] for h in heads], [qt[SIDE, h] for h in heads],
               [dat[SIDE, h] for h in heads], stats(SIDE, group), shade, 0)
        return carry

    def get_kv(j):
        slot = lax.rem(j, 2)
        return pltpu.make_async_copy(kv.at[:, j], v_kv.at[slot], kv_sem.at[slot])

    get_kv(begin).start()
    lax.fori_loop(0, HEADS // TOGETHER, own_head, 0)
    spread.onward()

    def pass_one(j, carry):
        @pl.when(j < end)
        def _():
            get_kv(j + 1).start()
        get_kv(j).wait()

        @pl.when(j != SIDE)
        def _():
            shade = same_image(me, j, SIDE)
            slot = lax.rem(j, 2)

            def head(group, carry):
                heads = [group * TOGETHER + i for i in range(TOGETHER)]
                blocks(heads, [v_kv[slot, 0, h] for h in heads], [v_kv[slot, 1, h] for h in heads], [qt[SIDE, h] for h in heads],
                       [dat[SIDE, h] for h in heads], stats(SIDE, group), shade, 1)
                return carry

            lax.fori_loop(0, HEADS // TOGETHER, head, 0)
        return carry

    lax.fori_loop(begin, end + 1, pass_one, 0)
    spread.arrive()
    if reduce:
        pass_on(0)
        pass_on(1)

    def pass_two(j, carry):
        @pl.when(j != SIDE)
        def _():
            shade = same_image(me, SIDE, j)

            def head(group, carry):
                heads = [group * TOGETHER + i for i in range(TOGETHER)]
                blocks(heads, [own_kv[0, h] for h in heads], [own_kv[1, h] for h in heads], [qt[j, h] for h in heads],
                       [dat[j, h] for h in heads], stats(j, group), shade, 2)
                return carry

            lax.fori_loop(0, HEADS // TOGETHER, head, 0)
        return carry

    lax.fori_loop(begin, end + 1, pass_two, 0)
    n1 = normed1[...]
    grads = []
    for p, total_grad in enumerate((dq, dk, dv)):
        value = total_grad[...] * HEAD_DIM ** (-0.5) if p < 2 else total_grad[...]
        g = value.reshape(D, ROWS_HERE).T.astype(bf)
        rows = t_mm(low_qkv[p], g)
        for t in range(LANES // 8):
            at = p * (LANES // 8) + t
            ups[at // 3, :, early + at % 3 * D:early + at % 3 * D + D] = rows[8 * t:8 * t + 8]
        glow = (select * mm_t(g, qkv_up[p])).astype(bf)
        g_qkv[:, p * D:(p + 1) * D] = t_mm(narrow(glow), n1)
        grads.append((g, glow))
    if reduce:
        for m in range(CHIPS):
            packed[1][m, :, 0:216] = g_qkv[:, 216 * m:216 * m + 216]
        to_mate(2).start()
        to_mate(3).start()
    for p, (g, glow) in enumerate(grads):
        for c in range(0, D, COLS):
            s = slice(c, c + COLS)
            t = (p * D + c) // COLS
            if t + 1 < 3 * D // COLS:
                fetch_qkv(t + 1).start()
            fetch_qkv(t).wait()
            y = mm_t(g, v_qkv[t % 2]) + mm_t(glow, qkv_down[p, s, :])
            wide[:, s] = y if p == 0 else wide[:, s] + y
        if reduce and p == 0:
            pass_on(2)
            pass_on(3)
    center, inv = moments(tokens[...].astype(jnp.float32))
    grad_tokens[...] = (dres[...] + norm_back(center, inv, gain[0:1], wide[...])).astype(bf)
    spread.end()
    if reduce:
        reducer = core == chip // half

        @pl.when(reducer)
        def _():
            finish_early()
            finish_late()
            for r in range(8):
                remote(final[r].at[1 - core], results[r], last_sem.at[0, r], last_sem.at[1, r], mate).wait_send()

        @pl.when(jnp.logical_not(reducer))
        def _():
            for r in range(8):
                pltpu.make_async_copy(results[r], results[r], last_sem.at[1, r]).wait()

        for i in range(4):
            to_mate(i).wait_send()
            for k in range(half):
                @pl.when(half * core + k != chip)
                def _():
                    to_chip(i, k).wait_send()


def backward(n, cotangent, tokens, w_qkv, w_out, w_fc1, w_fc2, gain, bias, qkv_down, qkv_up, out_down, out_up, ff_down, fc1_up,
             fc2_down, fc2_up, adapters, saved):
    bf, f32 = jnp.bfloat16, jnp.float32
    r = ROWS_HERE
    reduce = n == 4 * PLANE
    deep = SLOTS if reduce else LANES
    partial = [((CHIPS, 8, 5 * D + FP), f32)] + [((deep, w), f32) for w in DOWN]
    shares = [(108, LANES), (108, LANES), (36, LANES), (36, LANES), (36, LANES), (4, FP), (135, LANES), (36, LANES)]
    outs = [((r, D), bf)] + ([(s, f32) for s in shares] if reduce else partial)
    more = []
    if reduce:
        half = CHIPS // 2
        up, down = (2 * D + FP, 3 * D), (640, 256)
        more = [pltpu.VMEM(*v) for v in partial]
        more += [pltpu.VMEM((CHIPS, SLOTS, w), f32) for w in down]
        for rows, kind in ((half, f32), (half, bf), (CHIPS, bf)):
            for w, v in zip(up, down):
                more += [pltpu.VMEM((rows, 8, w), kind), pltpu.VMEM((rows, SLOTS, v), kind)]
        more += [pltpu.VMEM((2,) + s, f32) for s in shares]
        dma = pltpu.SemaphoreType.DMA
        more += [dma((2, 4)), dma((4, half)), dma((4, CHIPS)), dma((2, 8))]
    vmem = pl.BlockSpec(memory_space=pltpu.VMEM)
    away = pl.BlockSpec(memory_space=pl.ANY)
    dma = pltpu.SemaphoreType.DMA
    heads = (HEADS, HEAD_DIM, r)
    return pl.pallas_call(
        functools.partial(backward_kernel, n, adapters.shape[0]),
        out_shape=[jax.ShapeDtypeStruct(*o) for o in outs],
        in_specs=[vmem] * 2 + [away] * 4 + [vmem] * 10 + [pl.BlockSpec(memory_space=pltpu.SMEM)] + [vmem] * 3 + [away] + [vmem] * 7 + [away, vmem],
        out_specs=[vmem] * len(outs),
        scratch_shapes=[
            pltpu.VMEM((2, COLS, D), bf), pltpu.VMEM((D, D), bf), pltpu.VMEM((2, D, STEP), bf), pltpu.VMEM((2, STEP, D), bf),
            pltpu.VMEM((2, 2, HEADS, r, HEAD_DIM), bf), pltpu.VMEM((2, HEADS, r, HEAD_DIM), bf),
            pltpu.VMEM((r, D), f32), pltpu.VMEM((r, D), f32), pltpu.VMEM((r, LANES), f32),
            pltpu.VMEM((SPAN,) + heads, bf), pltpu.VMEM((SPAN, 2, HEADS, r), f32),
            pltpu.VMEM(heads, f32), pltpu.VMEM(heads, f32), pltpu.VMEM(heads, f32),
            dma((2, 6)), dma((2, SPAN)), dma((4,)), dma((2,)), dma((2,)), dma((2,)),
            pltpu.VMEM((2, r, STEP), f32), dma((2,)),
        ] + more,
        compiler_params=pltpu.CompilerParams(collective_id=2, has_side_effects=True, vmem_limit_bytes=63 << 20),
        name="layer_backward",
    )(cotangent, tokens, w_qkv, w_out, w_fc1, w_fc2, gain, bias, qkv_down, qkv_up, out_down, out_up, ff_down, fc1_up, fc2_down,
      fc2_up, adapters, *saved)


def local(
    tokens,
    qkv_weights,
    out_weights,
    fc1_weights,
    fc2_weights,
    ln_gain,
    bias_model,
    first_feedforward_bias,
    qkv_down,
    qkv_up,
    out_down,
    out_up,
    first_feedforward_down,
    fc1_up,
    fc2_down,
    fc2_up,
    adapter_of_image,
    cotangent,
):
    n = lax.axis_size("dp")
    shards = shards_of(n, qkv_weights, out_weights, fc1_weights, fc2_weights)
    tail = FP - FF
    fbias = jnp.pad(first_feedforward_bias, (0, tail))[None]
    fc1_up = jnp.pad(fc1_up, ((0, 0), (0, tail)))
    fc2_down = jnp.pad(fc2_down, ((0, tail), (0, 0)))
    factors = (qkv_down, qkv_up, out_down, out_up, first_feedforward_down, fc1_up, fc2_down, fc2_up, adapter_of_image)
    results = forward(n, tokens, *shards, ln_gain, bias_model, fbias, *factors)
    weights, output, saved = results[:4], results[4], results[5:]
    weights = [w.reshape(-1, w.shape[-1]) for w in weights]
    grad_tokens, *grads = backward(n, cotangent, tokens, *weights, ln_gain, bias_model, *factors, saved)
    if n == 4 * PLANE:
        grads[5] = grads[5][:, :FF]
        summed = [g.reshape(-1) for g in grads]
        summed[6] = summed[6][: FF * LANES // n]
        return (output, grad_tokens, *summed)
    ups, g_qkv, g_out, g_ff, g_fc2 = grads
    early = 2 * D + FP
    g_up = ups[:, :, early:].reshape(CHIPS, 8, 3, D).transpose(0, 2, 1, 3)
    parts = (
        g_qkv.T,
        g_up,
        g_out.T,
        ups[:, :, D + FP : early],
        g_ff.T,
        ups[:, :, D : D + FF],
        g_fc2.T[:FF],
        ups[:, :, :D],
    )
    summed = [lax.psum_scatter(g.reshape(-1), "dp", scatter_dimension=0, tiled=True) for g in parts]
    return (output, grad_tokens, *summed)


def solution(mesh):
    return jax.shard_map(
        local,
        mesh=mesh,
        in_specs=(P("dp", None),) + (P("dp"),) * 4 + (P(),) * 12 + (P("dp", None),),
        out_specs=(P("dp", None),) * 2 + (P("dp"),) * 8,
        check_vma=False,
    )
```

```python
import functools

import jax
import jax.numpy as jnp
from jax import lax
from jax.experimental import pallas as pl
from jax.experimental.pallas import tpu as pltpu
from jax.sharding import PartitionSpec as P

D = 1152
HEADS = 16
HEAD_DIM = 72
FF = 4304
FP = 4352
IMG = 729
RANK = 16
ADAPTERS = 8
epsilon = 1e-06


MESH = pl.DeviceIdType.MESH
PLANE = 8
ROWS = (216, 72, 72, 272)
WIDE = (D, D, FP, D)
TILES = tuple(rows // 8 for rows in ROWS)
def remote(src, dst, send, recv, to):
    return pltpu.make_async_remote_copy(src_ref=src, dst_ref=dst, send_sem=send, recv_sem=recv, device_id=(to,), device_id_type=MESH)

PIECES = (
    (0, (0, 14), (14, 13)),
    (1, (0, 5), (5, 4)),
    (2, (0, 4), (4, 5)),
    (3, (0, 8), (17, 8)),
    (3, (8, 9), (25, 9)),
)
FLAT = (1, 4)
START = (0, 4, 5, 6, 7)


class Carrier:
    def __init__(self, layers, ins, outs, scratch):
        (self.held, self.ahead, self.ahead_in, self.wide, self.tall, self.blocks, self.pair_send, self.pair_recv, self.ahead_sem,
         self.own_sem, self.z_send, self.hop_send, self.pair_out, self.ici_recv, self.pair_in) = scratch
        self.layers, self.ins, self.outs = layers, ins, outs
        me = self.me = lax.axis_index("dp")
        self.core = lax.rem(me, 2)
        x = lax.rem(me // 2, 2)
        y = lax.rem(me // 4, 2)
        self.z = me // PLANE
        self.chip = me // 2
        self.chips = 4 * layers
        self.mate = me + 1 - 2 * self.core
        self.to_x = me + 2 - 4 * x
        self.to_y = me + 4 - 8 * y
        self.nxt = lax.rem(self.chip + 1, self.chips) * 2 + self.core
        self.prv = lax.rem(self.chip + self.chips - 1, self.chips) * 2 + self.core
        self.levels = [(d, s) for d in range(layers) for s in ((0,) if d == 0 else (-1, 1))]
        plane = lax.rem(self.chip, 4)
        self.corners = (plane, plane + 1 - 2 * x, plane + 2 - 4 * y, 3 - plane)
        self.made = -1
        last = layers + 1
        self.queue = sorted((START[p] + step, p, step) for p in range(len(PIECES)) for step in range(last + 1))

    def greet(self, barrier):
        spot = lax.rem(self.me, PLANE)
        up = lax.rem(self.z + 1, self.layers) * PLANE + spot
        down = lax.rem(self.z + self.layers - 1, self.layers) * PLANE + spot
        peers = (self.mate, self.to_x, self.to_y, self.nxt, self.prv, up, down)
        for peer in peers:
            pl.semaphore_signal(barrier, inc=1, device_id=(peer,), device_id_type=MESH)
        return len(peers)

    def pair(self, a):
        return remote(self.ins[a], self.held[a].at[self.core], self.pair_send.at[a], self.pair_recv.at[a], self.mate)

    def keep(self, a):
        return pltpu.make_async_copy(self.ins[a], self.held[a].at[self.core], self.own_sem.at[a])

    def lay(self, a):
        whole = self.outs[a].at[pl.ds(self.chip * TILES[a], TILES[a])]
        return pltpu.make_async_copy(self.blocks[a], whole, self.own_sem.at[a])

    def look_ahead(self):
        return remote(self.ahead, self.ahead_in, self.ahead_sem.at[0], self.ahead_sem.at[1], self.prv)

    def begin(self):
        for a in range(4):
            self.pair(a).start()
            self.keep(a).start()

    def build(self, a):
        self.keep(a).wait()
        remote(self.ins[a], self.held[a].at[1 - self.core], self.pair_send.at[a], self.pair_recv.at[a], self.mate).wait_recv()
        half, w, held = ROWS[a] // 2, WIDE[a], self.held[a]
        if a < 3:
            rows = self.wide if a == 2 else self.tall
            rows[0:half, 0:w] = held[0].astype(jnp.float32)
            rows[half:2 * half, 0:w] = held[1].astype(jnp.float32)
            self.blocks[a][...] = rows[0:2 * half, 0:w].reshape(half // 4, 8, w).astype(jnp.bfloat16)
        else:
            tall = self.tall
            tall[0:135, :] = held[0].astype(jnp.float32)
            tall[134:135, :] = tall[134:135, :] + held[1, 0:1].astype(jnp.float32)
            tall[135:269, :] = held[1].astype(jnp.float32)[1:135]
            self.ahead[...] = tall[0:48, :].astype(jnp.bfloat16)
            self.look_ahead().start()
            self.look_ahead().wait_recv()
            tall[269:317, :] = jnp.where(self.chip + 1 < self.chips, self.ahead_in[...].astype(jnp.float32), 0.0)
            moved = pltpu.roll(tall[...], 320 - 3 * self.chip, axis=0)[0:272]
            self.blocks[3][...] = moved.reshape(34, 8, D).astype(jnp.bfloat16)
        self.lay(a).start()

    def spot(self, p, m, c):
        a, *cuts = PIECES[p]
        at, rows = cuts[c]
        return self.outs[a].at[pl.ds(m * TILES[a] + at, rows)]

    def level(self, d, s, go):
        if d == 0:
            go()
        else:
            pl.when((self.z - d >= 0) if s < 0 else (self.z + d < self.layers))(go)

    def cut(self, p, c):
        a, *cuts = PIECES[p]
        return self.blocks[a].at[pl.ds(*cuts[c])]

    def hops(self, p, src, m, c, slot, ways):
        for w in ways:
            if w == 2:
                remote(src, self.spot(p, m, c), self.pair_out.at[p, slot], self.pair_in.at[p, m], self.mate).start()
            else:
                to = (self.to_x, self.to_y)[w]
                remote(src, self.spot(p, m, c), self.hop_send.at[p, slot, w], self.ici_recv.at[p, m], to).start()

    def along(self, p, src, m, c, slot, up):
        def go():
            to = self.me + PLANE if up else self.me - PLANE
            remote(src, self.spot(p, m, c), self.z_send.at[p, slot, up], self.ici_recv.at[p, m], to).start()
        pl.when((self.z + 1 < self.layers) if up else (self.z > 0))(go)

    def arrived(self, p, m, c):
        s = self.spot(p, m, c)
        pltpu.make_async_copy(s, s, self.ici_recv.at[p, m]).wait()
        return s

    def flat_event(self, p, step, c):
        count = len(self.levels)
        if step == 0:
            self.hops(p, self.cut(p, c), self.chip, c, 0, (0, 1))
        for k in range(4):
            for i, (d, s) in enumerate(self.levels):
                if (0, 1, 1, 2)[k] + d != step:
                    continue
                def go():
                    m = (self.z + s * d) * 4 + self.corners[k]
                    own = k == 0 and d == 0
                    src = self.cut(p, c) if own else self.arrived(p, m, c)
                    slot = k * count + i
                    ways = () if own else (2,)
                    if d == 0 and k == 1 + c:
                        ways = (1 - c, 2)
                    for up in (0, 1):
                        if d == 0 or up == int(s < 0):
                            self.along(p, src, m, c, slot, up)
                    self.hops(p, src, m, c, slot, ways)
                self.level(d, s, go)

    def event(self, p, step, c):
        if p in FLAT:
            return self.flat_event(p, step, c)
        count = len(self.levels)
        if step == 0:
            self.hops(p, self.cut(p, c), self.chip, c, 0, (0, 1))
            for up in (0, 1):
                self.along(p, self.cut(p, c), self.chip, c, 0, up)
        for i, (d, s) in enumerate(self.levels):
            zz = self.z + s * d
            if d >= 1 and d == step:
                def go():
                    m = zz * 4 + self.corners[0]
                    src = self.arrived(p, m, c)
                    self.along(p, src, m, c, i, int(s < 0))
                    self.hops(p, src, m, c, i, (0, 1, 2))
                self.level(d, s, go)
            if d + 1 == step:
                def go():
                    m = zz * 4 + self.corners[1]
                    self.hops(p, self.arrived(p, m, c), m, c, count + i, (1, 2) if c == 0 else (2,))
                    m = zz * 4 + self.corners[2]
                    self.hops(p, self.arrived(p, m, c), m, c, 2 * count + i, (2,) if c == 0 else (0, 2))
                self.level(d, s, go)
            if d + 2 == step:
                def go():
                    m = zz * 4 + self.corners[3]
                    self.hops(p, self.arrived(p, m, c), m, c, 3 * count + i, (2,))
                self.level(d, s, go)

    def either(self, act):
        for c in (0, 1):
            pl.when(self.core == c)(lambda: act(c))

    def advance(self, steps=1):
        for _ in range(min(steps, len(self.queue))):
            _, p, step = self.queue.pop(0)
            if step == 0 and PIECES[p][0] > self.made:
                self.made = PIECES[p][0]
                self.build(self.made)
            self.either(lambda c: self.event(p, step, c))

    def ready(self, a):
        while any(PIECES[p][0] == a for _, p, _ in self.queue):
            self.advance()

        def act(c):
            for p, piece in enumerate(PIECES):
                if piece[0] != a:
                    continue
                for k in range(4):
                    for d, s in self.levels:
                        if k or d:
                            def go():
                                m = (self.z + s * d) * 4 + self.corners[k]
                                q = self.spot(p, m, 1 - c)
                                pltpu.make_async_copy(q, q, self.pair_in.at[p, m]).wait()
                            self.level(d, s, go)
        self.either(act)
        self.lay(a).wait()

    def end(self):
        count = len(self.levels)

        def act(c):
            for p in range(len(PIECES)):
                src = self.cut(p, c)

                def sent(sem):
                    pltpu.make_async_copy(src, src, sem).wait()
                for i, (d, s) in enumerate(self.levels):
                    def flat():
                        if d == 0:
                            sent(self.hop_send.at[p, 0, 0])
                            sent(self.hop_send.at[p, 0, 1])
                            sent(self.hop_send.at[p, (1 + c) * count, 1 - c])
                        for k in range(4):
                            if k or d:
                                sent(self.pair_out.at[p, k * count + i])
                            for up in (0, 1):
                                if d == 0 or up == int(s < 0):
                                    inside = (self.z + 1 < self.layers) if up else (self.z > 0)
                                    pl.when(inside)(lambda: sent(self.z_send.at[p, k * count + i, up]))

                    if p in FLAT:
                        self.level(d, s, flat)
                        continue

                    def go():
                        sent(self.hop_send.at[p, i, 0])
                        sent(self.hop_send.at[p, i, 1])
                        if c == 0:
                            sent(self.hop_send.at[p, count + i, 1])
                        else:
                            sent(self.hop_send.at[p, 2 * count + i, 0])
                        for k in range(4):
                            if k or d:
                                sent(self.pair_out.at[p, k * count + i])
                        for up in (0, 1):
                            if d == 0 or up == int(s < 0):
                                pl.when((self.z + 1 < self.layers) if up else (self.z > 0))(lambda: sent(self.z_send.at[p, i, up]))
                    self.level(d, s, go)
        self.either(act)
        for a in range(4):
            self.pair(a).wait_send()
        self.look_ahead().wait_send()


ROWS_HERE = 256
SIDE = 3
SPAN = 2 * SIDE + 1
LANES = 128
COLS = 384
STEP = 256
TOGETHER = 8
LOG2E = 1.4426950408889634
HIDE = -1e30


def mm(left, right):
    return jnp.dot(left, right, preferred_element_type=jnp.float32)


def mm_t(left, right):
    return lax.dot_general(left, right, (((1,), (1,)), ((), ())), preferred_element_type=jnp.float32)


def t_mm(left, right):
    return lax.dot_general(left, right, (((0,), (0,)), ((), ())), preferred_element_type=jnp.float32)


def moments(rows):
    center = rows - jnp.mean(rows, axis=-1, keepdims=True)
    return center, lax.rsqrt(jnp.mean(center * center, axis=-1, keepdims=True) + epsilon)


def shares_image(low, high):
    return (low * ROWS_HERE + ROWS_HERE - 1) // IMG >= (high * ROWS_HERE) // IMG


def met(me, n, k):
    other = me + k
    inside = (other >= 0) & (other < n)
    low, high = (me, other) if k > 0 else (other, me)
    return inside & shares_image(low, high)


def reach(me, n):
    first = jnp.int32(SIDE)
    last = jnp.int32(SIDE)
    for k in range(1, SIDE + 1):
        first = first - met(me, n, -k).astype(jnp.int32)
        last = last + met(me, n, k).astype(jnp.int32)
    return first, last


def slots_of(place, me):
    first = (me * ROWS_HERE) // IMG
    edge = first * IMG
    inside = jnp.where(place < edge + IMG, 0, 1)
    return jnp.where((place >= edge) & (place < edge + 2 * IMG), inside, -1)


def chosen_columns(adapters, images, me, block):
    shape = (ROWS_HERE, LANES)
    place = (me + block - SIDE) * ROWS_HERE + lax.broadcasted_iota(jnp.int32, shape, 0)
    column = lax.broadcasted_iota(jnp.int32, shape, 1)
    first = (me * ROWS_HERE) // IMG
    second = jnp.minimum(first + 1, images - 1)
    adapter = jnp.where(slots_of(place, me) == 0, adapters[first], adapters[second])
    return ((column >= adapter * RANK) & (column < adapter * RANK + RANK)).astype(jnp.float32)


def same_image(me, keys_block, query_block):
    shape = (ROWS_HERE, ROWS_HERE)
    key = (me + keys_block - SIDE) * ROWS_HERE + lax.broadcasted_iota(jnp.int32, shape, 0)
    query = (me + query_block - SIDE) * ROWS_HERE + lax.broadcasted_iota(jnp.int32, shape, 1)
    one = slots_of(key, me)
    return jnp.where((one == slots_of(query, me)) & (one >= 0), 0.0, HIDE)


class Spread:
    def __init__(self, me, n, kinds, send, recv):
        self.me, self.n, self.kinds, self.send, self.recv = me, n, kinds, send, recv
        self.out = 2 * lax.rem(me, 2) - 1
        self.mate = me - self.out

    def wants(self, device, other):
        low, high = jnp.minimum(device, other), jnp.maximum(device, other)
        return (low >= 0) & (high < self.n) & shares_image(low, high)

    def copy(self, what, i, src, block, to):
        own, held = self.kinds[what]
        at = SIDE + block - to
        return remote(src, held.at[at], self.send.at[what, i], self.recv.at[what, at], to)

    def direct(self):
        for i, step in enumerate((self.out, 3 * self.out, -2 * self.out)):
            yield i, self.me, self.me + step
        yield 3, self.me, self.mate

    def relayed(self):
        for i, step in ((4, self.out), (5, 2 * self.out)):
            yield i, self.me + step, self.mate

    def each(self, which, act):
        for i, block, to in which:
            def go():
                for what, (own, held) in enumerate(self.kinds):
                    src = own if i < 4 else held.at[SIDE + block - self.me]
                    act(what, block, self.copy(what, i, src, block, to))
            pl.when(self.wants(block, to))(go)

    def start(self):
        self.each(self.direct(), lambda what, block, copy: copy.start())

    def landed(self, what, at):
        ref = self.kinds[what][1].at[at]
        pltpu.make_async_copy(ref, ref, self.recv.at[what, at]).wait()

    def onward(self):
        def act(what, block, copy):
            self.landed(what, SIDE + block - self.me)
            copy.start()
        self.each(self.relayed(), act)

    def arrive(self):
        for step, relay in ((1, True), (2, True), (3, False), (-1, False), (-2, False), (-3, False)):
            block = self.me + step * self.out
            wanted = self.wants(self.me, block)
            if relay:
                wanted = wanted & jnp.logical_not(self.wants(block, self.mate))

            def go():
                for what in range(len(self.kinds)):
                    self.landed(what, SIDE + step * self.out)
            pl.when(wanted)(go)

    def end(self):
        self.each(self.direct(), lambda what, block, copy: copy.wait_send())
        self.each(self.relayed(), lambda what, block, copy: copy.wait_send())


def forward_kernel(n, images, tokens, in_qkv, in_out, in_fc1, in_fc2, gain, bias, fbias, qkv_down, qkv_up, out_down, out_up,
                   ff_down, fc1_up, fc2_down, fc2_up, adapters,
                   *rest):
    local_gather = n == 4 * PLANE
    shards = (in_qkv, in_out, in_fc1, in_fc2)
    weights, rest = (rest[:4], rest[4:]) if local_gather else (shards, rest)
    w_qkv, w_out, w_fc1, w_fc2 = weights
    (output, normed1, low_qkv, qt, kv, lse, mixed_t, mixed, low_out, resid, normed2, low_fc1, pre, low_fc2,
     xs, v_qkv, v_out, v_fc1, v_fc2, tmp, shade, acc, act, v_pre, x_send, x_recv, w_sem, fc1_sem, fc2_sem, pre_sem), rest = (
        rest[:30], rest[30:])
    me = lax.axis_index("dp")
    carrier = None
    if local_gather:
        carrier = Carrier(n // PLANE, shards, weights, (rest[:4],) + rest[4:8] + (rest[8:12],) + rest[12:])

    def advance(steps=1):
        if carrier:
            carrier.advance(steps)

    def ready(a):
        if carrier:
            carrier.ready(a)

    get_qkv = pltpu.make_async_copy(w_qkv, v_qkv, w_sem.at[0])
    get_out = pltpu.make_async_copy(w_out, v_out, w_sem.at[1])
    near = [k for k in range(-SIDE, SIDE + 1) if k]
    barrier = pltpu.get_barrier_semaphore()
    total = jnp.int32(0)
    for k in near:
        yes = met(me, n, k)
        total = total + yes.astype(jnp.int32)

        @pl.when(yes)
        def _():
            pl.semaphore_signal(barrier, inc=1, device_id=(me + k,), device_id_type=MESH)

    if carrier:
        total = total + carrier.greet(barrier)
    pl.semaphore_wait(barrier, total)
    if carrier:
        carrier.begin()
        advance(1)

    spread = Spread(me, n, [(tokens, xs)], x_send, x_recv)
    spread.start()
    xs[SIDE] = tokens[...]
    advance(1)
    spread.onward()
    begin, end = reach(me, n)
    for j in range(SPAN):
        shade[j] = same_image(me, j, SIDE)
    ready(0)
    get_qkv.start()
    advance(1)
    get_qkv.wait()
    m_qkv = v_qkv.reshape(3 * D, D)
    spread.arrive()

    def project(j, carry):
        center, inv = moments(xs[j].astype(jnp.float32))
        n1 = (center * inv * gain[0:1] + bias[0:1]).astype(jnp.bfloat16)
        select = chosen_columns(adapters, images, me, j)
        @pl.when(j == SIDE)
        def _():
            normed1[...] = n1
        for p in range(3):
            low = (select * mm(n1, qkv_down[p])).astype(jnp.bfloat16)
            @pl.when(j == SIDE)
            def _():
                low_qkv[p] = low
            for c in range(0, D, COLS):
                y = mm(n1, m_qkv[p * D:(p + 1) * D, c:c + COLS]) + mm(low, qkv_up[p, :, c:c + COLS])
                if p != 1:
                    y = y + bias[(1, 0, 2)[p]:(1, 0, 2)[p] + 1, c:c + COLS]
                (tmp, resid, tmp)[p][:, c:c + COLS] = y
            if p == 0:
                qt[j] = tmp[...].T.reshape(HEADS, HEAD_DIM, ROWS_HERE).astype(jnp.bfloat16)
            else:
                for h in range(HEADS):
                    kv[p - 1, j, h] = (tmp, resid, tmp)[p][:, h * HEAD_DIM:(h + 1) * HEAD_DIM].astype(jnp.bfloat16)
        return carry

    project(SIDE, 0)
    advance(1)
    lax.fori_loop(begin, jnp.int32(SIDE), project, 0)
    advance(2)
    lax.fori_loop(jnp.int32(SIDE + 1), end + 1, project, 0)
    advance(2)
    factor = HEAD_DIM ** (-0.5) * LOG2E

    def some_heads(group, carry):
        heads = [group * 4 + i for i in range(4)]
        queries = [qt[SIDE, h] for h in heads]

        def one_block(j, state):
            after = []
            for h, q, (top, total, o) in zip(heads, queries, state):
                s = mm(kv[0, j, h], q) * factor + shade[j]
                new = jnp.maximum(top, jnp.max(s, axis=0, keepdims=True))
                fade = jnp.exp2(top - new)
                p = jnp.exp2(s - new)
                total = total * fade + jnp.sum(p, axis=0, keepdims=True)
                o = o * fade + t_mm(kv[1, j, h], p.astype(jnp.bfloat16))
                after.append((new, total, o))
            return tuple(after)

        start = (jnp.full((1, ROWS_HERE), HIDE, jnp.float32), jnp.zeros((1, ROWS_HERE), jnp.float32),
                 jnp.zeros((HEAD_DIM, ROWS_HERE), jnp.float32))
        for h, (top, total, o) in zip(heads, lax.fori_loop(begin, end + 1, one_block, (start,) * 4)):
            mixed_t[h] = o / total
            lse[h] = top + jnp.log2(total)
        return carry

    for h in range(0, HEADS, 4):
        lax.fori_loop(h // 4, h // 4 + 1, some_heads, 0)
        advance(1)
    ready(1)
    get_out.start()
    att = mixed_t[...].reshape(D, ROWS_HERE).T.astype(jnp.bfloat16)
    mixed[...] = att
    select = chosen_columns(adapters, images, me, SIDE)
    get_out.wait()
    m_out = v_out.reshape(D, D)
    low = (select * mm(att, out_down[...])).astype(jnp.bfloat16)
    low_out[...] = low
    for c in range(0, D, COLS):
        s = slice(c, c + COLS)
        resid[:, s] = tokens[:, s].astype(jnp.float32) + mm(att, m_out[:, s]) + bias[3:4, s] + mm(low, out_up[:, s])
    center, inv = moments(resid[...])
    n2 = (center * inv * gain[1:2] + bias[4:5]).astype(jnp.bfloat16)
    normed2[...] = n2
    low1 = (select * mm(n2, ff_down[...])).astype(jnp.bfloat16)
    low_fc1[...] = low1

    def fetch1(i):
        slot = lax.rem(i, 2)
        cols = pl.ds(pl.multiple_of(i * STEP, STEP), STEP)
        return pltpu.make_async_copy(w_fc1.at[:, :, cols], v_fc1.at[slot], fc1_sem.at[slot])

    def fetch(i):
        slot = lax.rem(i, 2)
        rows = pl.ds(i * (STEP // 8), STEP // 8)
        return pltpu.make_async_copy(w_fc2.at[rows], v_fc2.at[slot], fc2_sem.at[slot])

    ready(2)
    fetch1(0).start()
    acc[...] = jnp.zeros_like(acc)

    def keep_pre(i):
        slot = lax.rem(i, 2)
        cols = pl.ds(pl.multiple_of(i * STEP, STEP), STEP)
        return pltpu.make_async_copy(v_pre.at[slot], pre.at[:, cols], pre_sem.at[slot])

    def feed(i, carry):
        @pl.when(i + 1 < FP // STEP)
        def _():
            fetch1(i + 1).start()
        fetch1(i).wait()
        s = pl.ds(pl.multiple_of(i * STEP, STEP), STEP)
        y = mm(n2, v_fc1[lax.rem(i, 2)].reshape(D, STEP)) + fbias[:, s] + mm(low1, fc1_up[:, s])
        slot = lax.rem(i, 2)

        @pl.when(i > 1)
        def _():
            keep_pre(i - 2).wait()
        v_pre[slot] = y
        keep_pre(i).start()
        a = (0.5 * y * (1.0 + jnp.tanh(0.7978845608028654 * (y + 0.044715 * y * y * y)))).astype(jnp.bfloat16)
        act[:, s] = a
        acc[...] += mm(a, fc2_down[s, :])
        return carry

    lax.fori_loop(0, FP // STEP, feed, 0)
    low2 = (select * acc[...]).astype(jnp.bfloat16)
    low_fc2[...] = low2
    for c in range(0, D, COLS):
        s = slice(c, c + COLS)
        tmp[:, s] = resid[:, s] + bias[5:6, s] + mm(low2, fc2_up[:, s])

    ready(3)
    fetch(0).start()

    def close(i, carry):
        @pl.when(i + 1 < FP // STEP)
        def _():
            fetch(i + 1).start()
        fetch(i).wait()
        s = pl.ds(pl.multiple_of(i * STEP, STEP), STEP)
        tmp[...] += mm(act[:, s], v_fc2[lax.rem(i, 2)].reshape(STEP, D))
        return carry

    lax.fori_loop(0, FP // STEP, close, 0)
    output[...] = tmp[...].astype(jnp.bfloat16)
    keep_pre(FP // STEP - 2).wait()
    keep_pre(FP // STEP - 1).wait()
    if carrier:
        carrier.end()
    spread.end()


def forward(n, tokens, qkv, out, fc1, fc2, gain, bias, fbias, qkv_down, qkv_up, out_down, out_up, ff_down, fc1_up,
            fc2_down, fc2_up, adapters):
    bf, f32 = jnp.bfloat16, jnp.float32
    r = ROWS_HERE
    local_gather = n == 4 * PLANE
    full = [((16 * TILES[a], 8, WIDE[a]), bf) for a in range(4)]
    outs = [
        ((r, D), bf), ((r, D), bf), ((3, r, LANES), bf), ((SPAN, HEADS, HEAD_DIM, r), bf), ((2, SPAN, HEADS, r, HEAD_DIM), bf),
        ((HEADS, 1, r), f32), ((HEADS, HEAD_DIM, r), f32), ((r, D), bf), ((r, LANES), bf), ((r, D), f32), ((r, D), bf),
        ((r, LANES), bf), ((r, FP), f32), ((r, LANES), bf),
    ]
    vmem = pl.BlockSpec(memory_space=pltpu.VMEM)
    away = pl.BlockSpec(memory_space=pl.ANY)
    dma = pltpu.SemaphoreType.DMA
    scratch = [
        pltpu.VMEM((SPAN, r, D), bf), pltpu.VMEM(*full[0]), pltpu.VMEM(*full[1]), pltpu.VMEM((2, D // 8, 8, STEP), bf),
        pltpu.VMEM((2, STEP // 8, 8, D), bf), pltpu.VMEM((r, D), f32), pltpu.VMEM((SPAN, r, r), f32), pltpu.VMEM((r, LANES), f32),
        pltpu.VMEM((r, FP), bf), pltpu.VMEM((2, r, STEP), f32), dma((1, 6)), dma((1, SPAN)), dma((2,)), dma((2,)), dma((2,)), dma((2,)),
    ]
    if local_gather:
        layers = n // PLANE
        slots, pieces, chips = 2 * layers - 1, len(PIECES), 4 * layers
        scratch += [pltpu.VMEM((2,) + s, bf) for s in ((108, D), (36, D), (36, FP), (135, D))]
        scratch += [pltpu.VMEM((48, D), bf), pltpu.VMEM((48, D), bf), pltpu.VMEM((72, FP), f32), pltpu.VMEM((320, D), f32)]
        scratch += [pltpu.VMEM((TILES[a], 8, WIDE[a]), bf) for a in range(4)]
        scratch += [dma((4,)), dma((4,)), dma((2,)), dma((4,)), dma((pieces, 4 * slots, 2)), dma((pieces, 3 * slots, 2)),
                    dma((pieces, 4 * slots)), dma((pieces, chips)), dma((pieces, chips))]
    results = pl.pallas_call(
        functools.partial(forward_kernel, n, adapters.shape[0]),
        out_shape=[jax.ShapeDtypeStruct(*o) for o in (full if local_gather else []) + outs],
        in_specs=[vmem] + [away] * 4 + [vmem] * 11 + [pl.BlockSpec(memory_space=pltpu.SMEM)],
        out_specs=([away] * 4 if local_gather else []) + [vmem] * 12 + [away, vmem],
        scratch_shapes=scratch,
        compiler_params=pltpu.CompilerParams(collective_id=1, has_side_effects=True, vmem_limit_bytes=63 << 20),
        name="layer_forward",
    )(tokens, qkv, out, fc1, fc2, gain, bias, fbias, qkv_down, qkv_up, out_down, out_up, ff_down, fc1_up, fc2_down, fc2_up, adapters)
    return results if local_gather else (qkv, out, fc1, fc2, *results)


def shards_of(n, qkv, out, fc1, fc2):
    if n == 4 * PLANE:
        core = lax.rem(lax.axis_index("dp"), 2)
        half = jnp.zeros((D // 2,), fc2.dtype)
        fc2 = jnp.where(core == 0, jnp.concatenate([fc2, half]), jnp.concatenate([half, fc2]))
        return (qkv.reshape(108, D), out.reshape(36, D), jnp.pad(fc1.reshape(36, FF), ((0, 0), (0, FP - FF))), fc2.reshape(135, D))
    qkv, out, fc1, fc2 = (lax.all_gather(v, "dp", axis=0, tiled=True) for v in (qkv, out, fc1, fc2))
    return (
        qkv.reshape(3 * D // 8, 8, D),
        out.reshape(D // 8, 8, D),
        jnp.pad(fc1.reshape(D, FF), ((0, 0), (0, FP - FF))).reshape(D // 8, 8, FP),
        jnp.pad(fc2.reshape(FF, D), ((0, FP - FF), (0, 0))).reshape(FP // 8, 8, D),
    )
CUT = 256
CHIPS = 16
SLOTS = 2 * RANK
DOWN = (3 * D, D, D, FP)


def norm_back(center, inv, gain_row, grad):
    u = center * inv
    g = grad * gain_row
    return inv * (g - jnp.mean(g, axis=-1, keepdims=True) - u * jnp.mean(g * u, axis=-1, keepdims=True))


def backward_kernel(n, images, cotangent, tokens, w_qkv, w_out, w_fc1, w_fc2, gain, bias, qkv_down, qkv_up, out_down, out_up,
                    ff_down, fc1_up, fc2_down, fc2_up, adapters,
                    normed1, low_qkv, qt, kv, lse, mixed_t, mixed, low_out, resid, normed2, low_fc1, pre, low_fc2,
                    grad_tokens, *rest):
    reduce = n == 4 * PLANE
    count = 8 if reduce else len(DOWN) + 1
    results, rest = rest[:count], rest[count:]
    (v_qkv, v_out, v_fc1, v_fc2, v_kv, own_kv, wide, dres, acc, dat, stat, dq, dk, dv,
     send, recv, w_sem, fc1_sem, fc2_sem, kv_sem, v_pre, pre_sem), rest = rest[:22], rest[22:]
    if reduce:
        (ups, *downs), rest = rest[:5], rest[5:]
        packed, mate_in, going, coming, final, mate_sem, far_send, far_recv, last_sem = (
            rest[0:2], rest[2:6], rest[6:10], rest[10:14], rest[14:22], *rest[22:26])
    else:
        ups, *downs = results
    g_qkv, g_out, g_ff, g_fc2 = downs
    me = lax.axis_index("dp")
    core = lax.rem(me, 2)
    chip = me // 2
    mate = me + 1 - 2 * core
    own = pltpu.make_async_copy(kv.at[:, SIDE], own_kv, w_sem.at[0])
    own.start()
    get_out = pltpu.make_async_copy(w_out, v_out, w_sem.at[1])
    get_out.start()

    def fetch_qkv(t):
        rows = pl.ds(t * COLS, COLS)
        return pltpu.make_async_copy(w_qkv.at[rows, :], v_qkv.at[t % 2], w_sem.at[2 + t % 2])

    fetch_qkv(0).start()

    def fetch1(i):
        slot = lax.rem(i, 2)
        cols = pl.ds(pl.multiple_of(i * STEP, STEP), STEP)
        return pltpu.make_async_copy(w_fc1.at[:, cols], v_fc1.at[slot], fc1_sem.at[slot])

    def fetch2(i):
        slot = lax.rem(i, 2)
        rows = pl.ds(pl.multiple_of(i * STEP, STEP), STEP)
        return pltpu.make_async_copy(w_fc2.at[rows, :], v_fc2.at[slot], fc2_sem.at[slot])

    def fetch_pre(i):
        slot = lax.rem(i, 2)
        cols = pl.ds(pl.multiple_of(i * STEP, STEP), STEP)
        return pltpu.make_async_copy(pre.at[:, cols], v_pre.at[slot], pre_sem.at[slot])

    fetch1(0).start()
    fetch2(0).start()
    fetch_pre(0).start()
    near = [k for k in range(-SIDE, SIDE + 1) if k]
    barrier = pltpu.get_barrier_semaphore()
    total = jnp.int32(0)
    for k in near:
        yes = met(me, n, k)
        total = total + yes.astype(jnp.int32)

        @pl.when(yes)
        def _():
            pl.semaphore_signal(barrier, inc=1, device_id=(me + k,), device_id_type=MESH)

    if reduce:
        for k in range(1, CHIPS):
            pl.semaphore_signal(barrier, inc=1, device_id=(lax.rem(me + 2 * k, n),), device_id_type=MESH)
        pl.semaphore_signal(barrier, inc=1, device_id=(mate,), device_id_type=MESH)
        total = total + CHIPS
    begin, end = reach(me, n)
    bf = jnp.bfloat16
    select = chosen_columns(adapters, images, me, SIDE)

    def narrow(glow):
        if not reduce:
            return glow
        first = (chip * 2 * ROWS_HERE) // IMG
        shape = (LANES, SLOTS)
        lane = lax.broadcasted_iota(jnp.int32, shape, 1)
        late = lane >= RANK
        adapter = jnp.where(late, adapters[jnp.minimum(first + 1, images - 1)], adapters[first])
        pick = lax.broadcasted_iota(jnp.int32, shape, 0) == adapter * RANK + lane - jnp.where(late, RANK, 0)
        place = me * ROWS_HERE + lax.broadcasted_iota(jnp.int32, (ROWS_HERE, SLOTS), 0)
        mine = (place >= (first + 1) * IMG) == (lax.broadcasted_iota(jnp.int32, (ROWS_HERE, SLOTS), 1) >= RANK)
        return jnp.where(mine, mm(glow, pick.astype(bf)), 0.0).astype(bf)

    def put_up(at, value):
        ups[:, :, at] = value.reshape(CHIPS, 8, value.shape[-1])

    e = cotangent[...]
    put_up(slice(0, D), t_mm(low_fc2[...], e))
    glow2 = (select * mm_t(e, fc2_up[...])).astype(bf)
    acc[...] = jnp.zeros_like(acc)
    wide[...] = jnp.zeros_like(wide)
    low1 = low_fc1[...]
    glow2n = narrow(glow2)

    def feed(i, carry):
        @pl.when(i + 1 < FP // STEP)
        def _():
            fetch1(i + 1).start()
            fetch2(i + 1).start()
            fetch_pre(i + 1).start()
        fetch_pre(i).wait()
        fetch1(i).wait()
        fetch2(i).wait()
        slot = lax.rem(i, 2)
        s = pl.ds(pl.multiple_of(i * STEP, STEP), STEP)
        y = v_pre[slot]
        t = jnp.tanh(0.7978845608028654 * (y + 0.044715 * y * y * y))
        half = 0.5 * (1.0 + t)
        a = (y * half).astype(bf)
        slope = half + 0.5 * y * (1.0 - t * t) * (0.7978845608028654 * (1.0 + 3.0 * 0.044715 * y * y))
        g_fc2[:, s] = t_mm(glow2n, a)
        g = mm_t(e, v_fc2[slot]) + mm_t(glow2, fc2_down[s, :])
        gp = (g * slope).astype(bf)
        put_up(pl.ds(pl.multiple_of(D + i * STEP, LANES), STEP), t_mm(low1, gp))
        acc[...] += mm_t(gp, fc1_up[:, s])
        wide[...] += mm_t(gp, v_fc1[slot])
        return carry

    lax.fori_loop(0, FP // STEP, feed, 0)
    glow1 = (select * acc[...]).astype(bf)
    g_ff[...] = t_mm(narrow(glow1), normed2[...])
    center, inv = moments(resid[...])
    dres[...] = e.astype(jnp.float32) + norm_back(center, inv, gain[1:2], wide[...] + mm_t(glow1, ff_down[...]))
    gb = dres[...].astype(bf)
    put_up(slice(D + FP, 2 * D + FP), t_mm(low_out[...], gb))
    glow = (select * mm_t(gb, out_up[...])).astype(bf)
    g_out[...] = t_mm(narrow(glow), mixed[...])
    get_out.wait()
    for c in range(0, D, COLS):
        wide[:, c:c + COLS] = mm_t(gb, v_out[c:c + COLS, :]) + mm_t(glow, out_down[c:c + COLS, :])
    da = wide[...].T.reshape(HEADS, HEAD_DIM, ROWS_HERE).astype(bf)
    dat[SIDE] = da
    delta = jnp.sum(da.astype(jnp.float32) * mixed_t[...], axis=1, keepdims=True)
    stat[SIDE, 0] = lse[...].reshape(HEADS, ROWS_HERE)
    stat[SIDE, 1] = delta.reshape(HEADS, ROWS_HERE)

    pl.semaphore_wait(barrier, total)

    half = CHIPS // 2
    early = 2 * D + FP
    if reduce:
        upper = (ups.at[:, :, 0:early], ups.at[:, :, early:early + 3 * D])

        def source(i):
            return upper[i // 2] if i % 2 == 0 else packed[i // 2]

        def to_mate(i):
            return remote(source(i).at[pl.ds(half * (1 - core), half)], mate_in[i], mate_sem.at[0, i], mate_sem.at[1, i], mate)

        def to_chip(i, k):
            return remote(going[i].at[k], coming[i].at[chip], far_send.at[i, k], far_recv.at[i, chip], 2 * (half * core + k) + core)

        def pass_on(i):
            to_mate(i).wait_recv()

            def one(k, carry):
                going[i][k] = (source(i)[half * core + k] + mate_in[i][k]).astype(bf)

                @pl.when(half * core + k != chip)
                def _():
                    to_chip(i, k).start()
                return carry

            lax.fori_loop(0, half, one, 0)

            @pl.when(core == chip // half)
            def _():
                coming[i][chip] = going[i][chip - half * core]

        def gathered(i):
            for k in range(CHIPS):
                @pl.when(chip != k)
                def _():
                    pltpu.make_async_copy(coming[i].at[k], coming[i].at[k], far_recv.at[i, k]).wait()

        def add_up(i):
            gathered(i)
            return lax.fori_loop(1, CHIPS, lambda k, sofar: sofar + coming[i][k].astype(jnp.float32), coming[i][0].astype(jnp.float32))

        def add_down(i):
            gathered(i)
            shape = (LANES, SLOTS)
            lane = lax.broadcasted_iota(jnp.int32, shape, 1)
            late = lane >= RANK
            sofar = None
            for k in range(CHIPS):
                first = (k * 2 * ROWS_HERE) // IMG
                adapter = jnp.where(late, adapters[min(first + 1, images - 1)], adapters[first])
                pick = lax.broadcasted_iota(jnp.int32, shape, 0) == adapter * RANK + lane - jnp.where(late, RANK, 0)
                part = mm(pick.astype(bf), coming[i][k])
                sofar = part if k == 0 else sofar + part
            return sofar.T

        def flat_rows(ref, start, rows):
            for t in range(D // LANES):
                ref[pl.ds(start * (D // LANES) + t, rows.shape[0], stride=D // LANES), :] = rows[:, t * LANES:(t + 1) * LANES]

        def hand_out(which):
            for r in which:
                results[r][...] = final[r][core]
                remote(final[r].at[1 - core], results[r], last_sem.at[0, r], last_sem.at[1, r], mate).start()

        (f_qkv_down, f_qkv_up, f_out_down, f_out_up, f_ff_down, f_fc1_up, f_fc2_down, f_fc2_up) = final

        def finish_early():
            v = add_up(0)
            for q in range(2):
                flat_rows(f_fc2_up.at[q], 0, v[4 * q:4 * q + 4, 0:D])
                f_fc1_up[q] = v[4 * q:4 * q + 4, D:D + FP]
                flat_rows(f_out_up.at[q], 0, v[4 * q:4 * q + 4, D + FP:2 * D + FP])
            v = add_down(1)
            f_fc2_down[0] = v[0:135]
            turned = pltpu.roll(v, 64, axis=1)
            left = lax.broadcasted_iota(jnp.int32, (135, LANES), 1) < 64
            f_fc2_down[1] = jnp.where(left, turned[134:269], turned[135:270])
            for q in range(2):
                f_ff_down[q] = v[384 + 36 * q:420 + 36 * q]
                f_out_down[q] = v[512 + 36 * q:548 + 36 * q]
            hand_out((2, 3, 4, 5, 6, 7))

        def finish_late():
            v = add_up(2)
            flat_rows(f_qkv_up.at[0], 0, v[:, 0:D])
            flat_rows(f_qkv_up.at[0], 8, v[0:4, D:2 * D])
            flat_rows(f_qkv_up.at[1], 0, v[4:8, D:2 * D])
            flat_rows(f_qkv_up.at[1], 4, v[:, 2 * D:3 * D])
            v = add_down(3)
            for q in range(2):
                f_qkv_down[q] = v[108 * q:108 * q + 108]
            hand_out((0, 1))

        for m in range(CHIPS):
            packed[0][m, :, 0:269] = g_fc2[:, 269 * m:269 * m + 269]
            packed[0][m, :, 384:456] = g_ff[:, 72 * m:72 * m + 72]
            packed[0][m, :, 512:584] = g_out[:, 72 * m:72 * m + 72]
        to_mate(0).start()
        to_mate(1).start()

    spread = Spread(me, n, [(dat.at[SIDE], dat), (stat.at[SIDE], stat)], send, recv)
    spread.start()
    factor = HEAD_DIM ** (-0.5) * LOG2E

    parts = ROWS_HERE // CUT

    def stats(j, group):
        both = [stat[j, i, pl.ds(pl.multiple_of(group * TOGETHER, TOGETHER), TOGETHER), :] for i in (0, 1)]
        return [(both[0][i:i + 1], both[1][i:i + 1]) for i in range(TOGETHER)]

    def blocks(heads, keys, vals, q, d, st, shade, which):
        add_q, add_k, add_v = [], [], []
        for i in range(len(heads)):
            more_q, more_k, more_v = None, [], []
            for c in range(parts):
                rows = slice(c * CUT, (c + 1) * CUT)
                s = mm(keys[i][rows], q[i]) * factor + shade[rows]
                p = jnp.exp2(s - st[i][0])
                ds = (p * (mm(vals[i][rows], d[i]) - st[i][1])).astype(bf)
                if which != 2:
                    y = t_mm(keys[i][rows], ds)
                    more_q = y if more_q is None else more_q + y
                if which != 1:
                    more_k.append(mm_t(q[i], ds))
                    more_v.append(mm_t(d[i], p.astype(bf)))
            add_q.append(more_q)
            add_k.append(jnp.concatenate(more_k, axis=1) if more_k else None)
            add_v.append(jnp.concatenate(more_v, axis=1) if more_v else None)
        if which == 1:
            add_q = [a + dq[h] for h, a in zip(heads, add_q)]
        if which == 2:
            add_k = [a + dk[h] for h, a in zip(heads, add_k)]
            add_v = [a + dv[h] for h, a in zip(heads, add_v)]
        for i, h in enumerate(heads):
            if which != 2:
                dq[h] = add_q[i]
            if which != 1:
                dk[h] = add_k[i]
                dv[h] = add_v[i]

    own.wait()
    shade = same_image(me, SIDE, SIDE)

    def own_head(group, carry):
        heads = [group * TOGETHER + i for i in range(TOGETHER)]
        blocks(heads, [own_kv[0, h] for h in heads], [own_kv[1, h] for h in heads], [qt[SIDE, h] for h in heads],
               [dat[SIDE, h] for h in heads], stats(SIDE, group), shade, 0)
        return carry

    def get_kv(j):
        slot = lax.rem(j, 2)
        return pltpu.make_async_copy(kv.at[:, j], v_kv.at[slot], kv_sem.at[slot])

    get_kv(begin).start()
    lax.fori_loop(0, HEADS // TOGETHER, own_head, 0)
    spread.onward()

    def pass_one(j, carry):
        @pl.when(j < end)
        def _():
            get_kv(j + 1).start()
        get_kv(j).wait()

        @pl.when(j != SIDE)
        def _():
            shade = same_image(me, j, SIDE)
            slot = lax.rem(j, 2)

            def head(group, carry):
                heads = [group * TOGETHER + i for i in range(TOGETHER)]
                blocks(heads, [v_kv[slot, 0, h] for h in heads], [v_kv[slot, 1, h] for h in heads], [qt[SIDE, h] for h in heads],
                       [dat[SIDE, h] for h in heads], stats(SIDE, group), shade, 1)
                return carry

            lax.fori_loop(0, HEADS // TOGETHER, head, 0)
        return carry

    lax.fori_loop(begin, end + 1, pass_one, 0)
    spread.arrive()
    if reduce:
        pass_on(0)
        pass_on(1)

    def pass_two(j, carry):
        @pl.when(j != SIDE)
        def _():
            shade = same_image(me, SIDE, j)

            def head(group, carry):
                heads = [group * TOGETHER + i for i in range(TOGETHER)]
                blocks(heads, [own_kv[0, h] for h in heads], [own_kv[1, h] for h in heads], [qt[j, h] for h in heads],
                       [dat[j, h] for h in heads], stats(j, group), shade, 2)
                return carry

            lax.fori_loop(0, HEADS // TOGETHER, head, 0)
        return carry

    lax.fori_loop(begin, end + 1, pass_two, 0)
    n1 = normed1[...]
    grads = []
    for p, total_grad in enumerate((dq, dk, dv)):
        value = total_grad[...] * HEAD_DIM ** (-0.5) if p < 2 else total_grad[...]
        g = value.reshape(D, ROWS_HERE).T.astype(bf)
        rows = t_mm(low_qkv[p], g)
        for t in range(LANES // 8):
            at = p * (LANES // 8) + t
            ups[at // 3, :, early + at % 3 * D:early + at % 3 * D + D] = rows[8 * t:8 * t + 8]
        glow = (select * mm_t(g, qkv_up[p])).astype(bf)
        g_qkv[:, p * D:(p + 1) * D] = t_mm(narrow(glow), n1)
        grads.append((g, glow))
    if reduce:
        for m in range(CHIPS):
            packed[1][m, :, 0:216] = g_qkv[:, 216 * m:216 * m + 216]
        to_mate(2).start()
        to_mate(3).start()
    for p, (g, glow) in enumerate(grads):
        for c in range(0, D, COLS):
            s = slice(c, c + COLS)
            t = (p * D + c) // COLS
            if t + 1 < 3 * D // COLS:
                fetch_qkv(t + 1).start()
            fetch_qkv(t).wait()
            y = mm_t(g, v_qkv[t % 2]) + mm_t(glow, qkv_down[p, s, :])
            wide[:, s] = y if p == 0 else wide[:, s] + y
        if reduce and p == 0:
            pass_on(2)
            pass_on(3)
    center, inv = moments(tokens[...].astype(jnp.float32))
    grad_tokens[...] = (dres[...] + norm_back(center, inv, gain[0:1], wide[...])).astype(bf)
    spread.end()
    if reduce:
        reducer = core == chip // half

        @pl.when(reducer)
        def _():
            finish_early()
            finish_late()
            for r in range(8):
                remote(final[r].at[1 - core], results[r], last_sem.at[0, r], last_sem.at[1, r], mate).wait_send()

        @pl.when(jnp.logical_not(reducer))
        def _():
            for r in range(8):
                pltpu.make_async_copy(results[r], results[r], last_sem.at[1, r]).wait()

        for i in range(4):
            to_mate(i).wait_send()
            for k in range(half):
                @pl.when(half * core + k != chip)
                def _():
                    to_chip(i, k).wait_send()


def backward(n, cotangent, tokens, w_qkv, w_out, w_fc1, w_fc2, gain, bias, qkv_down, qkv_up, out_down, out_up, ff_down, fc1_up,
             fc2_down, fc2_up, adapters, saved):
    bf, f32 = jnp.bfloat16, jnp.float32
    r = ROWS_HERE
    reduce = n == 4 * PLANE
    deep = SLOTS if reduce else LANES
    partial = [((CHIPS, 8, 5 * D + FP), f32)] + [((deep, w), f32) for w in DOWN]
    shares = [(108, LANES), (108, LANES), (36, LANES), (36, LANES), (36, LANES), (4, FP), (135, LANES), (36, LANES)]
    outs = [((r, D), bf)] + ([(s, f32) for s in shares] if reduce else partial)
    more = []
    if reduce:
        half = CHIPS // 2
        up, down = (2 * D + FP, 3 * D), (640, 256)
        more = [pltpu.VMEM(*v) for v in partial]
        more += [pltpu.VMEM((CHIPS, SLOTS, w), f32) for w in down]
        for rows, kind in ((half, f32), (half, bf), (CHIPS, bf)):
            for w, v in zip(up, down):
                more += [pltpu.VMEM((rows, 8, w), kind), pltpu.VMEM((rows, SLOTS, v), kind)]
        more += [pltpu.VMEM((2,) + s, f32) for s in shares]
        dma = pltpu.SemaphoreType.DMA
        more += [dma((2, 4)), dma((4, half)), dma((4, CHIPS)), dma((2, 8))]
    vmem = pl.BlockSpec(memory_space=pltpu.VMEM)
    away = pl.BlockSpec(memory_space=pl.ANY)
    dma = pltpu.SemaphoreType.DMA
    heads = (HEADS, HEAD_DIM, r)
    return pl.pallas_call(
        functools.partial(backward_kernel, n, adapters.shape[0]),
        out_shape=[jax.ShapeDtypeStruct(*o) for o in outs],
        in_specs=[vmem] * 2 + [away] * 4 + [vmem] * 10 + [pl.BlockSpec(memory_space=pltpu.SMEM)] + [vmem] * 3 + [away] + [vmem] * 7 + [away, vmem],
        out_specs=[vmem] * len(outs),
        scratch_shapes=[
            pltpu.VMEM((2, COLS, D), bf), pltpu.VMEM((D, D), bf), pltpu.VMEM((2, D, STEP), bf), pltpu.VMEM((2, STEP, D), bf),
            pltpu.VMEM((2, 2, HEADS, r, HEAD_DIM), bf), pltpu.VMEM((2, HEADS, r, HEAD_DIM), bf),
            pltpu.VMEM((r, D), f32), pltpu.VMEM((r, D), f32), pltpu.VMEM((r, LANES), f32),
            pltpu.VMEM((SPAN,) + heads, bf), pltpu.VMEM((SPAN, 2, HEADS, r), f32),
            pltpu.VMEM(heads, f32), pltpu.VMEM(heads, f32), pltpu.VMEM(heads, f32),
            dma((2, 6)), dma((2, SPAN)), dma((4,)), dma((2,)), dma((2,)), dma((2,)),
            pltpu.VMEM((2, r, STEP), f32), dma((2,)),
        ] + more,
        compiler_params=pltpu.CompilerParams(collective_id=2, has_side_effects=True, vmem_limit_bytes=63 << 20),
        name="layer_backward",
    )(cotangent, tokens, w_qkv, w_out, w_fc1, w_fc2, gain, bias, qkv_down, qkv_up, out_down, out_up, ff_down, fc1_up, fc2_down,
      fc2_up, adapters, *saved)


def deliver_kernel(*refs):
    half = len(refs) // 2
    for i in range(half):
        refs[half + i][...] = refs[i][...]


def deliver(*arrays):
    vmem = pl.BlockSpec(memory_space=pltpu.VMEM)
    return pl.pallas_call(
        deliver_kernel,
        out_shape=[jax.ShapeDtypeStruct(a.shape, a.dtype) for a in arrays],
        in_specs=[vmem] * len(arrays),
        out_specs=[vmem] * len(arrays),
        name="deliver",
    )(*arrays)

def local(
    tokens,
    qkv_weights,
    out_weights,
    fc1_weights,
    fc2_weights,
    ln_gain,
    bias_model,
    first_feedforward_bias,
    qkv_down,
    qkv_up,
    out_down,
    out_up,
    first_feedforward_down,
    fc1_up,
    fc2_down,
    fc2_up,
    adapter_of_image,
    cotangent,
):
    n = lax.axis_size("dp")
    shards = shards_of(n, qkv_weights, out_weights, fc1_weights, fc2_weights)
    tail = FP - FF
    fbias = jnp.pad(first_feedforward_bias, (0, tail))[None]
    fc1_up = jnp.pad(fc1_up, ((0, 0), (0, tail)))
    fc2_down = jnp.pad(fc2_down, ((0, tail), (0, 0)))
    factors = (qkv_down, qkv_up, out_down, out_up, first_feedforward_down, fc1_up, fc2_down, fc2_up, adapter_of_image)
    results = forward(n, tokens, *shards, ln_gain, bias_model, fbias, *factors)
    weights, output, saved = results[:4], results[4], results[5:]
    weights = [w.reshape(-1, w.shape[-1]) for w in weights]
    grad_tokens, *grads = backward(n, cotangent, tokens, *weights, ln_gain, bias_model, *factors, saved)
    if n == 4 * PLANE:
        output, grad_tokens, *grads = deliver(output, grad_tokens, *grads)
        grads[5] = grads[5][:, :FF]
        summed = [g.reshape(-1) for g in grads]
        summed[6] = summed[6][: FF * LANES // n]
        return (output, grad_tokens, *summed)
    ups, g_qkv, g_out, g_ff, g_fc2 = grads
    early = 2 * D + FP
    g_up = ups[:, :, early:].reshape(CHIPS, 8, 3, D).transpose(0, 2, 1, 3)
    parts = (
        g_qkv.T,
        g_up,
        g_out.T,
        ups[:, :, D + FP : early],
        g_ff.T,
        ups[:, :, D : D + FF],
        g_fc2.T[:FF],
        ups[:, :, :D],
    )
    summed = [lax.psum_scatter(g.reshape(-1), "dp", scatter_dimension=0, tiled=True) for g in parts]
    return (output, grad_tokens, *summed)


def solution(mesh):
    return jax.shard_map(
        local,
        mesh=mesh,
        in_specs=(P("dp", None),) + (P("dp"),) * 4 + (P(),) * 12 + (P("dp", None),),
        out_specs=(P("dp", None),) * 2 + (P("dp"),) * 8,
        check_vma=False,
    )
```

```python
import functools

import jax
import jax.numpy as jnp
from jax import lax
from jax.experimental import pallas as pl
from jax.experimental.pallas import tpu as pltpu
from jax.sharding import PartitionSpec as P

D = 1152
HEADS = 16
HEAD_DIM = 72
FF = 4304
FP = 4352
IMG = 729
RANK = 16
ADAPTERS = 8
epsilon = 1e-06


MESH = pl.DeviceIdType.MESH
PLANE = 8
ROWS = (216, 72, 72, 272)
WIDE = (D, D, FP, D)
TILES = tuple(rows // 8 for rows in ROWS)
def remote(src, dst, send, recv, to):
    return pltpu.make_async_remote_copy(src_ref=src, dst_ref=dst, send_sem=send, recv_sem=recv, device_id=(to,), device_id_type=MESH)

PIECES = (
    (0, (0, 14), (14, 13)),
    (1, (0, 5), (5, 4)),
    (2, (0, 4), (4, 5)),
    (3, (0, 8), (17, 8)),
    (3, (8, 9), (25, 9)),
)
FLAT = (1, 4)
START = (0, 4, 5, 6, 7)


class Carrier:
    def __init__(self, layers, ins, outs, scratch):
        (self.held, self.ahead, self.ahead_in, self.wide, self.tall, self.blocks, self.pair_send, self.pair_recv, self.ahead_sem,
         self.own_sem, self.z_send, self.hop_send, self.pair_out, self.ici_recv, self.pair_in) = scratch
        self.layers, self.ins, self.outs = layers, ins, outs
        me = self.me = lax.axis_index("dp")
        self.core = lax.rem(me, 2)
        x = lax.rem(me // 2, 2)
        y = lax.rem(me // 4, 2)
        self.z = me // PLANE
        self.chip = me // 2
        self.chips = 4 * layers
        self.mate = me + 1 - 2 * self.core
        self.to_x = me + 2 - 4 * x
        self.to_y = me + 4 - 8 * y
        self.nxt = lax.rem(self.chip + 1, self.chips) * 2 + self.core
        self.prv = lax.rem(self.chip + self.chips - 1, self.chips) * 2 + self.core
        self.levels = [(d, s) for d in range(layers) for s in ((0,) if d == 0 else (-1, 1))]
        plane = lax.rem(self.chip, 4)
        self.corners = (plane, plane + 1 - 2 * x, plane + 2 - 4 * y, 3 - plane)
        self.made = -1
        last = layers + 1
        self.queue = sorted((START[p] + step, p, step) for p in range(len(PIECES)) for step in range(last + 1))

    def greet(self, barrier):
        spot = lax.rem(self.me, PLANE)
        up = lax.rem(self.z + 1, self.layers) * PLANE + spot
        down = lax.rem(self.z + self.layers - 1, self.layers) * PLANE + spot
        peers = (self.mate, self.to_x, self.to_y, self.nxt, self.prv, up, down)
        for peer in peers:
            pl.semaphore_signal(barrier, inc=1, device_id=(peer,), device_id_type=MESH)
        return len(peers)

    def pair(self, a):
        return remote(self.ins[a], self.held[a].at[self.core], self.pair_send.at[a], self.pair_recv.at[a], self.mate)

    def keep(self, a):
        return pltpu.make_async_copy(self.ins[a], self.held[a].at[self.core], self.own_sem.at[a])

    def lay(self, a):
        whole = self.outs[a].at[pl.ds(self.chip * TILES[a], TILES[a])]
        return pltpu.make_async_copy(self.blocks[a], whole, self.own_sem.at[a])

    def look_ahead(self):
        return remote(self.ahead, self.ahead_in, self.ahead_sem.at[0], self.ahead_sem.at[1], self.prv)

    def begin(self):
        for a in range(4):
            self.pair(a).start()
            self.keep(a).start()

    def build(self, a):
        self.keep(a).wait()
        remote(self.ins[a], self.held[a].at[1 - self.core], self.pair_send.at[a], self.pair_recv.at[a], self.mate).wait_recv()
        half, w, held = ROWS[a] // 2, WIDE[a], self.held[a]
        if a < 3:
            rows = self.wide if a == 2 else self.tall
            rows[0:half, 0:w] = held[0].astype(jnp.float32)
            rows[half:2 * half, 0:w] = held[1].astype(jnp.float32)
            self.blocks[a][...] = rows[0:2 * half, 0:w].reshape(half // 4, 8, w).astype(jnp.bfloat16)
        else:
            tall = self.tall
            tall[0:135, :] = held[0].astype(jnp.float32)
            tall[134:135, :] = tall[134:135, :] + held[1, 0:1].astype(jnp.float32)
            tall[135:269, :] = held[1].astype(jnp.float32)[1:135]
            self.ahead[...] = tall[0:48, :].astype(jnp.bfloat16)
            self.look_ahead().start()
            self.look_ahead().wait_recv()
            tall[269:317, :] = jnp.where(self.chip + 1 < self.chips, self.ahead_in[...].astype(jnp.float32), 0.0)
            moved = pltpu.roll(tall[...], 320 - 3 * self.chip, axis=0)[0:272]
            self.blocks[3][...] = moved.reshape(34, 8, D).astype(jnp.bfloat16)
        self.lay(a).start()

    def spot(self, p, m, c):
        a, *cuts = PIECES[p]
        at, rows = cuts[c]
        return self.outs[a].at[pl.ds(m * TILES[a] + at, rows)]

    def level(self, d, s, go):
        if d == 0:
            go()
        else:
            pl.when((self.z - d >= 0) if s < 0 else (self.z + d < self.layers))(go)

    def cut(self, p, c):
        a, *cuts = PIECES[p]
        return self.blocks[a].at[pl.ds(*cuts[c])]

    def hops(self, p, src, m, c, slot, ways):
        for w in ways:
            if w == 2:
                remote(src, self.spot(p, m, c), self.pair_out.at[p, slot], self.pair_in.at[p, m], self.mate).start()
            else:
                to = (self.to_x, self.to_y)[w]
                remote(src, self.spot(p, m, c), self.hop_send.at[p, slot, w], self.ici_recv.at[p, m], to).start()

    def along(self, p, src, m, c, slot, up):
        def go():
            to = self.me + PLANE if up else self.me - PLANE
            remote(src, self.spot(p, m, c), self.z_send.at[p, slot, up], self.ici_recv.at[p, m], to).start()
        pl.when((self.z + 1 < self.layers) if up else (self.z > 0))(go)

    def arrived(self, p, m, c):
        s = self.spot(p, m, c)
        pltpu.make_async_copy(s, s, self.ici_recv.at[p, m]).wait()
        return s

    def flat_event(self, p, step, c):
        count = len(self.levels)
        if step == 0:
            self.hops(p, self.cut(p, c), self.chip, c, 0, (0, 1))
        for k in range(4):
            for i, (d, s) in enumerate(self.levels):
                if (0, 1, 1, 2)[k] + d != step:
                    continue
                def go():
                    m = (self.z + s * d) * 4 + self.corners[k]
                    own = k == 0 and d == 0
                    src = self.cut(p, c) if own else self.arrived(p, m, c)
                    slot = k * count + i
                    ways = () if own else (2,)
                    if d == 0 and k == 1 + c:
                        ways = (1 - c, 2)
                    for up in (0, 1):
                        if d == 0 or up == int(s < 0):
                            self.along(p, src, m, c, slot, up)
                    self.hops(p, src, m, c, slot, ways)
                self.level(d, s, go)

    def event(self, p, step, c):
        if p in FLAT:
            return self.flat_event(p, step, c)
        count = len(self.levels)
        if step == 0:
            self.hops(p, self.cut(p, c), self.chip, c, 0, (0, 1))
            for up in (0, 1):
                self.along(p, self.cut(p, c), self.chip, c, 0, up)
        for i, (d, s) in enumerate(self.levels):
            zz = self.z + s * d
            if d >= 1 and d == step:
                def go():
                    m = zz * 4 + self.corners[0]
                    src = self.arrived(p, m, c)
                    self.along(p, src, m, c, i, int(s < 0))
                    self.hops(p, src, m, c, i, (0, 1, 2))
                self.level(d, s, go)
            if d + 1 == step:
                def go():
                    m = zz * 4 + self.corners[1]
                    self.hops(p, self.arrived(p, m, c), m, c, count + i, (1, 2) if c == 0 else (2,))
                    m = zz * 4 + self.corners[2]
                    self.hops(p, self.arrived(p, m, c), m, c, 2 * count + i, (2,) if c == 0 else (0, 2))
                self.level(d, s, go)
            if d + 2 == step:
                def go():
                    m = zz * 4 + self.corners[3]
                    self.hops(p, self.arrived(p, m, c), m, c, 3 * count + i, (2,))
                self.level(d, s, go)

    def either(self, act):
        for c in (0, 1):
            pl.when(self.core == c)(lambda: act(c))

    def advance(self, steps=1):
        for _ in range(min(steps, len(self.queue))):
            _, p, step = self.queue.pop(0)
            if step == 0 and PIECES[p][0] > self.made:
                self.made = PIECES[p][0]
                self.build(self.made)
            self.either(lambda c: self.event(p, step, c))

    def ready(self, a):
        while any(PIECES[p][0] == a for _, p, _ in self.queue):
            self.advance()

        def act(c):
            for p, piece in enumerate(PIECES):
                if piece[0] != a:
                    continue
                for k in range(4):
                    for d, s in self.levels:
                        if k or d:
                            def go():
                                m = (self.z + s * d) * 4 + self.corners[k]
                                q = self.spot(p, m, 1 - c)
                                pltpu.make_async_copy(q, q, self.pair_in.at[p, m]).wait()
                            self.level(d, s, go)
        self.either(act)
        self.lay(a).wait()

    def end(self):
        count = len(self.levels)

        def act(c):
            for p in range(len(PIECES)):
                src = self.cut(p, c)

                def sent(sem):
                    pltpu.make_async_copy(src, src, sem).wait()
                for i, (d, s) in enumerate(self.levels):
                    def flat():
                        if d == 0:
                            sent(self.hop_send.at[p, 0, 0])
                            sent(self.hop_send.at[p, 0, 1])
                            sent(self.hop_send.at[p, (1 + c) * count, 1 - c])
                        for k in range(4):
                            if k or d:
                                sent(self.pair_out.at[p, k * count + i])
                            for up in (0, 1):
                                if d == 0 or up == int(s < 0):
                                    inside = (self.z + 1 < self.layers) if up else (self.z > 0)
                                    pl.when(inside)(lambda: sent(self.z_send.at[p, k * count + i, up]))

                    if p in FLAT:
                        self.level(d, s, flat)
                        continue

                    def go():
                        sent(self.hop_send.at[p, i, 0])
                        sent(self.hop_send.at[p, i, 1])
                        if c == 0:
                            sent(self.hop_send.at[p, count + i, 1])
                        else:
                            sent(self.hop_send.at[p, 2 * count + i, 0])
                        for k in range(4):
                            if k or d:
                                sent(self.pair_out.at[p, k * count + i])
                        for up in (0, 1):
                            if d == 0 or up == int(s < 0):
                                pl.when((self.z + 1 < self.layers) if up else (self.z > 0))(lambda: sent(self.z_send.at[p, i, up]))
                    self.level(d, s, go)
        self.either(act)
        for a in range(4):
            self.pair(a).wait_send()
        self.look_ahead().wait_send()


ROWS_HERE = 256
SIDE = 3
SPAN = 2 * SIDE + 1
LANES = 128
COLS = 384
STEP = 256
TOGETHER = 8
LOG2E = 1.4426950408889634
HIDE = -1e30


def mm(left, right):
    return jnp.dot(left, right, preferred_element_type=jnp.float32)


def mm_t(left, right):
    return lax.dot_general(left, right, (((1,), (1,)), ((), ())), preferred_element_type=jnp.float32)


def t_mm(left, right):
    return lax.dot_general(left, right, (((0,), (0,)), ((), ())), preferred_element_type=jnp.float32)


def moments(rows):
    center = rows - jnp.mean(rows, axis=-1, keepdims=True)
    return center, lax.rsqrt(jnp.mean(center * center, axis=-1, keepdims=True) + epsilon)


def shares_image(low, high):
    return (low * ROWS_HERE + ROWS_HERE - 1) // IMG >= (high * ROWS_HERE) // IMG


def met(me, n, k):
    other = me + k
    inside = (other >= 0) & (other < n)
    low, high = (me, other) if k > 0 else (other, me)
    return inside & shares_image(low, high)


def reach(me, n):
    first = jnp.int32(SIDE)
    last = jnp.int32(SIDE)
    for k in range(1, SIDE + 1):
        first = first - met(me, n, -k).astype(jnp.int32)
        last = last + met(me, n, k).astype(jnp.int32)
    return first, last


def slots_of(place, me):
    first = (me * ROWS_HERE) // IMG
    edge = first * IMG
    inside = jnp.where(place < edge + IMG, 0, 1)
    return jnp.where((place >= edge) & (place < edge + 2 * IMG), inside, -1)


def chosen_columns(adapters, images, me, block):
    shape = (ROWS_HERE, LANES)
    place = (me + block - SIDE) * ROWS_HERE + lax.broadcasted_iota(jnp.int32, shape, 0)
    column = lax.broadcasted_iota(jnp.int32, shape, 1)
    first = (me * ROWS_HERE) // IMG
    second = jnp.minimum(first + 1, images - 1)
    adapter = jnp.where(slots_of(place, me) == 0, adapters[first], adapters[second])
    return ((column >= adapter * RANK) & (column < adapter * RANK + RANK)).astype(jnp.float32)


def same_image(me, keys_block, query_block):
    shape = (ROWS_HERE, ROWS_HERE)
    key = (me + keys_block - SIDE) * ROWS_HERE + lax.broadcasted_iota(jnp.int32, shape, 0)
    query = (me + query_block - SIDE) * ROWS_HERE + lax.broadcasted_iota(jnp.int32, shape, 1)
    one = slots_of(key, me)
    return jnp.where((one == slots_of(query, me)) & (one >= 0), 0.0, HIDE)


class Spread:
    def __init__(self, me, n, kinds, send, recv):
        self.me, self.n, self.kinds, self.send, self.recv = me, n, kinds, send, recv
        self.out = 2 * lax.rem(me, 2) - 1
        self.mate = me - self.out

    def wants(self, device, other):
        low, high = jnp.minimum(device, other), jnp.maximum(device, other)
        return (low >= 0) & (high < self.n) & shares_image(low, high)

    def copy(self, what, i, src, block, to):
        own, held = self.kinds[what]
        at = SIDE + block - to
        return remote(src, held.at[at], self.send.at[what, i], self.recv.at[what, at], to)

    def direct(self):
        for i, step in enumerate((self.out, 3 * self.out, -2 * self.out)):
            yield i, self.me, self.me + step
        yield 3, self.me, self.mate

    def relayed(self):
        for i, step in ((4, self.out), (5, 2 * self.out)):
            yield i, self.me + step, self.mate

    def each(self, which, act):
        for i, block, to in which:
            def go():
                for what, (own, held) in enumerate(self.kinds):
                    src = own if i < 4 else held.at[SIDE + block - self.me]
                    act(what, block, self.copy(what, i, src, block, to))
            pl.when(self.wants(block, to))(go)

    def start(self):
        self.each(self.direct(), lambda what, block, copy: copy.start())

    def landed(self, what, at):
        ref = self.kinds[what][1].at[at]
        pltpu.make_async_copy(ref, ref, self.recv.at[what, at]).wait()

    def onward(self):
        def act(what, block, copy):
            self.landed(what, SIDE + block - self.me)
            copy.start()
        self.each(self.relayed(), act)

    def arrive(self):
        for step, relay in ((1, True), (2, True), (3, False), (-1, False), (-2, False), (-3, False)):
            block = self.me + step * self.out
            wanted = self.wants(self.me, block)
            if relay:
                wanted = wanted & jnp.logical_not(self.wants(block, self.mate))

            def go():
                for what in range(len(self.kinds)):
                    self.landed(what, SIDE + step * self.out)
            pl.when(wanted)(go)

    def end(self):
        self.each(self.direct(), lambda what, block, copy: copy.wait_send())
        self.each(self.relayed(), lambda what, block, copy: copy.wait_send())


def forward_kernel(n, images, tokens, in_qkv, in_out, in_fc1, in_fc2, gain, bias, fbias, qkv_down, qkv_up, out_down, out_up,
                   ff_down, fc1_up, fc2_down, fc2_up, adapters,
                   *rest):
    local_gather = n == 4 * PLANE
    shards = (in_qkv, in_out, in_fc1, in_fc2)
    weights, rest = (rest[:4], rest[4:]) if local_gather else (shards, rest)
    w_qkv, w_out, w_fc1, w_fc2 = weights
    (output, normed1, low_qkv, qt_out, kv_out, lse, mixed_t, mixed, low_out, resid, normed2, low_fc1, pre, low_fc2,
     xs, v_qkv, v_out, v_fc1, v_fc2, tmp, shade, acc, act, v_pre, x_send, x_recv, w_sem, fc1_sem, fc2_sem, pre_sem, qt, kv, held_sem), rest = (
        rest[:33], rest[33:])
    me = lax.axis_index("dp")
    carrier = None
    if local_gather:
        carrier = Carrier(n // PLANE, shards, weights, (rest[:4],) + rest[4:8] + (rest[8:12],) + rest[12:])

    def advance(steps=1):
        if carrier:
            carrier.advance(steps)

    def ready(a):
        if carrier:
            carrier.ready(a)

    get_qkv = pltpu.make_async_copy(w_qkv, v_qkv, w_sem.at[0])
    get_out = pltpu.make_async_copy(w_out, v_out, w_sem.at[1])
    near = [k for k in range(-SIDE, SIDE + 1) if k]
    barrier = pltpu.get_barrier_semaphore()
    total = jnp.int32(0)
    for k in near:
        yes = met(me, n, k)
        total = total + yes.astype(jnp.int32)

        @pl.when(yes)
        def _():
            pl.semaphore_signal(barrier, inc=1, device_id=(me + k,), device_id_type=MESH)

    if carrier:
        total = total + carrier.greet(barrier)
    pl.semaphore_wait(barrier, total)
    if carrier:
        carrier.begin()
        advance(1)

    spread = Spread(me, n, [(tokens, xs)], x_send, x_recv)
    spread.start()
    xs[SIDE] = tokens[...]
    advance(1)
    spread.onward()
    begin, end = reach(me, n)
    for j in range(SPAN):
        shade[j] = same_image(me, j, SIDE)
    ready(0)
    get_qkv.start()
    advance(1)
    get_qkv.wait()
    m_qkv = v_qkv.reshape(3 * D, D)
    spread.arrive()

    def project(j, carry):
        center, inv = moments(xs[j].astype(jnp.float32))
        n1 = (center * inv * gain[0:1] + bias[0:1]).astype(jnp.bfloat16)
        select = chosen_columns(adapters, images, me, j)
        @pl.when(j == SIDE)
        def _():
            normed1[...] = n1
        for p in range(3):
            low = (select * mm(n1, qkv_down[p])).astype(jnp.bfloat16)
            @pl.when(j == SIDE)
            def _():
                low_qkv[p] = low
            for c in range(0, D, COLS):
                y = mm(n1, m_qkv[p * D:(p + 1) * D, c:c + COLS]) + mm(low, qkv_up[p, :, c:c + COLS])
                if p != 1:
                    y = y + bias[(1, 0, 2)[p]:(1, 0, 2)[p] + 1, c:c + COLS]
                (tmp, resid, tmp)[p][:, c:c + COLS] = y
            if p == 0:
                qt[j] = tmp[...].T.reshape(HEADS, HEAD_DIM, ROWS_HERE).astype(jnp.bfloat16)
            else:
                for h in range(HEADS):
                    kv[p - 1, j, h] = (tmp, resid, tmp)[p][:, h * HEAD_DIM:(h + 1) * HEAD_DIM].astype(jnp.bfloat16)
        return carry

    project(SIDE, 0)
    advance(1)
    lax.fori_loop(begin, jnp.int32(SIDE), project, 0)
    advance(2)
    lax.fori_loop(jnp.int32(SIDE + 1), end + 1, project, 0)
    advance(2)
    factor = HEAD_DIM ** (-0.5) * LOG2E

    def some_heads(group, carry):
        heads = [group * 4 + i for i in range(4)]
        queries = [qt[SIDE, h] for h in heads]

        def one_block(j, state):
            after = []
            for h, q, (top, total, o) in zip(heads, queries, state):
                s = mm(kv[0, j, h], q) * factor + shade[j]
                new = jnp.maximum(top, jnp.max(s, axis=0, keepdims=True))
                fade = jnp.exp2(top - new)
                p = jnp.exp2(s - new)
                total = total * fade + jnp.sum(p, axis=0, keepdims=True)
                o = o * fade + t_mm(kv[1, j, h], p.astype(jnp.bfloat16))
                after.append((new, total, o))
            return tuple(after)

        start = (jnp.full((1, ROWS_HERE), HIDE, jnp.float32), jnp.zeros((1, ROWS_HERE), jnp.float32),
                 jnp.zeros((HEAD_DIM, ROWS_HERE), jnp.float32))
        for h, (top, total, o) in zip(heads, lax.fori_loop(begin, end + 1, one_block, (start,) * 4)):
            mixed_t[h] = o / total
            lse[h] = top + jnp.log2(total)
        return carry

    for h in range(0, HEADS, 4):
        lax.fori_loop(h // 4, h // 4 + 1, some_heads, 0)
        advance(1)
    keep_qt = pltpu.make_async_copy(qt, qt_out, held_sem.at[0])
    keep_kv = pltpu.make_async_copy(kv, kv_out, held_sem.at[1])
    keep_qt.start()
    keep_kv.start()
    ready(1)
    get_out.start()
    att = mixed_t[...].reshape(D, ROWS_HERE).T.astype(jnp.bfloat16)
    mixed[...] = att
    select = chosen_columns(adapters, images, me, SIDE)
    get_out.wait()
    m_out = v_out.reshape(D, D)
    low = (select * mm(att, out_down[...])).astype(jnp.bfloat16)
    low_out[...] = low
    for c in range(0, D, COLS):
        s = slice(c, c + COLS)
        resid[:, s] = tokens[:, s].astype(jnp.float32) + mm(att, m_out[:, s]) + bias[3:4, s] + mm(low, out_up[:, s])
    center, inv = moments(resid[...])
    n2 = (center * inv * gain[1:2] + bias[4:5]).astype(jnp.bfloat16)
    normed2[...] = n2
    low1 = (select * mm(n2, ff_down[...])).astype(jnp.bfloat16)
    low_fc1[...] = low1

    def fetch1(i):
        slot = lax.rem(i, 2)
        cols = pl.ds(pl.multiple_of(i * STEP, STEP), STEP)
        return pltpu.make_async_copy(w_fc1.at[:, :, cols], v_fc1.at[slot], fc1_sem.at[slot])

    def fetch(i):
        slot = lax.rem(i, 2)
        rows = pl.ds(i * (STEP // 8), STEP // 8)
        return pltpu.make_async_copy(w_fc2.at[rows], v_fc2.at[slot], fc2_sem.at[slot])

    ready(2)
    fetch1(0).start()
    acc[...] = jnp.zeros_like(acc)

    def keep_pre(i):
        slot = lax.rem(i, 2)
        cols = pl.ds(pl.multiple_of(i * STEP, STEP), STEP)
        return pltpu.make_async_copy(v_pre.at[slot], pre.at[:, cols], pre_sem.at[slot])

    def feed(i, carry):
        @pl.when(i + 1 < FP // STEP)
        def _():
            fetch1(i + 1).start()
        fetch1(i).wait()
        s = pl.ds(pl.multiple_of(i * STEP, STEP), STEP)
        y = mm(n2, v_fc1[lax.rem(i, 2)].reshape(D, STEP)) + fbias[:, s] + mm(low1, fc1_up[:, s])
        slot = lax.rem(i, 2)

        @pl.when(i > 1)
        def _():
            keep_pre(i - 2).wait()
        v_pre[slot] = y
        keep_pre(i).start()
        a = (0.5 * y * (1.0 + jnp.tanh(0.7978845608028654 * (y + 0.044715 * y * y * y)))).astype(jnp.bfloat16)
        act[:, s] = a
        acc[...] += mm(a, fc2_down[s, :])
        return carry

    lax.fori_loop(0, FP // STEP, feed, 0)
    low2 = (select * acc[...]).astype(jnp.bfloat16)
    low_fc2[...] = low2
    for c in range(0, D, COLS):
        s = slice(c, c + COLS)
        tmp[:, s] = resid[:, s] + bias[5:6, s] + mm(low2, fc2_up[:, s])

    ready(3)
    fetch(0).start()

    def close(i, carry):
        @pl.when(i + 1 < FP // STEP)
        def _():
            fetch(i + 1).start()
        fetch(i).wait()
        s = pl.ds(pl.multiple_of(i * STEP, STEP), STEP)
        tmp[...] += mm(act[:, s], v_fc2[lax.rem(i, 2)].reshape(STEP, D))
        return carry

    lax.fori_loop(0, FP // STEP, close, 0)
    output[...] = tmp[...].astype(jnp.bfloat16)
    keep_pre(FP // STEP - 2).wait()
    keep_pre(FP // STEP - 1).wait()
    keep_qt.wait()
    keep_kv.wait()
    if carrier:
        carrier.end()
    spread.end()


def forward(n, tokens, qkv, out, fc1, fc2, gain, bias, fbias, qkv_down, qkv_up, out_down, out_up, ff_down, fc1_up,
            fc2_down, fc2_up, adapters):
    bf, f32 = jnp.bfloat16, jnp.float32
    r = ROWS_HERE
    local_gather = n == 4 * PLANE
    full = [((16 * TILES[a], 8, WIDE[a]), bf) for a in range(4)]
    outs = [
        ((r, D), bf), ((r, D), bf), ((3, r, LANES), bf), ((SPAN, HEADS, HEAD_DIM, r), bf), ((2, SPAN, HEADS, r, HEAD_DIM), bf),
        ((HEADS, 1, r), f32), ((HEADS, HEAD_DIM, r), f32), ((r, D), bf), ((r, LANES), bf), ((r, D), f32), ((r, D), bf),
        ((r, LANES), bf), ((r, FP), f32), ((r, LANES), bf),
    ]
    vmem = pl.BlockSpec(memory_space=pltpu.VMEM)
    away = pl.BlockSpec(memory_space=pl.ANY)
    dma = pltpu.SemaphoreType.DMA
    scratch = [
        pltpu.VMEM((SPAN, r, D), bf), pltpu.VMEM(*full[0]), pltpu.VMEM(*full[1]), pltpu.VMEM((2, D // 8, 8, STEP), bf),
        pltpu.VMEM((2, STEP // 8, 8, D), bf), pltpu.VMEM((r, D), f32), pltpu.VMEM((SPAN, r, r), f32), pltpu.VMEM((r, LANES), f32),
        pltpu.VMEM((r, FP), bf), pltpu.VMEM((2, r, STEP), f32), dma((1, 6)), dma((1, SPAN)), dma((2,)), dma((2,)), dma((2,)), dma((2,)),
        pltpu.VMEM(*outs[3]), pltpu.VMEM(*outs[4]), dma((2,)),
    ]
    if local_gather:
        layers = n // PLANE
        slots, pieces, chips = 2 * layers - 1, len(PIECES), 4 * layers
        scratch += [pltpu.VMEM((2,) + s, bf) for s in ((108, D), (36, D), (36, FP), (135, D))]
        scratch += [pltpu.VMEM((48, D), bf), pltpu.VMEM((48, D), bf), pltpu.VMEM((72, FP), f32), pltpu.VMEM((320, D), f32)]
        scratch += [pltpu.VMEM((TILES[a], 8, WIDE[a]), bf) for a in range(4)]
        scratch += [dma((4,)), dma((4,)), dma((2,)), dma((4,)), dma((pieces, 4 * slots, 2)), dma((pieces, 3 * slots, 2)),
                    dma((pieces, 4 * slots)), dma((pieces, chips)), dma((pieces, chips))]
    results = pl.pallas_call(
        functools.partial(forward_kernel, n, adapters.shape[0]),
        out_shape=[jax.ShapeDtypeStruct(*o) for o in (full if local_gather else []) + outs],
        in_specs=[vmem] + [away] * 4 + [vmem] * 11 + [pl.BlockSpec(memory_space=pltpu.SMEM)],
        out_specs=([away] * 4 if local_gather else []) + [vmem] * 3 + [away] * 2 + [vmem] * 7 + [away, vmem],
        scratch_shapes=scratch,
        compiler_params=pltpu.CompilerParams(collective_id=1, has_side_effects=True, vmem_limit_bytes=63 << 20),
        name="layer_forward",
    )(tokens, qkv, out, fc1, fc2, gain, bias, fbias, qkv_down, qkv_up, out_down, out_up, ff_down, fc1_up, fc2_down, fc2_up, adapters)
    return results if local_gather else (qkv, out, fc1, fc2, *results)


def shards_of(n, qkv, out, fc1, fc2):
    if n == 4 * PLANE:
        core = lax.rem(lax.axis_index("dp"), 2)
        half = jnp.zeros((D // 2,), fc2.dtype)
        fc2 = jnp.where(core == 0, jnp.concatenate([fc2, half]), jnp.concatenate([half, fc2]))
        return (qkv.reshape(108, D), out.reshape(36, D), jnp.pad(fc1.reshape(36, FF), ((0, 0), (0, FP - FF))), fc2.reshape(135, D))
    qkv, out, fc1, fc2 = (lax.all_gather(v, "dp", axis=0, tiled=True) for v in (qkv, out, fc1, fc2))
    return (
        qkv.reshape(3 * D // 8, 8, D),
        out.reshape(D // 8, 8, D),
        jnp.pad(fc1.reshape(D, FF), ((0, 0), (0, FP - FF))).reshape(D // 8, 8, FP),
        jnp.pad(fc2.reshape(FF, D), ((0, FP - FF), (0, 0))).reshape(FP // 8, 8, D),
    )
CUT = 256
CHIPS = 16
SLOTS = 2 * RANK
DOWN = (3 * D, D, D, FP)


def norm_back(center, inv, gain_row, grad):
    u = center * inv
    g = grad * gain_row
    return inv * (g - jnp.mean(g, axis=-1, keepdims=True) - u * jnp.mean(g * u, axis=-1, keepdims=True))


def backward_kernel(n, images, cotangent, tokens, w_qkv, w_out, w_fc1, w_fc2, gain, bias, qkv_down, qkv_up, out_down, out_up,
                    ff_down, fc1_up, fc2_down, fc2_up, adapters,
                    normed1, low_qkv, qt, kv, lse, mixed_t, mixed, low_out, resid, normed2, low_fc1, pre, low_fc2,
                    grad_tokens, *rest):
    reduce = n == 4 * PLANE
    count = 8 if reduce else len(DOWN) + 1
    results, rest = rest[:count], rest[count:]
    (v_qkv, v_out, v_fc1, v_fc2, v_kv, own_kv, wide, dres, acc, dat, stat, dq, dk, dv,
     send, recv, w_sem, fc1_sem, fc2_sem, kv_sem, v_pre, pre_sem), rest = rest[:22], rest[22:]
    if reduce:
        (ups, *downs), rest = rest[:5], rest[5:]
        packed, mate_in, going, coming, final, mate_sem, far_send, far_recv, last_sem = (
            rest[0:2], rest[2:6], rest[6:10], rest[10:14], rest[14:22], *rest[22:26])
    else:
        ups, *downs = results
    g_qkv, g_out, g_ff, g_fc2 = downs
    me = lax.axis_index("dp")
    core = lax.rem(me, 2)
    chip = me // 2
    mate = me + 1 - 2 * core
    own = pltpu.make_async_copy(kv.at[:, SIDE], own_kv, w_sem.at[0])
    own.start()
    get_out = pltpu.make_async_copy(w_out, v_out, w_sem.at[1])
    get_out.start()

    def fetch_qkv(t):
        rows = pl.ds(t * COLS, COLS)
        return pltpu.make_async_copy(w_qkv.at[rows, :], v_qkv.at[t % 2], w_sem.at[2 + t % 2])

    fetch_qkv(0).start()

    def fetch1(i):
        slot = lax.rem(i, 2)
        cols = pl.ds(pl.multiple_of(i * STEP, STEP), STEP)
        return pltpu.make_async_copy(w_fc1.at[:, cols], v_fc1.at[slot], fc1_sem.at[slot])

    def fetch2(i):
        slot = lax.rem(i, 2)
        rows = pl.ds(pl.multiple_of(i * STEP, STEP), STEP)
        return pltpu.make_async_copy(w_fc2.at[rows, :], v_fc2.at[slot], fc2_sem.at[slot])

    def fetch_pre(i):
        slot = lax.rem(i, 2)
        cols = pl.ds(pl.multiple_of(i * STEP, STEP), STEP)
        return pltpu.make_async_copy(pre.at[:, cols], v_pre.at[slot], pre_sem.at[slot])

    fetch1(0).start()
    fetch2(0).start()
    fetch_pre(0).start()
    near = [k for k in range(-SIDE, SIDE + 1) if k]
    barrier = pltpu.get_barrier_semaphore()
    total = jnp.int32(0)
    for k in near:
        yes = met(me, n, k)
        total = total + yes.astype(jnp.int32)

        @pl.when(yes)
        def _():
            pl.semaphore_signal(barrier, inc=1, device_id=(me + k,), device_id_type=MESH)

    if reduce:
        for k in range(1, CHIPS):
            pl.semaphore_signal(barrier, inc=1, device_id=(lax.rem(me + 2 * k, n),), device_id_type=MESH)
        pl.semaphore_signal(barrier, inc=1, device_id=(mate,), device_id_type=MESH)
        total = total + CHIPS
    begin, end = reach(me, n)
    bf = jnp.bfloat16
    select = chosen_columns(adapters, images, me, SIDE)

    def narrow(glow):
        if not reduce:
            return glow
        first = (chip * 2 * ROWS_HERE) // IMG
        shape = (LANES, SLOTS)
        lane = lax.broadcasted_iota(jnp.int32, shape, 1)
        late = lane >= RANK
        adapter = jnp.where(late, adapters[jnp.minimum(first + 1, images - 1)], adapters[first])
        pick = lax.broadcasted_iota(jnp.int32, shape, 0) == adapter * RANK + lane - jnp.where(late, RANK, 0)
        place = me * ROWS_HERE + lax.broadcasted_iota(jnp.int32, (ROWS_HERE, SLOTS), 0)
        mine = (place >= (first + 1) * IMG) == (lax.broadcasted_iota(jnp.int32, (ROWS_HERE, SLOTS), 1) >= RANK)
        return jnp.where(mine, mm(glow, pick.astype(bf)), 0.0).astype(bf)

    def put_up(at, value):
        ups[:, :, at] = value.reshape(CHIPS, 8, value.shape[-1])

    e = cotangent[...]
    put_up(slice(0, D), t_mm(low_fc2[...], e))
    glow2 = (select * mm_t(e, fc2_up[...])).astype(bf)
    acc[...] = jnp.zeros_like(acc)
    wide[...] = jnp.zeros_like(wide)
    low1 = low_fc1[...]
    glow2n = narrow(glow2)

    def feed(i, carry):
        @pl.when(i + 1 < FP // STEP)
        def _():
            fetch1(i + 1).start()
            fetch2(i + 1).start()
            fetch_pre(i + 1).start()
        fetch_pre(i).wait()
        fetch1(i).wait()
        fetch2(i).wait()
        slot = lax.rem(i, 2)
        s = pl.ds(pl.multiple_of(i * STEP, STEP), STEP)
        y = v_pre[slot]
        t = jnp.tanh(0.7978845608028654 * (y + 0.044715 * y * y * y))
        half = 0.5 * (1.0 + t)
        a = (y * half).astype(bf)
        slope = half + 0.5 * y * (1.0 - t * t) * (0.7978845608028654 * (1.0 + 3.0 * 0.044715 * y * y))
        g_fc2[:, s] = t_mm(glow2n, a)
        g = mm_t(e, v_fc2[slot]) + mm_t(glow2, fc2_down[s, :])
        gp = (g * slope).astype(bf)
        put_up(pl.ds(pl.multiple_of(D + i * STEP, LANES), STEP), t_mm(low1, gp))
        acc[...] += mm_t(gp, fc1_up[:, s])
        wide[...] += mm_t(gp, v_fc1[slot])
        return carry

    lax.fori_loop(0, FP // STEP, feed, 0)
    glow1 = (select * acc[...]).astype(bf)
    g_ff[...] = t_mm(narrow(glow1), normed2[...])
    center, inv = moments(resid[...])
    dres[...] = e.astype(jnp.float32) + norm_back(center, inv, gain[1:2], wide[...] + mm_t(glow1, ff_down[...]))
    gb = dres[...].astype(bf)
    put_up(slice(D + FP, 2 * D + FP), t_mm(low_out[...], gb))
    glow = (select * mm_t(gb, out_up[...])).astype(bf)
    g_out[...] = t_mm(narrow(glow), mixed[...])
    get_out.wait()
    for c in range(0, D, COLS):
        wide[:, c:c + COLS] = mm_t(gb, v_out[c:c + COLS, :]) + mm_t(glow, out_down[c:c + COLS, :])
    da = wide[...].T.reshape(HEADS, HEAD_DIM, ROWS_HERE).astype(bf)
    dat[SIDE] = da
    delta = jnp.sum(da.astype(jnp.float32) * mixed_t[...], axis=1, keepdims=True)
    stat[SIDE, 0] = lse[...].reshape(HEADS, ROWS_HERE)
    stat[SIDE, 1] = delta.reshape(HEADS, ROWS_HERE)

    pl.semaphore_wait(barrier, total)

    half = CHIPS // 2
    early = 2 * D + FP
    if reduce:
        upper = (ups.at[:, :, 0:early], ups.at[:, :, early:early + 3 * D])

        def source(i):
            return upper[i // 2] if i % 2 == 0 else packed[i // 2]

        def to_mate(i):
            return remote(source(i).at[pl.ds(half * (1 - core), half)], mate_in[i], mate_sem.at[0, i], mate_sem.at[1, i], mate)

        def to_chip(i, k):
            return remote(going[i].at[k], coming[i].at[chip], far_send.at[i, k], far_recv.at[i, chip], 2 * (half * core + k) + core)

        def pass_on(i):
            to_mate(i).wait_recv()

            def one(k, carry):
                going[i][k] = (source(i)[half * core + k] + mate_in[i][k]).astype(bf)

                @pl.when(half * core + k != chip)
                def _():
                    to_chip(i, k).start()
                return carry

            lax.fori_loop(0, half, one, 0)

            @pl.when(core == chip // half)
            def _():
                coming[i][chip] = going[i][chip - half * core]

        def gathered(i):
            for k in range(CHIPS):
                @pl.when(chip != k)
                def _():
                    pltpu.make_async_copy(coming[i].at[k], coming[i].at[k], far_recv.at[i, k]).wait()

        def add_up(i):
            gathered(i)
            return lax.fori_loop(1, CHIPS, lambda k, sofar: sofar + coming[i][k].astype(jnp.float32), coming[i][0].astype(jnp.float32))

        def add_down(i):
            gathered(i)
            shape = (LANES, SLOTS)
            lane = lax.broadcasted_iota(jnp.int32, shape, 1)
            late = lane >= RANK
            sofar = None
            for k in range(CHIPS):
                first = (k * 2 * ROWS_HERE) // IMG
                adapter = jnp.where(late, adapters[min(first + 1, images - 1)], adapters[first])
                pick = lax.broadcasted_iota(jnp.int32, shape, 0) == adapter * RANK + lane - jnp.where(late, RANK, 0)
                part = mm(pick.astype(bf), coming[i][k])
                sofar = part if k == 0 else sofar + part
            return sofar.T

        def flat_rows(ref, start, rows):
            for t in range(D // LANES):
                ref[pl.ds(start * (D // LANES) + t, rows.shape[0], stride=D // LANES), :] = rows[:, t * LANES:(t + 1) * LANES]

        def hand_out(which):
            for r in which:
                results[r][...] = final[r][core]
                remote(final[r].at[1 - core], results[r], last_sem.at[0, r], last_sem.at[1, r], mate).start()

        (f_qkv_down, f_qkv_up, f_out_down, f_out_up, f_ff_down, f_fc1_up, f_fc2_down, f_fc2_up) = final

        def finish_early():
            v = add_up(0)
            for q in range(2):
                flat_rows(f_fc2_up.at[q], 0, v[4 * q:4 * q + 4, 0:D])
                f_fc1_up[q] = v[4 * q:4 * q + 4, D:D + FP]
                flat_rows(f_out_up.at[q], 0, v[4 * q:4 * q + 4, D + FP:2 * D + FP])
            v = add_down(1)
            f_fc2_down[0] = v[0:135]
            turned = pltpu.roll(v, 64, axis=1)
            left = lax.broadcasted_iota(jnp.int32, (135, LANES), 1) < 64
            f_fc2_down[1] = jnp.where(left, turned[134:269], turned[135:270])
            for q in range(2):
                f_ff_down[q] = v[384 + 36 * q:420 + 36 * q]
                f_out_down[q] = v[512 + 36 * q:548 + 36 * q]
            hand_out((2, 3, 4, 5, 6, 7))

        def finish_late():
            v = add_up(2)
            flat_rows(f_qkv_up.at[0], 0, v[:, 0:D])
            flat_rows(f_qkv_up.at[0], 8, v[0:4, D:2 * D])
            flat_rows(f_qkv_up.at[1], 0, v[4:8, D:2 * D])
            flat_rows(f_qkv_up.at[1], 4, v[:, 2 * D:3 * D])
            v = add_down(3)
            for q in range(2):
                f_qkv_down[q] = v[108 * q:108 * q + 108]
            hand_out((0, 1))

        for m in range(CHIPS):
            packed[0][m, :, 0:269] = g_fc2[:, 269 * m:269 * m + 269]
            packed[0][m, :, 384:456] = g_ff[:, 72 * m:72 * m + 72]
            packed[0][m, :, 512:584] = g_out[:, 72 * m:72 * m + 72]
        to_mate(0).start()
        to_mate(1).start()

    spread = Spread(me, n, [(dat.at[SIDE], dat), (stat.at[SIDE], stat)], send, recv)
    spread.start()
    factor = HEAD_DIM ** (-0.5) * LOG2E

    parts = ROWS_HERE // CUT

    def stats(j, group):
        both = [stat[j, i, pl.ds(pl.multiple_of(group * TOGETHER, TOGETHER), TOGETHER), :] for i in (0, 1)]
        return [(both[0][i:i + 1], both[1][i:i + 1]) for i in range(TOGETHER)]

    def blocks(heads, keys, vals, q, d, st, shade, which):
        add_q, add_k, add_v = [], [], []
        for i in range(len(heads)):
            more_q, more_k, more_v = None, [], []
            for c in range(parts):
                rows = slice(c * CUT, (c + 1) * CUT)
                s = mm(keys[i][rows], q[i]) * factor + shade[rows]
                p = jnp.exp2(s - st[i][0])
                ds = (p * (mm(vals[i][rows], d[i]) - st[i][1])).astype(bf)
                if which != 2:
                    y = t_mm(keys[i][rows], ds)
                    more_q = y if more_q is None else more_q + y
                if which != 1:
                    more_k.append(mm_t(q[i], ds))
                    more_v.append(mm_t(d[i], p.astype(bf)))
            add_q.append(more_q)
            add_k.append(jnp.concatenate(more_k, axis=1) if more_k else None)
            add_v.append(jnp.concatenate(more_v, axis=1) if more_v else None)
        if which == 1:
            add_q = [a + dq[h] for h, a in zip(heads, add_q)]
        if which == 2:
            add_k = [a + dk[h] for h, a in zip(heads, add_k)]
            add_v = [a + dv[h] for h, a in zip(heads, add_v)]
        for i, h in enumerate(heads):
            if which != 2:
                dq[h] = add_q[i]
            if which != 1:
                dk[h] = add_k[i]
                dv[h] = add_v[i]

    own.wait()
    shade = same_image(me, SIDE, SIDE)

    def own_head(group, carry):
        heads = [group * TOGETHER + i for i in range(TOGETHER)]
        blocks(heads, [own_kv[0, h] for h in heads], [own_kv[1, h] for h in heads], [qt[SIDE, h] for h in heads],
               [dat[SIDE, h] for h in heads], stats(SIDE, group), shade, 0)
        return carry

    def get_kv(j):
        slot = lax.rem(j, 2)
        return pltpu.make_async_copy(kv.at[:, j], v_kv.at[slot], kv_sem.at[slot])

    get_kv(begin).start()
    lax.fori_loop(0, HEADS // TOGETHER, own_head, 0)
    spread.onward()

    def pass_one(j, carry):
        @pl.when(j < end)
        def _():
            get_kv(j + 1).start()
        get_kv(j).wait()

        @pl.when(j != SIDE)
        def _():
            shade = same_image(me, j, SIDE)
            slot = lax.rem(j, 2)

            def head(group, carry):
                heads = [group * TOGETHER + i for i in range(TOGETHER)]
                blocks(heads, [v_kv[slot, 0, h] for h in heads], [v_kv[slot, 1, h] for h in heads], [qt[SIDE, h] for h in heads],
                       [dat[SIDE, h] for h in heads], stats(SIDE, group), shade, 1)
                return carry

            lax.fori_loop(0, HEADS // TOGETHER, head, 0)
        return carry

    lax.fori_loop(begin, end + 1, pass_one, 0)
    spread.arrive()
    if reduce:
        pass_on(0)
        pass_on(1)

    def pass_two(j, carry):
        @pl.when(j != SIDE)
        def _():
            shade = same_image(me, SIDE, j)

            def head(group, carry):
                heads = [group * TOGETHER + i for i in range(TOGETHER)]
                blocks(heads, [own_kv[0, h] for h in heads], [own_kv[1, h] for h in heads], [qt[j, h] for h in heads],
                       [dat[j, h] for h in heads], stats(j, group), shade, 2)
                return carry

            lax.fori_loop(0, HEADS // TOGETHER, head, 0)
        return carry

    lax.fori_loop(begin, end + 1, pass_two, 0)
    n1 = normed1[...]
    grads = []
    for p, total_grad in enumerate((dq, dk, dv)):
        value = total_grad[...] * HEAD_DIM ** (-0.5) if p < 2 else total_grad[...]
        g = value.reshape(D, ROWS_HERE).T.astype(bf)
        rows = t_mm(low_qkv[p], g)
        for t in range(LANES // 8):
            at = p * (LANES // 8) + t
            ups[at // 3, :, early + at % 3 * D:early + at % 3 * D + D] = rows[8 * t:8 * t + 8]
        glow = (select * mm_t(g, qkv_up[p])).astype(bf)
        g_qkv[:, p * D:(p + 1) * D] = t_mm(narrow(glow), n1)
        grads.append((g, glow))
    if reduce:
        for m in range(CHIPS):
            packed[1][m, :, 0:216] = g_qkv[:, 216 * m:216 * m + 216]
        to_mate(2).start()
        to_mate(3).start()
    for p, (g, glow) in enumerate(grads):
        for c in range(0, D, COLS):
            s = slice(c, c + COLS)
            t = (p * D + c) // COLS
            if t + 1 < 3 * D // COLS:
                fetch_qkv(t + 1).start()
            fetch_qkv(t).wait()
            y = mm_t(g, v_qkv[t % 2]) + mm_t(glow, qkv_down[p, s, :])
            wide[:, s] = y if p == 0 else wide[:, s] + y
        if reduce and p == 0:
            pass_on(2)
            pass_on(3)
    center, inv = moments(tokens[...].astype(jnp.float32))
    grad_tokens[...] = (dres[...] + norm_back(center, inv, gain[0:1], wide[...])).astype(bf)
    spread.end()
    if reduce:
        reducer = core == chip // half

        @pl.when(reducer)
        def _():
            finish_early()
            finish_late()
            for r in range(8):
                remote(final[r].at[1 - core], results[r], last_sem.at[0, r], last_sem.at[1, r], mate).wait_send()

        @pl.when(jnp.logical_not(reducer))
        def _():
            for r in range(8):
                pltpu.make_async_copy(results[r], results[r], last_sem.at[1, r]).wait()

        for i in range(4):
            to_mate(i).wait_send()
            for k in range(half):
                @pl.when(half * core + k != chip)
                def _():
                    to_chip(i, k).wait_send()


def backward(n, cotangent, tokens, w_qkv, w_out, w_fc1, w_fc2, gain, bias, qkv_down, qkv_up, out_down, out_up, ff_down, fc1_up,
             fc2_down, fc2_up, adapters, saved):
    bf, f32 = jnp.bfloat16, jnp.float32
    r = ROWS_HERE
    reduce = n == 4 * PLANE
    deep = SLOTS if reduce else LANES
    partial = [((CHIPS, 8, 5 * D + FP), f32)] + [((deep, w), f32) for w in DOWN]
    shares = [(108, LANES), (108, LANES), (36, LANES), (36, LANES), (36, LANES), (4, FP), (135, LANES), (36, LANES)]
    outs = [((r, D), bf)] + ([(s, f32) for s in shares] if reduce else partial)
    more = []
    if reduce:
        half = CHIPS // 2
        up, down = (2 * D + FP, 3 * D), (640, 256)
        more = [pltpu.VMEM(*v) for v in partial]
        more += [pltpu.VMEM((CHIPS, SLOTS, w), f32) for w in down]
        for rows, kind in ((half, f32), (half, bf), (CHIPS, bf)):
            for w, v in zip(up, down):
                more += [pltpu.VMEM((rows, 8, w), kind), pltpu.VMEM((rows, SLOTS, v), kind)]
        more += [pltpu.VMEM((2,) + s, f32) for s in shares]
        dma = pltpu.SemaphoreType.DMA
        more += [dma((2, 4)), dma((4, half)), dma((4, CHIPS)), dma((2, 8))]
    vmem = pl.BlockSpec(memory_space=pltpu.VMEM)
    away = pl.BlockSpec(memory_space=pl.ANY)
    dma = pltpu.SemaphoreType.DMA
    heads = (HEADS, HEAD_DIM, r)
    return pl.pallas_call(
        functools.partial(backward_kernel, n, adapters.shape[0]),
        out_shape=[jax.ShapeDtypeStruct(*o) for o in outs],
        in_specs=[vmem] * 2 + [away] * 4 + [vmem] * 10 + [pl.BlockSpec(memory_space=pltpu.SMEM)] + [vmem] * 3 + [away] + [vmem] * 7 + [away, vmem],
        out_specs=[vmem] * len(outs),
        scratch_shapes=[
            pltpu.VMEM((2, COLS, D), bf), pltpu.VMEM((D, D), bf), pltpu.VMEM((2, D, STEP), bf), pltpu.VMEM((2, STEP, D), bf),
            pltpu.VMEM((2, 2, HEADS, r, HEAD_DIM), bf), pltpu.VMEM((2, HEADS, r, HEAD_DIM), bf),
            pltpu.VMEM((r, D), f32), pltpu.VMEM((r, D), f32), pltpu.VMEM((r, LANES), f32),
            pltpu.VMEM((SPAN,) + heads, bf), pltpu.VMEM((SPAN, 2, HEADS, r), f32),
            pltpu.VMEM(heads, f32), pltpu.VMEM(heads, f32), pltpu.VMEM(heads, f32),
            dma((2, 6)), dma((2, SPAN)), dma((4,)), dma((2,)), dma((2,)), dma((2,)),
            pltpu.VMEM((2, r, STEP), f32), dma((2,)),
        ] + more,
        compiler_params=pltpu.CompilerParams(collective_id=2, has_side_effects=True, vmem_limit_bytes=63 << 20),
        name="layer_backward",
    )(cotangent, tokens, w_qkv, w_out, w_fc1, w_fc2, gain, bias, qkv_down, qkv_up, out_down, out_up, ff_down, fc1_up, fc2_down,
      fc2_up, adapters, *saved)


def deliver_kernel(*refs):
    half = len(refs) // 2
    for i in range(half):
        refs[half + i][...] = refs[i][...]


def deliver(*arrays):
    vmem = pl.BlockSpec(memory_space=pltpu.VMEM)
    return pl.pallas_call(
        deliver_kernel,
        out_shape=[jax.ShapeDtypeStruct(a.shape, a.dtype) for a in arrays],
        in_specs=[vmem] * len(arrays),
        out_specs=[vmem] * len(arrays),
        name="deliver",
    )(*arrays)

def local(
    tokens,
    qkv_weights,
    out_weights,
    fc1_weights,
    fc2_weights,
    ln_gain,
    bias_model,
    first_feedforward_bias,
    qkv_down,
    qkv_up,
    out_down,
    out_up,
    first_feedforward_down,
    fc1_up,
    fc2_down,
    fc2_up,
    adapter_of_image,
    cotangent,
):
    n = lax.axis_size("dp")
    shards = shards_of(n, qkv_weights, out_weights, fc1_weights, fc2_weights)
    tail = FP - FF
    fbias = jnp.pad(first_feedforward_bias, (0, tail))[None]
    fc1_up = jnp.pad(fc1_up, ((0, 0), (0, tail)))
    fc2_down = jnp.pad(fc2_down, ((0, tail), (0, 0)))
    factors = (qkv_down, qkv_up, out_down, out_up, first_feedforward_down, fc1_up, fc2_down, fc2_up, adapter_of_image)
    results = forward(n, tokens, *shards, ln_gain, bias_model, fbias, *factors)
    weights, output, saved = results[:4], results[4], results[5:]
    weights = [w.reshape(-1, w.shape[-1]) for w in weights]
    grad_tokens, *grads = backward(n, cotangent, tokens, *weights, ln_gain, bias_model, *factors, saved)
    if n == 4 * PLANE:
        output, grad_tokens, *grads = deliver(output, grad_tokens, *grads)
        grads[5] = grads[5][:, :FF]
        summed = [g.reshape(-1) for g in grads]
        summed[6] = summed[6][: FF * LANES // n]
        return (output, grad_tokens, *summed)
    ups, g_qkv, g_out, g_ff, g_fc2 = grads
    early = 2 * D + FP
    g_up = ups[:, :, early:].reshape(CHIPS, 8, 3, D).transpose(0, 2, 1, 3)
    parts = (
        g_qkv.T,
        g_up,
        g_out.T,
        ups[:, :, D + FP : early],
        g_ff.T,
        ups[:, :, D : D + FF],
        g_fc2.T[:FF],
        ups[:, :, :D],
    )
    summed = [lax.psum_scatter(g.reshape(-1), "dp", scatter_dimension=0, tiled=True) for g in parts]
    return (output, grad_tokens, *summed)


def solution(mesh):
    return jax.shard_map(
        local,
        mesh=mesh,
        in_specs=(P("dp", None),) + (P("dp"),) * 4 + (P(),) * 12 + (P("dp", None),),
        out_specs=(P("dp", None),) * 2 + (P("dp"),) * 8,
        check_vma=False,
    )
```

```python
import functools

import jax
import jax.numpy as jnp
from jax import lax
from jax.experimental import pallas as pl
from jax.experimental.pallas import tpu as pltpu
from jax.sharding import PartitionSpec as P

D = 1152
HEADS = 16
HEAD_DIM = 72
FF = 4304
FP = 4352
IMG = 729
RANK = 16
ADAPTERS = 8
epsilon = 1e-06


MESH = pl.DeviceIdType.MESH
PLANE = 8
ROWS = (216, 72, 72, 272)
WIDE = (D, D, FP, D)
TILES = tuple(rows // 8 for rows in ROWS)
def remote(src, dst, send, recv, to):
    return pltpu.make_async_remote_copy(src_ref=src, dst_ref=dst, send_sem=send, recv_sem=recv, device_id=(to,), device_id_type=MESH)

PIECES = (
    (0, (0, 14), (14, 13)),
    (1, (0, 5), (5, 4)),
    (2, (0, 4), (4, 5)),
    (3, (0, 8), (17, 8)),
    (3, (8, 9), (25, 9)),
)
FLAT = (1, 4)
START = (0, 4, 5, 6, 7)


class Carrier:
    def __init__(self, layers, ins, outs, scratch):
        (self.held, self.ahead, self.ahead_in, self.wide, self.tall, self.blocks, self.pair_send, self.pair_recv, self.ahead_sem,
         self.own_sem, self.z_send, self.hop_send, self.pair_out, self.ici_recv, self.pair_in) = scratch
        self.layers, self.ins, self.outs = layers, ins, outs
        me = self.me = lax.axis_index("dp")
        self.core = lax.rem(me, 2)
        x = lax.rem(me // 2, 2)
        y = lax.rem(me // 4, 2)
        self.z = me // PLANE
        self.chip = me // 2
        self.chips = 4 * layers
        self.mate = me + 1 - 2 * self.core
        self.to_x = me + 2 - 4 * x
        self.to_y = me + 4 - 8 * y
        self.nxt = lax.rem(self.chip + 1, self.chips) * 2 + self.core
        self.prv = lax.rem(self.chip + self.chips - 1, self.chips) * 2 + self.core
        self.levels = [(d, s) for d in range(layers) for s in ((0,) if d == 0 else (-1, 1))]
        plane = lax.rem(self.chip, 4)
        self.corners = (plane, plane + 1 - 2 * x, plane + 2 - 4 * y, 3 - plane)
        self.made = -1
        last = layers + 1
        self.queue = sorted((START[p] + step, p, step) for p in range(len(PIECES)) for step in range(last + 1))

    def greet(self, barrier):
        spot = lax.rem(self.me, PLANE)
        up = lax.rem(self.z + 1, self.layers) * PLANE + spot
        down = lax.rem(self.z + self.layers - 1, self.layers) * PLANE + spot
        peers = (self.mate, self.to_x, self.to_y, self.nxt, self.prv, up, down)
        for peer in peers:
            pl.semaphore_signal(barrier, inc=1, device_id=(peer,), device_id_type=MESH)
        return len(peers)

    def pair(self, a):
        return remote(self.ins[a], self.held[a].at[self.core], self.pair_send.at[a], self.pair_recv.at[a], self.mate)

    def keep(self, a):
        return pltpu.make_async_copy(self.ins[a], self.held[a].at[self.core], self.own_sem.at[a])

    def lay(self, a):
        whole = self.outs[a].at[pl.ds(self.chip * TILES[a], TILES[a])]
        return pltpu.make_async_copy(self.blocks[a], whole, self.own_sem.at[a])

    def look_ahead(self):
        return remote(self.ahead, self.ahead_in, self.ahead_sem.at[0], self.ahead_sem.at[1], self.prv)

    def begin(self):
        for a in range(4):
            self.pair(a).start()
            self.keep(a).start()

    def build(self, a):
        self.keep(a).wait()
        remote(self.ins[a], self.held[a].at[1 - self.core], self.pair_send.at[a], self.pair_recv.at[a], self.mate).wait_recv()
        half, w, held = ROWS[a] // 2, WIDE[a], self.held[a]
        if a < 3:
            rows = self.wide if a == 2 else self.tall
            rows[0:half, 0:w] = held[0].astype(jnp.float32)
            rows[half:2 * half, 0:w] = held[1].astype(jnp.float32)
            self.blocks[a][...] = rows[0:2 * half, 0:w].reshape(half // 4, 8, w).astype(jnp.bfloat16)
        else:
            tall = self.tall
            tall[0:135, :] = held[0].astype(jnp.float32)
            tall[134:135, :] = tall[134:135, :] + held[1, 0:1].astype(jnp.float32)
            tall[135:269, :] = held[1].astype(jnp.float32)[1:135]
            self.ahead[...] = tall[0:48, :].astype(jnp.bfloat16)
            self.look_ahead().start()
            self.look_ahead().wait_recv()
            tall[269:317, :] = jnp.where(self.chip + 1 < self.chips, self.ahead_in[...].astype(jnp.float32), 0.0)
            moved = pltpu.roll(tall[...], 320 - 3 * self.chip, axis=0)[0:272]
            self.blocks[3][...] = moved.reshape(34, 8, D).astype(jnp.bfloat16)
        self.lay(a).start()

    def spot(self, p, m, c):
        a, *cuts = PIECES[p]
        at, rows = cuts[c]
        return self.outs[a].at[pl.ds(m * TILES[a] + at, rows)]

    def level(self, d, s, go):
        if d == 0:
            go()
        else:
            pl.when((self.z - d >= 0) if s < 0 else (self.z + d < self.layers))(go)

    def cut(self, p, c):
        a, *cuts = PIECES[p]
        return self.blocks[a].at[pl.ds(*cuts[c])]

    def hops(self, p, src, m, c, slot, ways):
        for w in ways:
            if w == 2:
                remote(src, self.spot(p, m, c), self.pair_out.at[p, slot], self.pair_in.at[p, m], self.mate).start()
            else:
                to = (self.to_x, self.to_y)[w]
                remote(src, self.spot(p, m, c), self.hop_send.at[p, slot, w], self.ici_recv.at[p, m], to).start()

    def along(self, p, src, m, c, slot, up):
        def go():
            to = self.me + PLANE if up else self.me - PLANE
            remote(src, self.spot(p, m, c), self.z_send.at[p, slot, up], self.ici_recv.at[p, m], to).start()
        pl.when((self.z + 1 < self.layers) if up else (self.z > 0))(go)

    def arrived(self, p, m, c):
        s = self.spot(p, m, c)
        pltpu.make_async_copy(s, s, self.ici_recv.at[p, m]).wait()
        return s

    def flat_event(self, p, step, c):
        count = len(self.levels)
        if step == 0:
            self.hops(p, self.cut(p, c), self.chip, c, 0, (0, 1))
        for k in range(4):
            for i, (d, s) in enumerate(self.levels):
                if (0, 1, 1, 2)[k] + d != step:
                    continue
                def go():
                    m = (self.z + s * d) * 4 + self.corners[k]
                    own = k == 0 and d == 0
                    src = self.cut(p, c) if own else self.arrived(p, m, c)
                    slot = k * count + i
                    ways = () if own else (2,)
                    if d == 0 and k == 1 + c:
                        ways = (1 - c, 2)
                    for up in (0, 1):
                        if d == 0 or up == int(s < 0):
                            self.along(p, src, m, c, slot, up)
                    self.hops(p, src, m, c, slot, ways)
                self.level(d, s, go)

    def event(self, p, step, c):
        if p in FLAT:
            return self.flat_event(p, step, c)
        count = len(self.levels)
        if step == 0:
            self.hops(p, self.cut(p, c), self.chip, c, 0, (0, 1))
            for up in (0, 1):
                self.along(p, self.cut(p, c), self.chip, c, 0, up)
        for i, (d, s) in enumerate(self.levels):
            zz = self.z + s * d
            if d >= 1 and d == step:
                def go():
                    m = zz * 4 + self.corners[0]
                    src = self.arrived(p, m, c)
                    self.along(p, src, m, c, i, int(s < 0))
                    self.hops(p, src, m, c, i, (0, 1, 2))
                self.level(d, s, go)
            if d + 1 == step:
                def go():
                    m = zz * 4 + self.corners[1]
                    self.hops(p, self.arrived(p, m, c), m, c, count + i, (1, 2) if c == 0 else (2,))
                    m = zz * 4 + self.corners[2]
                    self.hops(p, self.arrived(p, m, c), m, c, 2 * count + i, (2,) if c == 0 else (0, 2))
                self.level(d, s, go)
            if d + 2 == step:
                def go():
                    m = zz * 4 + self.corners[3]
                    self.hops(p, self.arrived(p, m, c), m, c, 3 * count + i, (2,))
                self.level(d, s, go)

    def either(self, act):
        for c in (0, 1):
            pl.when(self.core == c)(lambda: act(c))

    def advance(self, steps=1):
        for _ in range(min(steps, len(self.queue))):
            _, p, step = self.queue.pop(0)
            if step == 0 and PIECES[p][0] > self.made:
                self.made = PIECES[p][0]
                self.build(self.made)
            self.either(lambda c: self.event(p, step, c))

    def ready(self, a):
        while any(PIECES[p][0] == a for _, p, _ in self.queue):
            self.advance()

        def act(c):
            for p, piece in enumerate(PIECES):
                if piece[0] != a:
                    continue
                for k in range(4):
                    for d, s in self.levels:
                        if k or d:
                            def go():
                                m = (self.z + s * d) * 4 + self.corners[k]
                                q = self.spot(p, m, 1 - c)
                                pltpu.make_async_copy(q, q, self.pair_in.at[p, m]).wait()
                            self.level(d, s, go)
        self.either(act)
        self.lay(a).wait()

    def end(self):
        count = len(self.levels)

        def act(c):
            for p in range(len(PIECES)):
                src = self.cut(p, c)

                def sent(sem):
                    pltpu.make_async_copy(src, src, sem).wait()
                for i, (d, s) in enumerate(self.levels):
                    def flat():
                        if d == 0:
                            sent(self.hop_send.at[p, 0, 0])
                            sent(self.hop_send.at[p, 0, 1])
                            sent(self.hop_send.at[p, (1 + c) * count, 1 - c])
                        for k in range(4):
                            if k or d:
                                sent(self.pair_out.at[p, k * count + i])
                            for up in (0, 1):
                                if d == 0 or up == int(s < 0):
                                    inside = (self.z + 1 < self.layers) if up else (self.z > 0)
                                    pl.when(inside)(lambda: sent(self.z_send.at[p, k * count + i, up]))

                    if p in FLAT:
                        self.level(d, s, flat)
                        continue

                    def go():
                        sent(self.hop_send.at[p, i, 0])
                        sent(self.hop_send.at[p, i, 1])
                        if c == 0:
                            sent(self.hop_send.at[p, count + i, 1])
                        else:
                            sent(self.hop_send.at[p, 2 * count + i, 0])
                        for k in range(4):
                            if k or d:
                                sent(self.pair_out.at[p, k * count + i])
                        for up in (0, 1):
                            if d == 0 or up == int(s < 0):
                                pl.when((self.z + 1 < self.layers) if up else (self.z > 0))(lambda: sent(self.z_send.at[p, i, up]))
                    self.level(d, s, go)
        self.either(act)
        for a in range(4):
            self.pair(a).wait_send()
        self.look_ahead().wait_send()


ROWS_HERE = 256
SIDE = 3
SPAN = 2 * SIDE + 1
LANES = 128
COLS = 384
STEP = 256
TOGETHER = 8
LOG2E = 1.4426950408889634
HIDE = -1e30


def mm(left, right):
    return jnp.dot(left, right, preferred_element_type=jnp.float32)


def mm_t(left, right):
    return lax.dot_general(left, right, (((1,), (1,)), ((), ())), preferred_element_type=jnp.float32)


def t_mm(left, right):
    return lax.dot_general(left, right, (((0,), (0,)), ((), ())), preferred_element_type=jnp.float32)


def moments(rows):
    center = rows - jnp.mean(rows, axis=-1, keepdims=True)
    return center, lax.rsqrt(jnp.mean(center * center, axis=-1, keepdims=True) + epsilon)


def shares_image(low, high):
    return (low * ROWS_HERE + ROWS_HERE - 1) // IMG >= (high * ROWS_HERE) // IMG


def met(me, n, k):
    other = me + k
    inside = (other >= 0) & (other < n)
    low, high = (me, other) if k > 0 else (other, me)
    return inside & shares_image(low, high)


def reach(me, n):
    first = jnp.int32(SIDE)
    last = jnp.int32(SIDE)
    for k in range(1, SIDE + 1):
        first = first - met(me, n, -k).astype(jnp.int32)
        last = last + met(me, n, k).astype(jnp.int32)
    return first, last


def slots_of(place, me):
    first = (me * ROWS_HERE) // IMG
    edge = first * IMG
    inside = jnp.where(place < edge + IMG, 0, 1)
    return jnp.where((place >= edge) & (place < edge + 2 * IMG), inside, -1)


def chosen_columns(adapters, images, me, block):
    shape = (ROWS_HERE, LANES)
    place = (me + block - SIDE) * ROWS_HERE + lax.broadcasted_iota(jnp.int32, shape, 0)
    column = lax.broadcasted_iota(jnp.int32, shape, 1)
    first = (me * ROWS_HERE) // IMG
    second = jnp.minimum(first + 1, images - 1)
    adapter = jnp.where(slots_of(place, me) == 0, adapters[first], adapters[second])
    return ((column >= adapter * RANK) & (column < adapter * RANK + RANK)).astype(jnp.float32)


def same_image(me, keys_block, query_block):
    shape = (ROWS_HERE, ROWS_HERE)
    key = (me + keys_block - SIDE) * ROWS_HERE + lax.broadcasted_iota(jnp.int32, shape, 0)
    query = (me + query_block - SIDE) * ROWS_HERE + lax.broadcasted_iota(jnp.int32, shape, 1)
    one = slots_of(key, me)
    return jnp.where((one == slots_of(query, me)) & (one >= 0), 0.0, HIDE)


class Spread:
    def __init__(self, me, n, kinds, send, recv):
        self.me, self.n, self.kinds, self.send, self.recv = me, n, kinds, send, recv
        self.out = 2 * lax.rem(me, 2) - 1
        self.mate = me - self.out

    def wants(self, device, other):
        low, high = jnp.minimum(device, other), jnp.maximum(device, other)
        return (low >= 0) & (high < self.n) & shares_image(low, high)

    def copy(self, what, i, src, block, to):
        own, held = self.kinds[what]
        at = SIDE + block - to
        return remote(src, held.at[at], self.send.at[what, i], self.recv.at[what, at], to)

    def direct(self):
        for i, step in enumerate((self.out, 3 * self.out, -2 * self.out)):
            yield i, self.me, self.me + step
        yield 3, self.me, self.mate

    def relayed(self):
        for i, step in ((4, self.out), (5, 2 * self.out)):
            yield i, self.me + step, self.mate

    def each(self, which, act):
        for i, block, to in which:
            def go():
                for what, (own, held) in enumerate(self.kinds):
                    src = own if i < 4 else held.at[SIDE + block - self.me]
                    act(what, block, self.copy(what, i, src, block, to))
            pl.when(self.wants(block, to))(go)

    def start(self):
        self.each(self.direct(), lambda what, block, copy: copy.start())

    def landed(self, what, at):
        ref = self.kinds[what][1].at[at]
        pltpu.make_async_copy(ref, ref, self.recv.at[what, at]).wait()

    def onward(self):
        def act(what, block, copy):
            self.landed(what, SIDE + block - self.me)
            copy.start()
        self.each(self.relayed(), act)

    def arrive(self):
        for step, relay in ((1, True), (2, True), (3, False), (-1, False), (-2, False), (-3, False)):
            block = self.me + step * self.out
            wanted = self.wants(self.me, block)
            if relay:
                wanted = wanted & jnp.logical_not(self.wants(block, self.mate))

            def go():
                for what in range(len(self.kinds)):
                    self.landed(what, SIDE + step * self.out)
            pl.when(wanted)(go)

    def end(self):
        self.each(self.direct(), lambda what, block, copy: copy.wait_send())
        self.each(self.relayed(), lambda what, block, copy: copy.wait_send())


def forward_kernel(n, images, tokens, in_qkv, in_out, in_fc1, in_fc2, gain, bias, fbias, qkv_down, qkv_up, out_down, out_up,
                   ff_down, fc1_up, fc2_down, fc2_up, adapters,
                   *rest):
    local_gather = n == 4 * PLANE
    shards = (in_qkv, in_out, in_fc1, in_fc2)
    weights, rest = (rest[:4], rest[4:]) if local_gather else (shards, rest)
    w_qkv, w_out, w_fc1, w_fc2 = weights
    (output, normed1, low_qkv, qt_out, kv_out, lse, mixed_t, mixed, low_out, resid, normed2, low_fc1, pre, low_fc2,
     xs, v_qkv, v_out, v_fc1, v_fc2, tmp, shade, acc, act, v_pre, x_send, x_recv, w_sem, fc1_sem, fc2_sem, pre_sem, qt, kv, held_sem), rest = (
        rest[:33], rest[33:])
    me = lax.axis_index("dp")
    carrier = None
    if local_gather:
        carrier = Carrier(n // PLANE, shards, weights, (rest[:4],) + rest[4:8] + (rest[8:12],) + rest[12:])

    def advance(steps=1):
        if carrier:
            carrier.advance(steps)

    def ready(a):
        if carrier:
            carrier.ready(a)

    get_qkv = pltpu.make_async_copy(w_qkv, v_qkv, w_sem.at[0])
    get_out = pltpu.make_async_copy(w_out, v_out, w_sem.at[1])
    near = [k for k in range(-SIDE, SIDE + 1) if k]
    barrier = pltpu.get_barrier_semaphore()
    total = jnp.int32(0)
    for k in near:
        yes = met(me, n, k)
        total = total + yes.astype(jnp.int32)

        @pl.when(yes)
        def _():
            pl.semaphore_signal(barrier, inc=1, device_id=(me + k,), device_id_type=MESH)

    if carrier:
        total = total + carrier.greet(barrier)
    pl.semaphore_wait(barrier, total)
    if carrier:
        carrier.begin()
        advance(1)

    spread = Spread(me, n, [(tokens, xs)], x_send, x_recv)
    spread.start()
    xs[SIDE] = tokens[...]
    advance(1)
    spread.onward()
    begin, end = reach(me, n)
    for j in range(SPAN):
        shade[j] = same_image(me, j, SIDE)
    ready(0)
    get_qkv.start()
    advance(1)
    get_qkv.wait()
    m_qkv = v_qkv.reshape(3 * D, D)
    spread.arrive()

    def project(j, carry):
        center, inv = moments(xs[j].astype(jnp.float32))
        n1 = (center * inv * gain[0:1] + bias[0:1]).astype(jnp.bfloat16)
        select = chosen_columns(adapters, images, me, j)
        @pl.when(j == SIDE)
        def _():
            normed1[...] = n1
        for p in range(3):
            low = (select * mm(n1, qkv_down[p])).astype(jnp.bfloat16)
            @pl.when(j == SIDE)
            def _():
                low_qkv[p] = low
            for c in range(0, D, COLS):
                y = mm(n1, m_qkv[p * D:(p + 1) * D, c:c + COLS]) + mm(low, qkv_up[p, :, c:c + COLS])
                if p != 1:
                    y = y + bias[(1, 0, 2)[p]:(1, 0, 2)[p] + 1, c:c + COLS]
                (tmp, resid, tmp)[p][:, c:c + COLS] = y
            if p == 0:
                qt[j] = tmp[...].T.reshape(HEADS, HEAD_DIM, ROWS_HERE).astype(jnp.bfloat16)
            else:
                for h in range(HEADS):
                    kv[p - 1, j, h] = (tmp, resid, tmp)[p][:, h * HEAD_DIM:(h + 1) * HEAD_DIM].astype(jnp.bfloat16)
        return carry

    project(SIDE, 0)
    advance(1)
    lax.fori_loop(begin, jnp.int32(SIDE), project, 0)
    advance(1)
    lax.fori_loop(jnp.int32(SIDE + 1), end + 1, project, 0)
    advance(1)
    factor = HEAD_DIM ** (-0.5) * LOG2E

    def some_heads(group, carry):
        heads = [group * 4 + i for i in range(4)]
        queries = [qt[SIDE, h] for h in heads]

        def one_block(j, state):
            after = []
            for h, q, (top, total, o) in zip(heads, queries, state):
                s = mm(kv[0, j, h], q) * factor + shade[j]
                new = jnp.maximum(top, jnp.max(s, axis=0, keepdims=True))
                fade = jnp.exp2(top - new)
                p = jnp.exp2(s - new)
                total = total * fade + jnp.sum(p, axis=0, keepdims=True)
                o = o * fade + t_mm(kv[1, j, h], p.astype(jnp.bfloat16))
                after.append((new, total, o))
            return tuple(after)

        start = (jnp.full((1, ROWS_HERE), HIDE, jnp.float32), jnp.zeros((1, ROWS_HERE), jnp.float32),
                 jnp.zeros((HEAD_DIM, ROWS_HERE), jnp.float32))
        for h, (top, total, o) in zip(heads, lax.fori_loop(begin, end + 1, one_block, (start,) * 4)):
            mixed_t[h] = o / total
            lse[h] = top + jnp.log2(total)
        return carry

    for h in range(0, HEADS, 4):
        lax.fori_loop(h // 4, h // 4 + 1, some_heads, 0)
        advance(1)
    keep_qt = pltpu.make_async_copy(qt, qt_out, held_sem.at[0])
    keep_kv = pltpu.make_async_copy(kv, kv_out, held_sem.at[1])
    keep_qt.start()
    keep_kv.start()
    ready(1)
    get_out.start()
    att = mixed_t[...].reshape(D, ROWS_HERE).T.astype(jnp.bfloat16)
    mixed[...] = att
    select = chosen_columns(adapters, images, me, SIDE)
    get_out.wait()
    m_out = v_out.reshape(D, D)
    low = (select * mm(att, out_down[...])).astype(jnp.bfloat16)
    low_out[...] = low
    for c in range(0, D, COLS):
        s = slice(c, c + COLS)
        resid[:, s] = tokens[:, s].astype(jnp.float32) + mm(att, m_out[:, s]) + bias[3:4, s] + mm(low, out_up[:, s])
    center, inv = moments(resid[...])
    n2 = (center * inv * gain[1:2] + bias[4:5]).astype(jnp.bfloat16)
    normed2[...] = n2
    low1 = (select * mm(n2, ff_down[...])).astype(jnp.bfloat16)
    low_fc1[...] = low1

    def fetch1(i):
        slot = lax.rem(i, 2)
        cols = pl.ds(pl.multiple_of(i * STEP, STEP), STEP)
        return pltpu.make_async_copy(w_fc1.at[:, :, cols], v_fc1.at[slot], fc1_sem.at[slot])

    def fetch(i):
        slot = lax.rem(i, 2)
        rows = pl.ds(i * (STEP // 8), STEP // 8)
        return pltpu.make_async_copy(w_fc2.at[rows], v_fc2.at[slot], fc2_sem.at[slot])

    ready(2)
    fetch1(0).start()
    acc[...] = jnp.zeros_like(acc)

    def keep_pre(i):
        slot = lax.rem(i, 2)
        cols = pl.ds(pl.multiple_of(i * STEP, STEP), STEP)
        return pltpu.make_async_copy(v_pre.at[slot], pre.at[:, cols], pre_sem.at[slot])

    def feed(i, carry):
        @pl.when(i + 1 < FP // STEP)
        def _():
            fetch1(i + 1).start()
        fetch1(i).wait()
        s = pl.ds(pl.multiple_of(i * STEP, STEP), STEP)
        y = mm(n2, v_fc1[lax.rem(i, 2)].reshape(D, STEP)) + fbias[:, s] + mm(low1, fc1_up[:, s])
        slot = lax.rem(i, 2)

        @pl.when(i > 1)
        def _():
            keep_pre(i - 2).wait()
        v_pre[slot] = y
        keep_pre(i).start()
        a = (0.5 * y * (1.0 + jnp.tanh(0.7978845608028654 * (y + 0.044715 * y * y * y)))).astype(jnp.bfloat16)
        act[:, s] = a
        acc[...] += mm(a, fc2_down[s, :])
        return carry

    lax.fori_loop(0, FP // STEP, feed, 0)
    low2 = (select * acc[...]).astype(jnp.bfloat16)
    low_fc2[...] = low2
    for c in range(0, D, COLS):
        s = slice(c, c + COLS)
        tmp[:, s] = resid[:, s] + bias[5:6, s] + mm(low2, fc2_up[:, s])

    ready(3)
    fetch(0).start()

    def close(i, carry):
        @pl.when(i + 1 < FP // STEP)
        def _():
            fetch(i + 1).start()
        fetch(i).wait()
        s = pl.ds(pl.multiple_of(i * STEP, STEP), STEP)
        tmp[...] += mm(act[:, s], v_fc2[lax.rem(i, 2)].reshape(STEP, D))
        return carry

    lax.fori_loop(0, FP // STEP, close, 0)
    output[...] = tmp[...].astype(jnp.bfloat16)
    keep_pre(FP // STEP - 2).wait()
    keep_pre(FP // STEP - 1).wait()
    keep_qt.wait()
    keep_kv.wait()
    if carrier:
        carrier.end()
    spread.end()


def forward(n, tokens, qkv, out, fc1, fc2, gain, bias, fbias, qkv_down, qkv_up, out_down, out_up, ff_down, fc1_up,
            fc2_down, fc2_up, adapters):
    bf, f32 = jnp.bfloat16, jnp.float32
    r = ROWS_HERE
    local_gather = n == 4 * PLANE
    full = [((16 * TILES[a], 8, WIDE[a]), bf) for a in range(4)]
    outs = [
        ((r, D), bf), ((r, D), bf), ((3, r, LANES), bf), ((SPAN, HEADS, HEAD_DIM, r), bf), ((2, SPAN, HEADS, r, HEAD_DIM), bf),
        ((HEADS, 1, r), f32), ((HEADS, HEAD_DIM, r), f32), ((r, D), bf), ((r, LANES), bf), ((r, D), f32), ((r, D), bf),
        ((r, LANES), bf), ((r, FP), f32), ((r, LANES), bf),
    ]
    vmem = pl.BlockSpec(memory_space=pltpu.VMEM)
    away = pl.BlockSpec(memory_space=pl.ANY)
    dma = pltpu.SemaphoreType.DMA
    scratch = [
        pltpu.VMEM((SPAN, r, D), bf), pltpu.VMEM(*full[0]), pltpu.VMEM(*full[1]), pltpu.VMEM((2, D // 8, 8, STEP), bf),
        pltpu.VMEM((2, STEP // 8, 8, D), bf), pltpu.VMEM((r, D), f32), pltpu.VMEM((SPAN, r, r), f32), pltpu.VMEM((r, LANES), f32),
        pltpu.VMEM((r, FP), bf), pltpu.VMEM((2, r, STEP), f32), dma((1, 6)), dma((1, SPAN)), dma((2,)), dma((2,)), dma((2,)), dma((2,)),
        pltpu.VMEM(*outs[3]), pltpu.VMEM(*outs[4]), dma((2,)),
    ]
    if local_gather:
        layers = n // PLANE
        slots, pieces, chips = 2 * layers - 1, len(PIECES), 4 * layers
        scratch += [pltpu.VMEM((2,) + s, bf) for s in ((108, D), (36, D), (36, FP), (135, D))]
        scratch += [pltpu.VMEM((48, D), bf), pltpu.VMEM((48, D), bf), pltpu.VMEM((72, FP), f32), pltpu.VMEM((320, D), f32)]
        scratch += [pltpu.VMEM((TILES[a], 8, WIDE[a]), bf) for a in range(4)]
        scratch += [dma((4,)), dma((4,)), dma((2,)), dma((4,)), dma((pieces, 4 * slots, 2)), dma((pieces, 3 * slots, 2)),
                    dma((pieces, 4 * slots)), dma((pieces, chips)), dma((pieces, chips))]
    results = pl.pallas_call(
        functools.partial(forward_kernel, n, adapters.shape[0]),
        out_shape=[jax.ShapeDtypeStruct(*o) for o in (full if local_gather else []) + outs],
        in_specs=[vmem] + [away] * 4 + [vmem] * 11 + [pl.BlockSpec(memory_space=pltpu.SMEM)],
        out_specs=([away] * 4 if local_gather else []) + [vmem] * 3 + [away] * 2 + [vmem] * 7 + [away, vmem],
        scratch_shapes=scratch,
        compiler_params=pltpu.CompilerParams(collective_id=1, has_side_effects=True, vmem_limit_bytes=63 << 20),
        name="layer_forward",
    )(tokens, qkv, out, fc1, fc2, gain, bias, fbias, qkv_down, qkv_up, out_down, out_up, ff_down, fc1_up, fc2_down, fc2_up, adapters)
    return results if local_gather else (qkv, out, fc1, fc2, *results)


def shards_of(n, qkv, out, fc1, fc2):
    if n == 4 * PLANE:
        core = lax.rem(lax.axis_index("dp"), 2)
        half = jnp.zeros((D // 2,), fc2.dtype)
        fc2 = jnp.where(core == 0, jnp.concatenate([fc2, half]), jnp.concatenate([half, fc2]))
        return (qkv.reshape(108, D), out.reshape(36, D), jnp.pad(fc1.reshape(36, FF), ((0, 0), (0, FP - FF))), fc2.reshape(135, D))
    qkv, out, fc1, fc2 = (lax.all_gather(v, "dp", axis=0, tiled=True) for v in (qkv, out, fc1, fc2))
    return (
        qkv.reshape(3 * D // 8, 8, D),
        out.reshape(D // 8, 8, D),
        jnp.pad(fc1.reshape(D, FF), ((0, 0), (0, FP - FF))).reshape(D // 8, 8, FP),
        jnp.pad(fc2.reshape(FF, D), ((0, FP - FF), (0, 0))).reshape(FP // 8, 8, D),
    )
CUT = 256
CHIPS = 16
SLOTS = 2 * RANK
DOWN = (3 * D, D, D, FP)


def norm_back(center, inv, gain_row, grad):
    u = center * inv
    g = grad * gain_row
    return inv * (g - jnp.mean(g, axis=-1, keepdims=True) - u * jnp.mean(g * u, axis=-1, keepdims=True))


def backward_kernel(n, images, cotangent, tokens, w_qkv, w_out, w_fc1, w_fc2, gain, bias, qkv_down, qkv_up, out_down, out_up,
                    ff_down, fc1_up, fc2_down, fc2_up, adapters,
                    normed1, low_qkv, qt, kv, lse, mixed_t, mixed, low_out, resid, normed2, low_fc1, pre, low_fc2,
                    grad_tokens, *rest):
    reduce = n == 4 * PLANE
    count = 8 if reduce else len(DOWN) + 1
    results, rest = rest[:count], rest[count:]
    (v_qkv, v_out, v_fc1, v_fc2, v_kv, own_kv, wide, dres, acc, dat, stat, dq, dk, dv,
     send, recv, w_sem, fc1_sem, fc2_sem, kv_sem, v_pre, pre_sem), rest = rest[:22], rest[22:]
    if reduce:
        (ups, *downs), rest = rest[:5], rest[5:]
        packed, mate_in, going, coming, final, mate_sem, far_send, far_recv, last_sem = (
            rest[0:2], rest[2:6], rest[6:10], rest[10:14], rest[14:22], *rest[22:26])
    else:
        ups, *downs = results
    g_qkv, g_out, g_ff, g_fc2 = downs
    me = lax.axis_index("dp")
    core = lax.rem(me, 2)
    chip = me // 2
    mate = me + 1 - 2 * core
    own = pltpu.make_async_copy(kv.at[:, SIDE], own_kv, w_sem.at[0])
    own.start()
    get_out = pltpu.make_async_copy(w_out, v_out, w_sem.at[1])
    get_out.start()

    def fetch_qkv(t):
        rows = pl.ds(t * COLS, COLS)
        return pltpu.make_async_copy(w_qkv.at[rows, :], v_qkv.at[t % 2], w_sem.at[2 + t % 2])

    fetch_qkv(0).start()

    def fetch1(i):
        slot = lax.rem(i, 2)
        cols = pl.ds(pl.multiple_of(i * STEP, STEP), STEP)
        return pltpu.make_async_copy(w_fc1.at[:, cols], v_fc1.at[slot], fc1_sem.at[slot])

    def fetch2(i):
        slot = lax.rem(i, 2)
        rows = pl.ds(pl.multiple_of(i * STEP, STEP), STEP)
        return pltpu.make_async_copy(w_fc2.at[rows, :], v_fc2.at[slot], fc2_sem.at[slot])

    def fetch_pre(i):
        slot = lax.rem(i, 2)
        cols = pl.ds(pl.multiple_of(i * STEP, STEP), STEP)
        return pltpu.make_async_copy(pre.at[:, cols], v_pre.at[slot], pre_sem.at[slot])

    fetch1(0).start()
    fetch2(0).start()
    fetch_pre(0).start()
    near = [k for k in range(-SIDE, SIDE + 1) if k]
    barrier = pltpu.get_barrier_semaphore()
    total = jnp.int32(0)
    for k in near:
        yes = met(me, n, k)
        total = total + yes.astype(jnp.int32)

        @pl.when(yes)
        def _():
            pl.semaphore_signal(barrier, inc=1, device_id=(me + k,), device_id_type=MESH)

    if reduce:
        for k in range(1, CHIPS):
            pl.semaphore_signal(barrier, inc=1, device_id=(lax.rem(me + 2 * k, n),), device_id_type=MESH)
        pl.semaphore_signal(barrier, inc=1, device_id=(mate,), device_id_type=MESH)
        total = total + CHIPS
    begin, end = reach(me, n)
    bf = jnp.bfloat16
    select = chosen_columns(adapters, images, me, SIDE)

    def narrow(glow):
        if not reduce:
            return glow
        first = (chip * 2 * ROWS_HERE) // IMG
        shape = (LANES, SLOTS)
        lane = lax.broadcasted_iota(jnp.int32, shape, 1)
        late = lane >= RANK
        adapter = jnp.where(late, adapters[jnp.minimum(first + 1, images - 1)], adapters[first])
        pick = lax.broadcasted_iota(jnp.int32, shape, 0) == adapter * RANK + lane - jnp.where(late, RANK, 0)
        place = me * ROWS_HERE + lax.broadcasted_iota(jnp.int32, (ROWS_HERE, SLOTS), 0)
        mine = (place >= (first + 1) * IMG) == (lax.broadcasted_iota(jnp.int32, (ROWS_HERE, SLOTS), 1) >= RANK)
        return jnp.where(mine, mm(glow, pick.astype(bf)), 0.0).astype(bf)

    def put_up(at, value):
        ups[:, :, at] = value.reshape(CHIPS, 8, value.shape[-1])

    e = cotangent[...]
    put_up(slice(0, D), t_mm(low_fc2[...], e))
    glow2 = (select * mm_t(e, fc2_up[...])).astype(bf)
    acc[...] = jnp.zeros_like(acc)
    wide[...] = jnp.zeros_like(wide)
    low1 = low_fc1[...]
    glow2n = narrow(glow2)

    def feed(i, carry):
        @pl.when(i + 1 < FP // STEP)
        def _():
            fetch1(i + 1).start()
            fetch2(i + 1).start()
            fetch_pre(i + 1).start()
        fetch_pre(i).wait()
        fetch1(i).wait()
        fetch2(i).wait()
        slot = lax.rem(i, 2)
        s = pl.ds(pl.multiple_of(i * STEP, STEP), STEP)
        y = v_pre[slot]
        t = jnp.tanh(0.7978845608028654 * (y + 0.044715 * y * y * y))
        half = 0.5 * (1.0 + t)
        a = (y * half).astype(bf)
        slope = half + 0.5 * y * (1.0 - t * t) * (0.7978845608028654 * (1.0 + 3.0 * 0.044715 * y * y))
        g_fc2[:, s] = t_mm(glow2n, a)
        g = mm_t(e, v_fc2[slot]) + mm_t(glow2, fc2_down[s, :])
        gp = (g * slope).astype(bf)
        put_up(pl.ds(pl.multiple_of(D + i * STEP, LANES), STEP), t_mm(low1, gp))
        acc[...] += mm_t(gp, fc1_up[:, s])
        wide[...] += mm_t(gp, v_fc1[slot])
        return carry

    lax.fori_loop(0, FP // STEP, feed, 0)
    glow1 = (select * acc[...]).astype(bf)
    g_ff[...] = t_mm(narrow(glow1), normed2[...])
    center, inv = moments(resid[...])
    dres[...] = e.astype(jnp.float32) + norm_back(center, inv, gain[1:2], wide[...] + mm_t(glow1, ff_down[...]))
    gb = dres[...].astype(bf)
    put_up(slice(D + FP, 2 * D + FP), t_mm(low_out[...], gb))
    glow = (select * mm_t(gb, out_up[...])).astype(bf)
    g_out[...] = t_mm(narrow(glow), mixed[...])
    get_out.wait()
    for c in range(0, D, COLS):
        wide[:, c:c + COLS] = mm_t(gb, v_out[c:c + COLS, :]) + mm_t(glow, out_down[c:c + COLS, :])
    da = wide[...].T.reshape(HEADS, HEAD_DIM, ROWS_HERE).astype(bf)
    dat[SIDE] = da
    delta = jnp.sum(da.astype(jnp.float32) * mixed_t[...], axis=1, keepdims=True)
    stat[SIDE, 0] = lse[...].reshape(HEADS, ROWS_HERE)
    stat[SIDE, 1] = delta.reshape(HEADS, ROWS_HERE)

    pl.semaphore_wait(barrier, total)

    half = CHIPS // 2
    early = 2 * D + FP
    if reduce:
        upper = (ups.at[:, :, 0:early], ups.at[:, :, early:early + 3 * D])

        def source(i):
            return upper[i // 2] if i % 2 == 0 else packed[i // 2]

        def to_mate(i):
            return remote(source(i).at[pl.ds(half * (1 - core), half)], mate_in[i], mate_sem.at[0, i], mate_sem.at[1, i], mate)

        def to_chip(i, k):
            return remote(going[i].at[k], coming[i].at[chip], far_send.at[i, k], far_recv.at[i, chip], 2 * (half * core + k) + core)

        def pass_on(i):
            to_mate(i).wait_recv()

            def one(k, carry):
                going[i][k] = (source(i)[half * core + k] + mate_in[i][k]).astype(bf)

                @pl.when(half * core + k != chip)
                def _():
                    to_chip(i, k).start()
                return carry

            lax.fori_loop(0, half, one, 0)

            @pl.when(core == chip // half)
            def _():
                coming[i][chip] = going[i][chip - half * core]

        def gathered(i):
            for k in range(CHIPS):
                @pl.when(chip != k)
                def _():
                    pltpu.make_async_copy(coming[i].at[k], coming[i].at[k], far_recv.at[i, k]).wait()

        def add_up(i):
            gathered(i)
            return lax.fori_loop(1, CHIPS, lambda k, sofar: sofar + coming[i][k].astype(jnp.float32), coming[i][0].astype(jnp.float32))

        def add_down(i):
            gathered(i)
            shape = (LANES, SLOTS)
            lane = lax.broadcasted_iota(jnp.int32, shape, 1)
            late = lane >= RANK
            sofar = None
            for k in range(CHIPS):
                first = (k * 2 * ROWS_HERE) // IMG
                adapter = jnp.where(late, adapters[min(first + 1, images - 1)], adapters[first])
                pick = lax.broadcasted_iota(jnp.int32, shape, 0) == adapter * RANK + lane - jnp.where(late, RANK, 0)
                part = mm(pick.astype(bf), coming[i][k])
                sofar = part if k == 0 else sofar + part
            return sofar.T

        def flat_rows(ref, start, rows):
            for t in range(D // LANES):
                ref[pl.ds(start * (D // LANES) + t, rows.shape[0], stride=D // LANES), :] = rows[:, t * LANES:(t + 1) * LANES]

        def hand_out(which):
            for r in which:
                results[r][...] = final[r][core]
                remote(final[r].at[1 - core], results[r], last_sem.at[0, r], last_sem.at[1, r], mate).start()

        (f_qkv_down, f_qkv_up, f_out_down, f_out_up, f_ff_down, f_fc1_up, f_fc2_down, f_fc2_up) = final

        def finish_early():
            v = add_up(0)
            for q in range(2):
                flat_rows(f_fc2_up.at[q], 0, v[4 * q:4 * q + 4, 0:D])
                f_fc1_up[q] = v[4 * q:4 * q + 4, D:D + FP]
                flat_rows(f_out_up.at[q], 0, v[4 * q:4 * q + 4, D + FP:2 * D + FP])
            v = add_down(1)
            f_fc2_down[0] = v[0:135]
            turned = pltpu.roll(v, 64, axis=1)
            left = lax.broadcasted_iota(jnp.int32, (135, LANES), 1) < 64
            f_fc2_down[1] = jnp.where(left, turned[134:269], turned[135:270])
            for q in range(2):
                f_ff_down[q] = v[384 + 36 * q:420 + 36 * q]
                f_out_down[q] = v[512 + 36 * q:548 + 36 * q]
            hand_out((2, 3, 4, 5, 6, 7))

        def finish_late():
            v = add_up(2)
            flat_rows(f_qkv_up.at[0], 0, v[:, 0:D])
            flat_rows(f_qkv_up.at[0], 8, v[0:4, D:2 * D])
            flat_rows(f_qkv_up.at[1], 0, v[4:8, D:2 * D])
            flat_rows(f_qkv_up.at[1], 4, v[:, 2 * D:3 * D])
            v = add_down(3)
            for q in range(2):
                f_qkv_down[q] = v[108 * q:108 * q + 108]
            hand_out((0, 1))

        for m in range(CHIPS):
            packed[0][m, :, 0:269] = g_fc2[:, 269 * m:269 * m + 269]
            packed[0][m, :, 384:456] = g_ff[:, 72 * m:72 * m + 72]
            packed[0][m, :, 512:584] = g_out[:, 72 * m:72 * m + 72]
        to_mate(0).start()
        to_mate(1).start()

    spread = Spread(me, n, [(dat.at[SIDE], dat), (stat.at[SIDE], stat)], send, recv)
    spread.start()
    factor = HEAD_DIM ** (-0.5) * LOG2E

    parts = ROWS_HERE // CUT

    def stats(j, group):
        both = [stat[j, i, pl.ds(pl.multiple_of(group * TOGETHER, TOGETHER), TOGETHER), :] for i in (0, 1)]
        return [(both[0][i:i + 1], both[1][i:i + 1]) for i in range(TOGETHER)]

    def blocks(heads, keys, vals, q, d, st, shade, which):
        add_q, add_k, add_v = [], [], []
        for i in range(len(heads)):
            more_q, more_k, more_v = None, [], []
            for c in range(parts):
                rows = slice(c * CUT, (c + 1) * CUT)
                s = mm(keys[i][rows], q[i]) * factor + shade[rows]
                p = jnp.exp2(s - st[i][0])
                ds = (p * (mm(vals[i][rows], d[i]) - st[i][1])).astype(bf)
                if which != 2:
                    y = t_mm(keys[i][rows], ds)
                    more_q = y if more_q is None else more_q + y
                if which != 1:
                    more_k.append(mm_t(q[i], ds))
                    more_v.append(mm_t(d[i], p.astype(bf)))
            add_q.append(more_q)
            add_k.append(jnp.concatenate(more_k, axis=1) if more_k else None)
            add_v.append(jnp.concatenate(more_v, axis=1) if more_v else None)
        if which == 1:
            add_q = [a + dq[h] for h, a in zip(heads, add_q)]
        if which == 2:
            add_k = [a + dk[h] for h, a in zip(heads, add_k)]
            add_v = [a + dv[h] for h, a in zip(heads, add_v)]
        for i, h in enumerate(heads):
            if which != 2:
                dq[h] = add_q[i]
            if which != 1:
                dk[h] = add_k[i]
                dv[h] = add_v[i]

    own.wait()
    shade = same_image(me, SIDE, SIDE)

    def own_head(group, carry):
        heads = [group * TOGETHER + i for i in range(TOGETHER)]
        blocks(heads, [own_kv[0, h] for h in heads], [own_kv[1, h] for h in heads], [qt[SIDE, h] for h in heads],
               [dat[SIDE, h] for h in heads], stats(SIDE, group), shade, 0)
        return carry

    def get_kv(j):
        slot = lax.rem(j, 2)
        return pltpu.make_async_copy(kv.at[:, j], v_kv.at[slot], kv_sem.at[slot])

    get_kv(begin).start()
    lax.fori_loop(0, HEADS // TOGETHER, own_head, 0)
    spread.onward()

    def pass_one(j, carry):
        @pl.when(j < end)
        def _():
            get_kv(j + 1).start()
        get_kv(j).wait()

        @pl.when(j != SIDE)
        def _():
            shade = same_image(me, j, SIDE)
            slot = lax.rem(j, 2)

            def head(group, carry):
                heads = [group * TOGETHER + i for i in range(TOGETHER)]
                blocks(heads, [v_kv[slot, 0, h] for h in heads], [v_kv[slot, 1, h] for h in heads], [qt[SIDE, h] for h in heads],
                       [dat[SIDE, h] for h in heads], stats(SIDE, group), shade, 1)
                return carry

            lax.fori_loop(0, HEADS // TOGETHER, head, 0)
        return carry

    lax.fori_loop(begin, end + 1, pass_one, 0)
    spread.arrive()
    if reduce:
        pass_on(0)
        pass_on(1)

    def pass_two(j, carry):
        @pl.when(j != SIDE)
        def _():
            shade = same_image(me, SIDE, j)

            def head(group, carry):
                heads = [group * TOGETHER + i for i in range(TOGETHER)]
                blocks(heads, [own_kv[0, h] for h in heads], [own_kv[1, h] for h in heads], [qt[j, h] for h in heads],
                       [dat[j, h] for h in heads], stats(j, group), shade, 2)
                return carry

            lax.fori_loop(0, HEADS // TOGETHER, head, 0)
        return carry

    lax.fori_loop(begin, end + 1, pass_two, 0)
    n1 = normed1[...]
    grads = []
    for p, total_grad in enumerate((dq, dk, dv)):
        value = total_grad[...] * HEAD_DIM ** (-0.5) if p < 2 else total_grad[...]
        g = value.reshape(D, ROWS_HERE).T.astype(bf)
        rows = t_mm(low_qkv[p], g)
        for t in range(LANES // 8):
            at = p * (LANES // 8) + t
            ups[at // 3, :, early + at % 3 * D:early + at % 3 * D + D] = rows[8 * t:8 * t + 8]
        glow = (select * mm_t(g, qkv_up[p])).astype(bf)
        g_qkv[:, p * D:(p + 1) * D] = t_mm(narrow(glow), n1)
        grads.append((g, glow))
    if reduce:
        for m in range(CHIPS):
            packed[1][m, :, 0:216] = g_qkv[:, 216 * m:216 * m + 216]
        to_mate(2).start()
        to_mate(3).start()
    for p, (g, glow) in enumerate(grads):
        for c in range(0, D, COLS):
            s = slice(c, c + COLS)
            t = (p * D + c) // COLS
            if t + 1 < 3 * D // COLS:
                fetch_qkv(t + 1).start()
            fetch_qkv(t).wait()
            y = mm_t(g, v_qkv[t % 2]) + mm_t(glow, qkv_down[p, s, :])
            wide[:, s] = y if p == 0 else wide[:, s] + y
        if reduce and p == 0:
            pass_on(2)
            pass_on(3)
    center, inv = moments(tokens[...].astype(jnp.float32))
    grad_tokens[...] = (dres[...] + norm_back(center, inv, gain[0:1], wide[...])).astype(bf)
    spread.end()
    if reduce:
        reducer = core == chip // half

        @pl.when(reducer)
        def _():
            finish_early()
            finish_late()
            for r in range(8):
                remote(final[r].at[1 - core], results[r], last_sem.at[0, r], last_sem.at[1, r], mate).wait_send()

        @pl.when(jnp.logical_not(reducer))
        def _():
            for r in range(8):
                pltpu.make_async_copy(results[r], results[r], last_sem.at[1, r]).wait()

        for i in range(4):
            to_mate(i).wait_send()
            for k in range(half):
                @pl.when(half * core + k != chip)
                def _():
                    to_chip(i, k).wait_send()


def backward(n, cotangent, tokens, w_qkv, w_out, w_fc1, w_fc2, gain, bias, qkv_down, qkv_up, out_down, out_up, ff_down, fc1_up,
             fc2_down, fc2_up, adapters, saved):
    bf, f32 = jnp.bfloat16, jnp.float32
    r = ROWS_HERE
    reduce = n == 4 * PLANE
    deep = SLOTS if reduce else LANES
    partial = [((CHIPS, 8, 5 * D + FP), f32)] + [((deep, w), f32) for w in DOWN]
    shares = [(108, LANES), (108, LANES), (36, LANES), (36, LANES), (36, LANES), (4, FP), (135, LANES), (36, LANES)]
    outs = [((r, D), bf)] + ([(s, f32) for s in shares] if reduce else partial)
    more = []
    if reduce:
        half = CHIPS // 2
        up, down = (2 * D + FP, 3 * D), (640, 256)
        more = [pltpu.VMEM(*v) for v in partial]
        more += [pltpu.VMEM((CHIPS, SLOTS, w), f32) for w in down]
        for rows, kind in ((half, f32), (half, bf), (CHIPS, bf)):
            for w, v in zip(up, down):
                more += [pltpu.VMEM((rows, 8, w), kind), pltpu.VMEM((rows, SLOTS, v), kind)]
        more += [pltpu.VMEM((2,) + s, f32) for s in shares]
        dma = pltpu.SemaphoreType.DMA
        more += [dma((2, 4)), dma((4, half)), dma((4, CHIPS)), dma((2, 8))]
    vmem = pl.BlockSpec(memory_space=pltpu.VMEM)
    away = pl.BlockSpec(memory_space=pl.ANY)
    dma = pltpu.SemaphoreType.DMA
    heads = (HEADS, HEAD_DIM, r)
    return pl.pallas_call(
        functools.partial(backward_kernel, n, adapters.shape[0]),
        out_shape=[jax.ShapeDtypeStruct(*o) for o in outs],
        in_specs=[vmem] * 2 + [away] * 4 + [vmem] * 10 + [pl.BlockSpec(memory_space=pltpu.SMEM)] + [vmem] * 3 + [away] + [vmem] * 7 + [away, vmem],
        out_specs=[vmem] * len(outs),
        scratch_shapes=[
            pltpu.VMEM((2, COLS, D), bf), pltpu.VMEM((D, D), bf), pltpu.VMEM((2, D, STEP), bf), pltpu.VMEM((2, STEP, D), bf),
            pltpu.VMEM((2, 2, HEADS, r, HEAD_DIM), bf), pltpu.VMEM((2, HEADS, r, HEAD_DIM), bf),
            pltpu.VMEM((r, D), f32), pltpu.VMEM((r, D), f32), pltpu.VMEM((r, LANES), f32),
            pltpu.VMEM((SPAN,) + heads, bf), pltpu.VMEM((SPAN, 2, HEADS, r), f32),
            pltpu.VMEM(heads, f32), pltpu.VMEM(heads, f32), pltpu.VMEM(heads, f32),
            dma((2, 6)), dma((2, SPAN)), dma((4,)), dma((2,)), dma((2,)), dma((2,)),
            pltpu.VMEM((2, r, STEP), f32), dma((2,)),
        ] + more,
        compiler_params=pltpu.CompilerParams(collective_id=2, has_side_effects=True, vmem_limit_bytes=63 << 20),
        name="layer_backward",
    )(cotangent, tokens, w_qkv, w_out, w_fc1, w_fc2, gain, bias, qkv_down, qkv_up, out_down, out_up, ff_down, fc1_up, fc2_down,
      fc2_up, adapters, *saved)


def deliver_kernel(*refs):
    half = len(refs) // 2
    for i in range(half):
        refs[half + i][...] = refs[i][...]


def deliver(*arrays):
    vmem = pl.BlockSpec(memory_space=pltpu.VMEM)
    return pl.pallas_call(
        deliver_kernel,
        out_shape=[jax.ShapeDtypeStruct(a.shape, a.dtype) for a in arrays],
        in_specs=[vmem] * len(arrays),
        out_specs=[vmem] * len(arrays),
        name="deliver",
    )(*arrays)

def local(
    tokens,
    qkv_weights,
    out_weights,
    fc1_weights,
    fc2_weights,
    ln_gain,
    bias_model,
    first_feedforward_bias,
    qkv_down,
    qkv_up,
    out_down,
    out_up,
    first_feedforward_down,
    fc1_up,
    fc2_down,
    fc2_up,
    adapter_of_image,
    cotangent,
):
    n = lax.axis_size("dp")
    shards = shards_of(n, qkv_weights, out_weights, fc1_weights, fc2_weights)
    tail = FP - FF
    fbias = jnp.pad(first_feedforward_bias, (0, tail))[None]
    fc1_up = jnp.pad(fc1_up, ((0, 0), (0, tail)))
    fc2_down = jnp.pad(fc2_down, ((0, tail), (0, 0)))
    factors = (qkv_down, qkv_up, out_down, out_up, first_feedforward_down, fc1_up, fc2_down, fc2_up, adapter_of_image)
    results = forward(n, tokens, *shards, ln_gain, bias_model, fbias, *factors)
    weights, output, saved = results[:4], results[4], results[5:]
    weights = [w.reshape(-1, w.shape[-1]) for w in weights]
    grad_tokens, *grads = backward(n, cotangent, tokens, *weights, ln_gain, bias_model, *factors, saved)
    if n == 4 * PLANE:
        output, grad_tokens, *grads = deliver(output, grad_tokens, *grads)
        grads[5] = grads[5][:, :FF]
        summed = [g.reshape(-1) for g in grads]
        summed[6] = summed[6][: FF * LANES // n]
        return (output, grad_tokens, *summed)
    ups, g_qkv, g_out, g_ff, g_fc2 = grads
    early = 2 * D + FP
    g_up = ups[:, :, early:].reshape(CHIPS, 8, 3, D).transpose(0, 2, 1, 3)
    parts = (
        g_qkv.T,
        g_up,
        g_out.T,
        ups[:, :, D + FP : early],
        g_ff.T,
        ups[:, :, D : D + FF],
        g_fc2.T[:FF],
        ups[:, :, :D],
    )
    summed = [lax.psum_scatter(g.reshape(-1), "dp", scatter_dimension=0, tiled=True) for g in parts]
    return (output, grad_tokens, *summed)


def solution(mesh):
    return jax.shard_map(
        local,
        mesh=mesh,
        in_specs=(P("dp", None),) + (P("dp"),) * 4 + (P(),) * 12 + (P("dp", None),),
        out_specs=(P("dp", None),) * 2 + (P("dp"),) * 8,
        check_vma=False,
    )
```
